32 devices in a mesh: dp: 8 (over y, x, core), tensor: 4 (over z).
Axes of the slice: x: 2, y: 2, z: 4, core: 2. Of those that a mesh axis runs over, the one named last changes fastest.
Arguments:
- tokens: bfloat16 [8, 736, 1152], P('dp', 'tensor'), may hold values from -45 to 45
- key_mask: int32 [8, 736], P('dp'), may hold values from 0 to 1, as said below
- query_weight: bfloat16 [1152, 1152], P('dp', 'tensor'), may hold values from -0.1875 to 0.1875
- key_weight: bfloat16 [1152, 1152], P('dp', 'tensor'), may hold values from -0.1875 to 0.1875
- value_weight: bfloat16 [1152, 1152], P('dp', 'tensor'), may hold values from -0.1875 to 0.1875
- out_weight: bfloat16 [1152, 1152], P('tensor', 'dp'), may hold values from -0.375 to 0.375
- up_weight: bfloat16 [1152, 4304], P('dp', 'tensor'), may hold values from -0.1875 to 0.1875
- down_weight: bfloat16 [4304, 1152], P('tensor', 'dp'), may hold values from -0.09375 to 0.09375
- first_gain: bfloat16 [1152], P('dp'), may hold values from 0.5 to 1.5
- first_shift: bfloat16 [1152], P('dp'), may hold values from -3 to 3
- query_bias: bfloat16 [1152], P('dp'), may hold values from -3 to 3
- value_bias: bfloat16 [1152], P('dp'), may hold values from -3 to 3
- out_bias: bfloat16 [1152], P('dp'), may hold values from -3 to 3
- second_gain: bfloat16 [1152], P('dp'), may hold values from 0.5 to 1.5
- second_shift: bfloat16 [1152], P('dp'), may hold values from -3 to 3
- up_bias: bfloat16 [4304], P('dp'), may hold values from -3 to 3
- down_bias: bfloat16 [1152], P('dp'), may hold values from -3 to 3
- cotangent: bfloat16 [8, 736, 1152], P('dp', 'tensor'), may hold values from -6 to 6
Outputs:
- output: bfloat16 [8, 736, 1152], P('dp', 'tensor')
- input_grad: float32 [8, 736, 1152], P('dp', 'tensor')
- query_grad: float32 [1152, 1152], P('dp', 'tensor')
- key_grad: float32 [1152, 1152], P('dp', 'tensor')
- value_grad: float32 [1152, 1152], P('dp', 'tensor')
- out_grad: float32 [1152, 1152], P('tensor', 'dp')
- up_grad: float32 [1152, 4304], P('dp', 'tensor')
- down_grad: float32 [4304, 1152], P('tensor', 'dp')
- first_gain_grad: float32 [1152], P('dp')
- first_shift_grad: float32 [1152], P('dp')
- query_bias_grad: float32 [1152], P('dp')
- value_bias_grad: float32 [1152], P('dp')
- out_bias_grad: float32 [1152], P('dp')
- second_gain_grad: float32 [1152], P('dp')
- second_shift_grad: float32 [1152], P('dp')
- up_bias_grad: float32 [4304], P('dp')
- down_bias_grad: float32 [1152], P('dp')
The draws below stay inside these ranges and needn't reach their ends.
Inputs may be any that keep to these rules, and one draw needn't show every extreme that they name: `key_mask`: each image's ones form a prefix of its positions, at least its first three quarters.
All inputs are finite; a program needn't handle non-finite values.
Results may differ from the reference program's by a relative error of at most 0.017.
The reference program's roundings to bfloat16 on the way (of `first`, `probs`, `mixed`, `second`, `act`, `grad_pre_low`, `grad_mixed` and `grad_scores`) count: a program that leaves them out, or rounds other values in their place, can miss the bound.
Values may be sent and summed in bfloat16 or wider, within the bound.
A program may use at most 128 MiB of HBM per device.

```python
import math
import jax
import jax.numpy as jnp
from jax import lax

D = 1152
FF = 4304
H = 16
HD = 72
S = 736
IMAGES = 8
N_TENSOR = 4


def draw_tokens(key, part):
    streams = jax.random.split(key, 3)
    base = jax.random.normal(streams[0], (IMAGES, S, D), jnp.float32)
    base = jnp.clip(base, -4.0, 4.0)
    row_scale = jnp.exp(jax.random.uniform(streams[1], (IMAGES, S, 1), jnp.float32, -1.15, 1.15))
    column_scale = jnp.exp(jax.random.uniform(streams[2], (1, 1, D), jnp.float32, -1.15, 1.15))
    return (base * row_scale * column_scale).astype(jnp.bfloat16)


def draw_first_gain(key, part):
    values = jax.random.uniform(key, (D,), jnp.float32, 0.5, 1.5)
    return jnp.clip(values, 0.5, 1.5).astype(jnp.bfloat16)


def draw_down_bias(key, part):
    stream = jax.random.fold_in(key, 17)
    values = jnp.clip(0.8 * jax.random.normal(stream, (D,), jnp.float32), -3.0, 3.0)
    return values.astype(jnp.bfloat16)


def draw_key_mask(key, part):
    padding = jax.random.randint(key, (IMAGES,), 0, S // 4 + 1)
    lengths = S - padding
    places = jnp.arange(S, dtype=jnp.int32)
    return (places[None, :] < lengths[:, None]).astype(jnp.int32)


def levels(key, dims, cuts, smallest, largest):
    loudness, own = 1.0, jax.random.fold_in(key, 6)
    for dim, blocks in cuts:
        heights = jnp.exp(jax.random.uniform(jax.random.fold_in(own, dim), (blocks,), jnp.float32, smallest / len(cuts), largest / len(cuts)))
        loudness = loudness * jnp.repeat(heights, dims[dim] // blocks).reshape([-1 if axis == dim else 1 for axis in range(len(dims))])
    return loudness


def scatter_about(own_key, dims, spread, limit, cuts=(), kind=jnp.bfloat16):
    entries = jax.random.normal(own_key, dims, jnp.float32) * spread
    if len(cuts) > 0:
        entries = levels(own_key, dims, cuts, -0.22, 0.18) * entries
    return jnp.clip(entries, min=-limit, max=limit).astype(kind)


def setup_inputs(seed: int = 0) -> dict:
    key_of = jax.random.split(jax.random.key(seed), 19)
    tokens = draw_tokens(jax.random.fold_in(key_of[18], 71), 0)
    key_mask = draw_key_mask(jax.random.fold_in(key_of[18], 71), 0)
    query_weight = scatter_about(key_of[2], (D, D), D ** -0.5, 0.1875, ((0, 8), (1, 4)))
    key_weight = scatter_about(key_of[3], (D, D), D ** -0.5, 0.1875, ((0, 8), (1, 4)))
    value_weight = scatter_about(key_of[4], (D, D), D ** -0.5, 0.1875, ((0, 8), (1, 4)))
    out_weight = scatter_about(key_of[5], (D, D), (D // 4) ** -0.5, 0.375, ((0, 4), (1, 8)))
    up_weight = scatter_about(key_of[6], (D, FF), D ** -0.5, 0.1875, ((0, 8), (1, 4)))
    down_weight = scatter_about(key_of[7], (FF, D), FF ** -0.5, 0.09375, ((0, 4), (1, 8)))
    first_gain = draw_first_gain(jax.random.fold_in(key_of[18], 71), 0)
    first_shift = scatter_about(key_of[9], (D,), 0.5, 3.0, ((0, 8),))
    query_bias = scatter_about(key_of[10], (D,), 0.5, 3.0, ((0, 8),))
    value_bias = scatter_about(key_of[11], (D,), 0.5, 3.0, ((0, 8),))
    out_bias = scatter_about(key_of[12], (D,), 0.5, 3.0, ((0, 8),))
    second_gain = jnp.clip(1.0 + 0.1 * jax.random.normal(key_of[13], (D,), jnp.float32), 0.5, 1.5).astype(jnp.bfloat16)
    second_shift = scatter_about(key_of[14], (D,), 0.5, 3.0, ((0, 8),))
    up_bias = scatter_about(key_of[15], (FF,), 0.5, 3.0, ((0, 8),))
    down_bias = draw_down_bias(jax.random.fold_in(key_of[18], 71), 0)
    cotangent = scatter_about(key_of[17], (IMAGES, S, D), 1.0, 6.0, ((0, 8), (1, 4)))
    return {"tokens": tokens, "key_mask": key_mask, "query_weight": query_weight, "key_weight": key_weight, "value_weight": value_weight, "out_weight": out_weight, "up_weight": up_weight, "down_weight": down_weight, "first_gain": first_gain, "first_shift": first_shift, "query_bias": query_bias, "value_bias": value_bias, "out_bias": out_bias, "second_gain": second_gain, "second_shift": second_shift, "up_bias": up_bias, "down_bias": down_bias, "cotangent": cotangent}


EPSILON = 1e-06
GELU_COEF = 0.7978845608028654
MASK_FILL = -1e+30

def norm_forward(inputs, gain_vec, shift_vec):
    centred = inputs - lax.optimization_barrier(jnp.mean(inputs, axis=-1, keepdims=True))
    inv_std = lax.rsqrt(lax.optimization_barrier(jnp.mean(centred * centred, axis=-1, keepdims=True)) + EPSILON)
    normed = centred * inv_std
    return (normed * gain_vec + shift_vec, normed, inv_std)

def norm_backward(grad_in, normed, inv_std, gain_vec):
    scaled = grad_in * gain_vec
    return inv_std * (scaled - lax.optimization_barrier(jnp.mean(scaled, axis=-1, keepdims=True)) - normed * lax.optimization_barrier(jnp.mean(scaled * normed, axis=-1, keepdims=True)))

def gelu_pair(pre_act):
    tanh_val = jnp.tanh(GELU_COEF * (pre_act + 0.044715 * pre_act * pre_act * pre_act))
    gelu_value = 0.5 * pre_act * (1.0 + tanh_val)
    gelu_slope = 0.5 * (1.0 + tanh_val) + 0.5 * pre_act * (1.0 - tanh_val * tanh_val) * GELU_COEF * (1.0 + 3.0 * 0.044715 * pre_act * pre_act)
    return (gelu_value, gelu_slope)

def group_parts(left, right, groups):
    inner = left.shape[1] // groups
    left_groups = left.astype(jnp.float32).reshape(left.shape[0], groups, inner)
    right_groups = right.astype(jnp.float32).reshape(groups, inner, right.shape[1])
    return jnp.einsum('rgk,gkn->grn', left_groups, right_groups)

def round_sum(parts):
    rounded = lax.optimization_barrier(parts.astype(jnp.bfloat16))
    return lax.optimization_barrier(jnp.sum(rounded.astype(jnp.float32), axis=0))

def mat_dot(left, right):
    return jnp.dot(left, right, preferred_element_type=jnp.float32)

def reference(tokens, key_mask, query_weight, key_weight, value_weight, out_weight, up_weight, down_weight, first_gain, first_shift, query_bias, value_bias, out_bias, second_gain, second_shift, up_bias, down_bias, cotangent):
    gain_one = first_gain.astype(jnp.float32)
    shift_one = first_shift.astype(jnp.float32)
    bias_query = query_bias.astype(jnp.float32)
    bias_value = value_bias.astype(jnp.float32)
    bias_out = out_bias.astype(jnp.float32)
    gain_two = second_gain.astype(jnp.float32)
    shift_two = second_shift.astype(jnp.float32)
    bias_up = up_bias.astype(jnp.float32)
    bias_down = down_bias.astype(jnp.float32)
    scale_factor = 1.0 / math.sqrt(HD)
    head_shape = (S, H, HD)

    def one_image(carry, item):
        image_tokens, valid, image_cot = item
        inputs = image_tokens.astype(jnp.float32)
        first, normed_one, inv_one = norm_forward(inputs, gain_one, shift_one)
        first_low = first.astype(jnp.bfloat16)
        query = ((mat_dot(first_low, query_weight) + bias_query) * scale_factor).astype(jnp.bfloat16)
        keys = mat_dot(first_low, key_weight).astype(jnp.bfloat16)
        values = (mat_dot(first_low, value_weight) + bias_value).astype(jnp.bfloat16)
        query_heads = query.reshape(head_shape).astype(jnp.float32)
        keys_heads = keys.reshape(head_shape).astype(jnp.float32)
        values_heads = values.reshape(head_shape).astype(jnp.float32)
        scores = jnp.einsum('qhd,khd->hqk', query_heads, keys_heads)
        scores = jnp.where(valid[None, None, :] > 0, scores, MASK_FILL)
        highest = lax.optimization_barrier(jnp.max(scores, axis=-1, keepdims=True))
        logsum = highest + jnp.log(lax.optimization_barrier(jnp.sum(jnp.exp(scores - highest), axis=-1, keepdims=True)))
        probs_full = jnp.exp(scores - logsum)
        probs = probs_full.astype(jnp.bfloat16)
        mixed_heads = jnp.einsum('hqk,khd->qhd', probs.astype(jnp.float32), values_heads).astype(jnp.bfloat16)
        mixed = mixed_heads.reshape(S, D)
        hidden = inputs + round_sum(group_parts(mixed, out_weight, N_TENSOR)) + bias_out
        second, normed_two, inv_two = norm_forward(hidden, gain_two, shift_two)
        second_low = second.astype(jnp.bfloat16)
        pre_act = mat_dot(second_low, up_weight) + bias_up
        gelu_value, gelu_slope = gelu_pair(pre_act)
        act = gelu_value.astype(jnp.bfloat16)
        output = (hidden + round_sum(group_parts(act, down_weight, N_TENSOR)) + bias_down).astype(jnp.bfloat16)
        grad_out = image_cot.astype(jnp.float32)
        down_bias_grad = lax.optimization_barrier(jnp.sum(grad_out, axis=0))
        down_grad = mat_dot(act.T, image_cot)
        grad_pre = mat_dot(image_cot, down_weight.T) * gelu_slope
        up_bias_grad = lax.optimization_barrier(jnp.sum(grad_pre, axis=0))
        grad_pre_low = grad_pre.astype(jnp.bfloat16)
        up_grad = mat_dot(second_low.T, grad_pre_low)
        grad_second = round_sum(group_parts(grad_pre_low, up_weight.T, N_TENSOR))
        second_gain_grad = lax.optimization_barrier(jnp.sum(grad_second * normed_two, axis=0))
        second_shift_grad = lax.optimization_barrier(jnp.sum(grad_second, axis=0))
        grad_hidden = grad_out + norm_backward(grad_second, normed_two, inv_two, gain_two)
        out_bias_grad = lax.optimization_barrier(jnp.sum(grad_hidden, axis=0))
        hidden_low = grad_hidden.astype(jnp.bfloat16)
        grad_mixed = mat_dot(hidden_low, out_weight.T).astype(jnp.bfloat16)
        out_grad = mat_dot(mixed.T, hidden_low)
        grad_mixed_heads = grad_mixed.reshape(head_shape).astype(jnp.float32)
        grad_values_f = jnp.einsum('hqk,qhd->khd', probs.astype(jnp.float32), grad_mixed_heads).reshape(S, D)
        value_bias_grad = lax.optimization_barrier(jnp.sum(grad_values_f, axis=0))
        grad_probs = jnp.einsum('qhd,khd->hqk', grad_mixed_heads, values_heads)
        delta = lax.optimization_barrier(jnp.sum(grad_mixed_heads * mixed_heads.astype(jnp.float32), axis=-1)).T
        grad_scores = (probs_full * (grad_probs - delta[:, :, None])).astype(jnp.bfloat16).astype(jnp.float32)
        grad_query_f = (jnp.einsum('hqk,khd->qhd', grad_scores, keys_heads) * scale_factor).reshape(S, D)
        grad_keys_f = jnp.einsum('hqk,qhd->khd', grad_scores, query_heads).reshape(S, D)
        query_bias_grad = lax.optimization_barrier(jnp.sum(grad_query_f, axis=0))
        grad_query = grad_query_f.astype(jnp.bfloat16)
        grad_keys = grad_keys_f.astype(jnp.bfloat16)
        grad_values = grad_values_f.astype(jnp.bfloat16)
        query_grad = mat_dot(first_low.T, grad_query)
        key_grad = mat_dot(first_low.T, grad_keys)
        value_grad = mat_dot(first_low.T, grad_values)
        first_parts = group_parts(grad_query, query_weight.T, N_TENSOR) + group_parts(grad_keys, key_weight.T, N_TENSOR) + group_parts(grad_values, value_weight.T, N_TENSOR)
        grad_first = round_sum(first_parts)
        first_gain_grad = lax.optimization_barrier(jnp.sum(grad_first * normed_one, axis=0))
        first_shift_grad = lax.optimization_barrier(jnp.sum(grad_first, axis=0))
        input_grad = grad_hidden + norm_backward(grad_first, normed_one, inv_one, gain_one)
        terms = (query_grad, key_grad, value_grad, out_grad, up_grad, down_grad, first_gain_grad, first_shift_grad, query_bias_grad, value_bias_grad, out_bias_grad, second_gain_grad, second_shift_grad, up_bias_grad, down_bias_grad)
        new_carry = tuple((total + term for total, term in zip(carry, terms)))
        return (new_carry, (output, input_grad))
    start = (jnp.zeros((D, D), jnp.float32), jnp.zeros((D, D), jnp.float32), jnp.zeros((D, D), jnp.float32), jnp.zeros((D, D), jnp.float32), jnp.zeros((D, FF), jnp.float32), jnp.zeros((FF, D), jnp.float32), jnp.zeros((D,), jnp.float32), jnp.zeros((D,), jnp.float32), jnp.zeros((D,), jnp.float32), jnp.zeros((D,), jnp.float32), jnp.zeros((D,), jnp.float32), jnp.zeros((D,), jnp.float32), jnp.zeros((D,), jnp.float32), jnp.zeros((FF,), jnp.float32), jnp.zeros((D,), jnp.float32))
    totals, stacked = lax.scan(one_image, start, (tokens, key_mask, cotangent))
    output, input_grad = stacked
    return (output, input_grad, totals[0], totals[1], totals[2], totals[3], totals[4], totals[5], totals[6], totals[7], totals[8], totals[9], totals[10], totals[11], totals[12], totals[13], totals[14])
```

```python
from functools import partial
import math

import jax
import jax.numpy as jnp
from jax import lax
from jax.experimental import pallas as pl
from jax.experimental.pallas import tpu as pltpu
from jax.sharding import PartitionSpec as P

HD = 72
EPSILON = 1e-06
GELU_COEF = 0.7978845608028654
MASK_FILL = -1e30
MESH = pl.DeviceIdType.MESH
ANY = pl.BlockSpec(memory_space=pl.ANY)
VM = pl.BlockSpec(memory_space=pltpu.VMEM)
DMA = pltpu.SemaphoreType.DMA
VMEM_BYTES = 60 << 20
F32 = jnp.float32
BF16 = jnp.bfloat16


def remote(src, dst, send_sem, recv_sem, device):
    return pltpu.make_async_remote_copy(
        src_ref=src,
        dst_ref=dst,
        send_sem=send_sem,
        recv_sem=recv_sem,
        device_id=device,
        device_id_type=MESH,
    )


class Place:
    def __init__(self, dp_size, line):
        self.dp_size, self.line, self.chips = dp_size, line, dp_size // 2
        self.dp = lax.axis_index("dp")
        self.z = lax.axis_index("tensor")
        self.core = lax.rem(self.dp, 2)
        self.chip = lax.div(self.dp, 2)
        self.sibling = (2 * self.chip + 1 - self.core, self.z)

    def chip_at(self, k):
        return lax.rem(self.chip + k + self.chips, self.chips)

    def peer(self, k):
        return (2 * self.chip_at(k) + self.core, self.z)

    def along(self, k):
        return (self.dp, lax.rem(self.z + k + self.line, self.line))

    def enter(self, across=True, line=True):
        barrier = pltpu.get_barrier_semaphore()
        devices = []
        if across:
            devices += [self.peer(k) for k in range(1, self.chips)] + [self.sibling]
        if line:
            devices += [self.along(k) for k in range(1, self.line)]
        for device in devices:
            pl.semaphore_signal(barrier, inc=1, device_id=device, device_id_type=MESH)
        pl.semaphore_wait(barrier, len(devices))


class DpGather:
    @staticmethod
    def sems(place_chips):
        return [DMA((place_chips,)), DMA((place_chips,)), DMA((2 * place_chips,)), DMA(())]

    def __init__(self, place, src, dst, sems):
        self.p, self.src, self.dst = place, src, dst
        self.across, self.inside, self.recv, self.local = sems

    def start(self):
        p = self.p
        mine = self.dst.at[p.dp]
        for k in range(1, p.chips):
            remote(self.src, mine, self.across.at[k], self.recv.at[p.dp], p.peer(k)).start()
        remote(self.src, mine, self.inside.at[0], self.recv.at[p.dp], p.sibling).start()
        pltpu.make_async_copy(self.src, mine, self.local).start()

    def forward(self):
        p = self.p
        for k in range(1, p.chips):
            slot = 2 * p.chip_at(-k) + p.core
            block = self.dst.at[slot]
            remote(block, block, self.across.at[k], self.recv.at[slot], p.sibling).wait_recv()
            remote(block, block, self.inside.at[k], self.recv.at[slot], p.sibling).start()

    def finish(self):
        p = self.p
        mine = self.dst.at[p.dp]
        for k in range(p.chips):
            slot = 2 * p.chip_at(-k) + 1 - p.core
            block = self.dst.at[slot]
            remote(block, block, self.inside.at[k], self.recv.at[slot], p.sibling).wait_recv()
        for k in range(p.chips):
            remote(self.src, mine, self.inside.at[k], self.recv.at[0], p.sibling).wait_send()
            if k > 0:
                remote(self.src, mine, self.across.at[k], self.recv.at[0], p.sibling).wait_send()
        pltpu.make_async_copy(self.src, mine, self.local).wait()


class LineGather:
    @staticmethod
    def sems(line):
        return [DMA((line,)), DMA((line,)), DMA((line,)), DMA(())]

    def __init__(self, place, src, dst, sems):
        self.p, self.src, self.dst = place, src, dst
        self.right, self.left, self.recv, self.local = sems

    def send(self, src, slot, step):
        p = self.p

        @pl.when(p.z < p.line - 1)
        def _():
            remote(src, self.dst.at[slot], self.right.at[step], self.recv.at[slot], (p.dp, p.z + 1)).start()

    def send_left(self, src, slot, step):
        p = self.p

        @pl.when(p.z > 0)
        def _():
            remote(src, self.dst.at[slot], self.left.at[step], self.recv.at[slot], (p.dp, p.z - 1)).start()

    def start(self):
        p = self.p
        self.send(self.src, p.z, 0)
        self.send_left(self.src, p.z, 0)
        pltpu.make_async_copy(self.src, self.dst.at[p.z], self.local).start()

    def arrive(self, slot):
        block = self.dst.at[slot]
        remote(block, block, self.right.at[0], self.recv.at[slot], self.p.sibling).wait_recv()

    def step(self, s):
        p = self.p

        @pl.when(p.z >= s)
        def _():
            self.arrive(p.z - s)
            self.send(self.dst.at[p.z - s], p.z - s, s)

        @pl.when(p.z + s < p.line)
        def _():
            self.arrive(p.z + s)
            self.send_left(self.dst.at[p.z + s], p.z + s, s)

    def finish(self):
        p = self.p
        block = self.dst.at[0]
        for s in range(p.line):

            @pl.when(jnp.logical_and(p.z >= s, p.z < p.line - 1))
            def _():
                remote(self.src, block, self.right.at[s], self.recv.at[0], p.sibling).wait_send()

            @pl.when(jnp.logical_and(p.z + s < p.line, p.z > 0))
            def _():
                remote(self.src, block, self.left.at[s], self.recv.at[0], p.sibling).wait_send()

        pltpu.make_async_copy(self.src, self.dst.at[p.z], self.local).wait()


class LineExchange:
    @staticmethod
    def sems(line):
        return [DMA((line,)), DMA((line,)), DMA(())]

    def __init__(self, place, src, dst, sems):
        self.p, self.src, self.dst = place, src, dst
        self.sent, self.recv, self.local = sems

    def start(self):
        p = self.p
        for k in range(1, p.line):
            to = p.along(k)
            remote(self.src.at[to[1]], self.dst.at[p.z], self.sent.at[k], self.recv.at[p.z], to).start()
        pltpu.make_async_copy(self.src.at[p.z], self.dst.at[p.z], self.local).start()

    def finish(self):
        p = self.p
        for k in range(1, p.line):
            slot = p.along(k)[1]
            block = self.dst.at[slot]
            remote(block, block, self.sent.at[k], self.recv.at[slot], p.sibling).wait_recv()
        for k in range(1, p.line):
            block = self.src.at[0]
            remote(block, block, self.sent.at[k], self.recv.at[0], p.sibling).wait_send()
        pltpu.make_async_copy(self.src.at[p.z], self.dst.at[p.z], self.local).wait()


class LineSum:
    @staticmethod
    def sems(line):
        return [DMA((line,)), DMA((line,)), DMA((line,))]

    def __init__(self, place, part, from_left, from_right, sems):
        self.p, self.part, self.from_left, self.from_right = place, part, from_left, from_right
        self.sent, self.recv_left, self.recv_right = sems

    def add(self, d, got):
        self.part[d] = (self.part[d].astype(F32) + got[d].astype(F32)).astype(BF16)

    def wait(self, got, recv, d):
        remote(got.at[d], got.at[d], self.sent.at[d], recv.at[d], self.p.sibling).wait_recv()

    def move(self, i):
        p = self.p
        d = p.line - 1 - i

        @pl.when(p.z < d)
        def _():
            @pl.when(p.z > 0)
            def _():
                self.wait(self.from_left, self.recv_left, d)
                self.add(d, self.from_left)

            remote(self.part.at[d], self.from_left.at[d], self.sent.at[d], self.recv_left.at[d], (p.dp, p.z + 1)).start()

        @pl.when(p.z > i)
        def _():
            @pl.when(p.z < p.line - 1)
            def _():
                self.wait(self.from_right, self.recv_right, i)
                self.add(i, self.from_right)

            remote(self.part.at[i], self.from_right.at[i], self.sent.at[i], self.recv_right.at[i], (p.dp, p.z - 1)).start()

    def finish(self, out):
        p = self.p
        out[...] = self.part[p.z].astype(F32)

        @pl.when(p.z > 0)
        def _():
            self.wait(self.from_left, self.recv_left, p.z)
            out[...] += self.from_left[p.z].astype(F32)

        @pl.when(p.z < p.line - 1)
        def _():
            self.wait(self.from_right, self.recv_right, p.z)
            out[...] += self.from_right[p.z].astype(F32)

        for d in range(p.line):

            @pl.when(p.z != d)
            def _():
                block = self.part.at[d]
                remote(block, block, self.sent.at[d], self.recv_left.at[d], p.sibling).wait_send()


class DpSum:
    @staticmethod
    def sems(chips):
        return [DMA((chips,)), DMA((chips,)), DMA((chips,)), DMA((chips,))]

    def __init__(self, place, part, near, far, sems):
        self.p, self.part, self.near, self.far = place, part, near, far
        self.sent, self.recv, self.sent_far, self.recv_far = sems

    def start(self):
        p = self.p
        for k in [*range(1, p.chips), 0]:
            chip = p.chip_at(k)
            remote(self.part.at[2 * chip + 1 - p.core], self.near.at[k], self.sent.at[k], self.recv.at[k], p.sibling).start()

    def wait_near(self, k):
        block = self.near.at[k]
        remote(block, block, self.sent.at[k], self.recv.at[k], self.p.sibling).wait_recv()

    def move(self):
        p = self.p
        for k in range(1, p.chips):
            slot = 2 * p.chip_at(k) + p.core
            self.wait_near(k)
            self.part[slot] = (self.part[slot].astype(F32) + self.near[k].astype(F32)).astype(BF16)
            remote(self.part.at[slot], self.far.at[k], self.sent_far.at[k], self.recv_far.at[k], p.peer(k)).start()

    def finish(self):
        p = self.p
        self.wait_near(0)
        total = self.part[p.dp].astype(F32) + self.near[0].astype(F32)
        for k in range(1, p.chips):
            block = self.far.at[k]
            remote(block, block, self.sent_far.at[k], self.recv_far.at[k], p.sibling).wait_recv()
            total += self.far[k].astype(F32)
        for k in range(p.chips):
            block = self.near.at[0]
            remote(block, block, self.sent.at[k], self.recv.at[0], p.sibling).wait_send()
            if k > 0:
                remote(block, block, self.sent_far.at[k], self.recv.at[0], p.sibling).wait_send()
        return total


def params(collective_id):
    return pltpu.CompilerParams(
        collective_id=collective_id, has_side_effects=True, vmem_limit_bytes=VMEM_BYTES
    )


def shape(*dims, dtype=BF16):
    return jax.ShapeDtypeStruct(dims, dtype)


def gather_all(sizes, across, chained, along):
    n, t = sizes
    count = (len(across), len(chained), len(along))

    def kernel(*refs):
        refs = list(refs)
        take = lambda m: [refs.pop(0) for _ in range(m)]
        a_in, c_in, l_in = take(count[0]), take(count[1]), take(count[2])
        a_out, c_out, l_out = take(count[0]), take(count[1]), take(count[2])
        c_mid = take(count[1])
        place = Place(n, t)
        dp_ops = [DpGather(place, s, d, take(4)) for s, d in zip(a_in, a_out)]
        mid_ops = [LineGather(place, s, d, take(4)) for s, d in zip(c_in, c_mid)]
        tail_ops = [DpGather(place, s, d, take(4)) for s, d in zip(c_mid, c_out)]
        line_ops = [LineGather(place, s, d, take(4)) for s, d in zip(l_in, l_out)]
        place.enter()
        for op in mid_ops + line_ops + dp_ops:
            op.start()
        for s in range(1, t):
            for op in mid_ops:
                op.step(s)
        for op in mid_ops:
            op.finish()
        for op in tail_ops:
            op.start()
        for s in range(1, t):
            for op in line_ops:
                op.step(s)
        for op in dp_ops + tail_ops:
            op.forward()
        for op in line_ops + dp_ops + tail_ops:
            op.finish()

    outs = (
        [shape(n, *a.shape, dtype=a.dtype) for a in across]
        + [shape(n, t, *a.shape, dtype=a.dtype) for a in chained]
        + [shape(t, *a.shape, dtype=a.dtype) for a in along]
    )
    scratch = [pltpu.VMEM((t, *a.shape), a.dtype) for a in chained]
    for _ in across:
        scratch += DpGather.sems(n // 2)
    for _ in chained:
        scratch += LineGather.sems(t)
    for _ in chained:
        scratch += DpGather.sems(n // 2)
    for _ in along:
        scratch += LineGather.sems(t)
    return pl.pallas_call(
        kernel,
        out_shape=outs,
        in_specs=[ANY] * sum(count),
        out_specs=[ANY] * sum(count),
        scratch_shapes=scratch,
        compiler_params=params(0),
        name="gather_all",
    )(*across, *chained, *along)


def line_gather(sizes, block, collective_id):
    n, t = sizes

    def kernel(src, dst, *sems):
        place = Place(n, t)
        op = LineGather(place, src, dst, sems)
        place.enter(across=False)
        op.start()
        for s in range(1, t):
            op.step(s)
        op.finish()

    return pl.pallas_call(
        kernel,
        out_shape=shape(t, *block.shape),
        in_specs=[ANY],
        out_specs=ANY,
        scratch_shapes=LineGather.sems(t),
        compiler_params=params(collective_id),
        name="line_gather",
    )(block)


def line_exchange(sizes, blocks, collective_id):
    n, t = sizes

    def kernel(src, dst, *sems):
        place = Place(n, t)
        op = LineExchange(place, src, dst, sems)
        place.enter(across=False)
        op.start()
        op.finish()

    return pl.pallas_call(
        kernel,
        out_shape=shape(*blocks.shape),
        in_specs=[ANY],
        out_specs=ANY,
        scratch_shapes=LineExchange.sems(t),
        compiler_params=params(collective_id),
        name="line_exchange",
    )(blocks)


def line_sum(sizes, parts, collective_id):
    n, t = sizes
    m = len(parts)

    def kernel(*refs):
        refs = list(refs)
        take = lambda c: [refs.pop(0) for _ in range(c)]
        ins, outs, work, left, right = take(m), take(m), take(m), take(m), take(m)
        place = Place(n, t)
        ops = [LineSum(place, *r, take(3)) for r in zip(work, left, right)]
        place.enter(across=False)
        for op, src in zip(ops, ins):
            op.part[...] = src[...]
        for op in ops:
            for i in range(t - 1):
                op.move(i)
        for op, out in zip(ops, outs):
            op.finish(out)

    scratch = [pltpu.VMEM(p.shape, BF16) for _ in range(3) for p in parts]
    for _ in parts:
        scratch += LineSum.sems(t)
    return pl.pallas_call(
        kernel,
        out_shape=[shape(*p.shape[1:], dtype=F32) for p in parts],
        in_specs=[VM] * m,
        out_specs=[VM] * m,
        scratch_shapes=scratch,
        compiler_params=params(collective_id),
        name="line_sum",
    )(*parts)


def sum_all(sizes, across, chained, collective_id):
    n, t = sizes
    chips = n // 2
    m, c = len(across), len(chained)

    def kernel(*refs):
        refs = list(refs)
        take = lambda q: [refs.pop(0) for _ in range(q)]
        ins, outs = take(m + c), take(m + c)
        work, near, far = take(m + c), take(m + c), take(m + c)
        mid, got = take(c), take(c)
        place = Place(n, t)
        ops = [DpSum(place, *r, take(4)) for r in zip(work, near, far)]
        tails = [LineExchange(place, s, d, take(3)) for s, d in zip(mid, got)]
        place.enter()
        order = ops[m:] + ops[:m]
        sources = ins[m:] + ins[:m]
        for op, src in zip(order, sources):
            op.part[...] = src[...]
            op.start()
        for op in order:
            op.move()
        for op, s, tail in zip(ops[m:], mid, tails):
            s[...] = op.finish().astype(BF16)
            tail.start()
        for op, out in zip(ops[:m], outs[:m]):
            out[...] = op.finish()
        for tail, d, out in zip(tails, got, outs[m:]):
            tail.finish()
            out[...] = jnp.sum(d[...].astype(F32), axis=0)

    every = [*across, *chained]
    scratch = [pltpu.VMEM(p.shape, BF16) for p in every]
    scratch += [pltpu.VMEM((chips, *p.shape[1:]), BF16) for _ in range(2) for p in every]
    scratch += [pltpu.VMEM(p.shape[1:], BF16) for _ in range(2) for p in chained]
    for _ in every:
        scratch += DpSum.sems(chips)
    for _ in chained:
        scratch += LineExchange.sems(t)
    outs = [shape(*p.shape[1:], dtype=F32) for p in across] + [shape(*p.shape[2:], dtype=F32) for p in chained]
    return pl.pallas_call(
        kernel,
        out_shape=outs,
        in_specs=[VM] * len(every),
        out_specs=[VM] * len(every),
        scratch_shapes=scratch,
        compiler_params=params(collective_id),
        name="sum_all",
    )(*every)


def vector_sum(sizes, parts, collective_id):
    n, t = sizes

    def kernel(src, out, got, mid, got_line, sent, recv, sent_line, recv_line):
        place = Place(n, t)
        barrier = pltpu.get_barrier_semaphore()
        others = [lax.rem(place.dp + k, n) for k in range(1, n)]
        devices = [(d, place.z) for d in others] + [place.along(k) for k in range(1, t)]
        for device in devices:
            pl.semaphore_signal(barrier, inc=1, device_id=device, device_id_type=MESH)
        pl.semaphore_wait(barrier, len(devices))
        for k in range(1, n):
            remote(src.at[others[k - 1]], got.at[k], sent.at[k], recv.at[k], (others[k - 1], place.z)).start()
        total = src[place.dp]
        for k in range(1, n):
            remote(got.at[k], got.at[k], sent.at[k], recv.at[k], place.sibling).wait()
            total += got[k]
        mid[...] = total
        for k in range(1, t):
            remote(mid, got_line.at[k], sent_line.at[k], recv_line.at[k], place.along(k)).start()
        for k in range(1, t):
            remote(mid, got_line.at[k], sent_line.at[k], recv_line.at[k], place.sibling).wait()
            total += got_line[k]
        out[...] = total

    block = parts.shape[1:]
    return pl.pallas_call(
        kernel,
        out_shape=shape(*block, dtype=F32),
        in_specs=[VM],
        out_specs=VM,
        scratch_shapes=[
            pltpu.VMEM((n, *block), F32),
            pltpu.VMEM(block, F32),
            pltpu.VMEM((t, *block), F32),
            DMA((n,)),
            DMA((n,)),
            DMA((t,)),
            DMA((t,)),
        ],
        compiler_params=params(collective_id),
        name="vector_sum",
    )(parts)


def norm_forward(inputs, gain_vec, shift_vec):
    centred = inputs - jnp.mean(inputs, axis=-1, keepdims=True)
    inv_std = lax.rsqrt(jnp.mean(centred * centred, axis=-1, keepdims=True) + EPSILON)
    normed = centred * inv_std
    return (normed * gain_vec + shift_vec, normed, inv_std)


def norm_backward(grad_in, normed, inv_std, gain_vec):
    scaled = grad_in * gain_vec
    return inv_std * (
        scaled
        - jnp.mean(scaled, axis=-1, keepdims=True)
        - normed * jnp.mean(scaled * normed, axis=-1, keepdims=True)
    )


def gelu_pair(pre_act):
    tanh_val = jnp.tanh(GELU_COEF * (pre_act + 0.044715 * pre_act * pre_act * pre_act))
    gelu_value = 0.5 * pre_act * (1.0 + tanh_val)
    gelu_slope = 0.5 * (1.0 + tanh_val) + 0.5 * pre_act * (
        1.0 - tanh_val * tanh_val
    ) * GELU_COEF * (1.0 + 3.0 * 0.044715 * pre_act * pre_act)
    return (gelu_value, gelu_slope)


def mat_dot(left, right):
    return jnp.dot(left, right, preferred_element_type=jnp.float32)


def attend(query, keys, values, valid):
    scores = jnp.einsum("qhd,khd->hqk", query, keys, preferred_element_type=jnp.float32)
    scores = jnp.where(valid[None, None, :] > 0, scores, MASK_FILL)
    highest = jnp.max(scores, axis=-1, keepdims=True)
    logsum = highest + jnp.log(jnp.sum(jnp.exp(scores - highest), axis=-1, keepdims=True))
    probs = jnp.exp(scores - logsum).astype(jnp.bfloat16)
    mixed = jnp.einsum("hqk,khd->qhd", probs, values, preferred_element_type=jnp.float32)
    return (mixed.astype(jnp.bfloat16), logsum[..., 0])


def attend_back(scale_factor, query, keys, values, valid, logsum, mixed, grad):
    scores = jnp.einsum("qhd,khd->hqk", query, keys, preferred_element_type=jnp.float32)
    scores = jnp.where(valid[None, None, :] > 0, scores, MASK_FILL)
    probs_full = jnp.exp(scores - logsum[:, :, None])
    probs = probs_full.astype(jnp.bfloat16)
    grad_values = jnp.einsum("hqk,qhd->khd", probs, grad, preferred_element_type=jnp.float32)
    grad_probs = jnp.einsum("qhd,khd->hqk", grad, values, preferred_element_type=jnp.float32)
    delta = jnp.sum(grad.astype(jnp.float32) * mixed.astype(jnp.float32), axis=-1).T
    grad_scores = (probs_full * (grad_probs - delta[:, :, None])).astype(jnp.bfloat16)
    grad_query = (
        jnp.einsum("hqk,khd->qhd", grad_scores, keys, preferred_element_type=jnp.float32)
        * scale_factor
    )
    grad_keys = jnp.einsum("hqk,qhd->khd", grad_scores, query, preferred_element_type=jnp.float32)
    return (grad_query, grad_keys, grad_values)


def shards(
    sizes,
    tokens,
    key_mask,
    query_weight,
    key_weight,
    value_weight,
    out_weight,
    up_weight,
    down_weight,
    first_gain,
    first_shift,
    query_bias,
    value_bias,
    out_bias,
    second_gain,
    second_shift,
    up_bias,
    down_bias,
    cotangent,
):
    n, t = sizes
    z = lax.axis_index("tensor")
    images, rows, width = tokens.shape
    share = first_gain.shape[0]
    up_share = up_bias.shape[0]
    cols = query_weight.shape[1]
    hidden_cols = up_weight.shape[1]
    heads = cols // HD
    seq = t * rows
    scale_factor = 1.0 / math.sqrt(HD)

    small = [first_gain, first_shift, query_bias, value_bias, out_bias, second_gain, second_shift, down_bias]
    pack = jnp.stack([jnp.pad(v, (0, up_share - share)) for v in small] + [up_bias])
    pack = jnp.pad(pack, ((0, 16 - len(small) - 1), (0, 0)))
    qkv_all, up_all, down_all, vec_all, out_all, token_rows, grad_rows = gather_all(
        sizes,
        [
            jnp.concatenate([query_weight, key_weight, value_weight], axis=1),
            up_weight,
            down_weight.T,
            pack,
        ],
        [out_weight.T],
        [tokens[0], cotangent[0]],
    )
    qkv_full = qkv_all.reshape(width, 3 * cols)
    up_full = up_all.reshape(width, hidden_cols)
    down_full = down_all.reshape(width, hidden_cols)
    out_full = out_all.transpose(1, 0, 2, 3).reshape(t, width, cols)
    vec = vec_all.astype(F32)
    gain_one, shift_one, query_bias_all, value_bias_all, out_bias_all, gain_two, shift_two, down_bias_all = [
        vec[:, i, :share].reshape(-1) for i in range(8)
    ]
    up_bias_all = vec[:, 8, :].reshape(-1)
    query_bias_local = lax.dynamic_slice_in_dim(query_bias_all, z * cols, cols)
    value_bias_local = lax.dynamic_slice_in_dim(value_bias_all, z * cols, cols)
    up_bias_local = lax.dynamic_slice_in_dim(up_bias_all, z * hidden_cols, hidden_cols)

    inputs = tokens[0].astype(F32)
    normed_one, inv_one = norm_forward(inputs, gain_one, shift_one)[1:]
    first = norm_forward(token_rows.reshape(seq, width).astype(F32), gain_one, shift_one)[0].astype(BF16)
    qkv = mat_dot(first, qkv_full)
    head_shape = (seq, heads, HD)
    query = ((qkv[:, :cols] + query_bias_local) * scale_factor).astype(BF16).reshape(head_shape)
    keys = qkv[:, cols : 2 * cols].astype(BF16).reshape(head_shape)
    values = (qkv[:, 2 * cols :] + value_bias_local).astype(BF16).reshape(head_shape)
    mixed, logsum = attend(query, keys, values, key_mask[0])
    mixed_rows = line_exchange(sizes, mixed.reshape(t, rows, cols), 1)
    terms = jnp.einsum("trc,tdc->trd", mixed_rows, out_full, preferred_element_type=F32).astype(BF16)
    hidden = inputs + jnp.sum(terms.astype(F32), axis=0) + out_bias_all
    second, normed_two, inv_two = norm_forward(hidden, gain_two, shift_two)
    second_all = line_gather(sizes, second.astype(BF16), 2).reshape(seq, width)
    pre_act = mat_dot(second_all, up_full) + up_bias_local
    gelu_value, gelu_slope = gelu_pair(pre_act)
    act = gelu_value.astype(BF16)
    cot_all = grad_rows.reshape(seq, width)
    out_part = mat_dot(act, down_full.T).astype(BF16)
    grad_pre = mat_dot(cot_all, down_full) * gelu_slope
    up_bias_part = jnp.sum(grad_pre, axis=0)
    grad_pre_low = grad_pre.astype(BF16)
    second_part = mat_dot(grad_pre_low, up_full.T).astype(BF16)
    grad_second, mlp_out = line_sum(
        sizes, [second_part.reshape(t, rows, width), out_part.reshape(t, rows, width)], 3
    )
    output = (hidden + mlp_out + down_bias_all).astype(BF16)
    down_grad = mat_dot(cot_all.T, act).astype(BF16)
    up_grad = mat_dot(second_all.T, grad_pre_low).astype(BF16)
    grad_out = cotangent[0].astype(F32)
    down_bias_grad = jnp.sum(grad_out, axis=0)
    second_gain_grad = jnp.sum(grad_second * normed_two, axis=0)
    second_shift_grad = jnp.sum(grad_second, axis=0)
    grad_hidden = grad_out + norm_backward(grad_second, normed_two, inv_two, gain_two)
    out_bias_grad = jnp.sum(grad_hidden, axis=0)
    hidden_low = grad_hidden.astype(BF16)
    grad_mixed_rows = jnp.einsum("rd,tdc->trc", hidden_low, out_full, preferred_element_type=F32).astype(BF16)
    out_grad = jnp.einsum("rd,trc->tdc", hidden_low, mixed_rows, preferred_element_type=F32).astype(BF16)
    grad_mixed = line_exchange(sizes, grad_mixed_rows, 4).reshape(head_shape)
    grad_query_f, grad_keys_f, grad_values_f = attend_back(
        scale_factor, query, keys, values, key_mask[0], logsum, mixed, grad_mixed
    )
    grad_query_f = grad_query_f.reshape(seq, cols)
    grad_keys_f = grad_keys_f.reshape(seq, cols)
    grad_values_f = grad_values_f.reshape(seq, cols)
    query_bias_part = jnp.sum(grad_query_f, axis=0)
    value_bias_part = jnp.sum(grad_values_f, axis=0)
    grad_qkv = jnp.concatenate([g.astype(BF16) for g in (grad_query_f, grad_keys_f, grad_values_f)], axis=1)
    first_part = mat_dot(grad_qkv, qkv_full.T).astype(BF16)
    (grad_first,) = line_sum(sizes, [first_part.reshape(t, rows, width)], 5)
    qkv_grad = mat_dot(first.T, grad_qkv).astype(BF16)
    qkv_share, up_grad_share, down_share, out_share = sum_all(
        sizes,
        [
            qkv_grad.reshape(n, share, 3 * cols),
            up_grad.reshape(n, share, hidden_cols),
            down_grad.reshape(n, share, hidden_cols),
        ],
        [out_grad.reshape(t, n, share, cols).transpose(1, 0, 2, 3)],
        6,
    )
    first_gain_grad = jnp.sum(grad_first * normed_one, axis=0)
    first_shift_grad = jnp.sum(grad_first, axis=0)
    input_grad = grad_hidden + norm_backward(grad_first, normed_one, inv_one, gain_one)
    placed = lambda part, full: lax.dynamic_update_slice_in_dim(
        jnp.zeros((full,), F32), part, z * part.shape[0], 0
    )
    wide = jnp.stack(
        [
            first_gain_grad,
            first_shift_grad,
            placed(query_bias_part, width),
            placed(value_bias_part, width),
            out_bias_grad,
            second_gain_grad,
            second_shift_grad,
            down_bias_grad,
        ]
    ).reshape(8, n, share)
    wide = jnp.pad(wide, ((0, 0), (0, 0), (0, up_share - share)))
    last = placed(up_bias_part, up_bias_all.shape[0]).reshape(1, n, up_share)
    wide = jnp.pad(jnp.concatenate([wide, last]), ((0, 7), (0, 0), (0, 0))).transpose(1, 0, 2)
    vectors = vector_sum(sizes, wide, 7)
    outs = [vectors[i, :share] for i in range(8)]
    return (
        output[None],
        input_grad[None],
        qkv_share[:, :cols],
        qkv_share[:, cols : 2 * cols],
        qkv_share[:, 2 * cols :],
        out_share.T,
        up_grad_share,
        down_share.T,
        outs[0],
        outs[1],
        outs[2],
        outs[3],
        outs[4],
        outs[5],
        outs[6],
        vectors[8, :],
        outs[7],
    )


def solution(mesh):
    sizes = (mesh.shape["dp"], mesh.shape["tensor"])
    split = P("dp", "tensor")
    return jax.shard_map(
        partial(shards, sizes),
        mesh=mesh,
        in_specs=(P("dp", "tensor", None), P("dp", None), split, split, split, P("tensor", "dp"), split, P("tensor", "dp"))
        + (P("dp"),) * 9
        + (P("dp", "tensor", None),),
        out_specs=(P("dp", "tensor", None), P("dp", "tensor", None), split, split, split, P("tensor", "dp"), split, P("tensor", "dp"))
        + (P("dp"),) * 9,
        check_vma=False,
    )
```

```python
from functools import partial
import math

import jax
import jax.numpy as jnp
from jax import lax
from jax.experimental import pallas as pl
from jax.experimental.pallas import tpu as pltpu
from jax.sharding import PartitionSpec as P

HD = 72
EPSILON = 1e-06
GELU_COEF = 0.7978845608028654
MASK_FILL = -1e30
MESH = pl.DeviceIdType.MESH
ANY = pl.BlockSpec(memory_space=pl.ANY)
VM = pl.BlockSpec(memory_space=pltpu.VMEM)
DMA = pltpu.SemaphoreType.DMA
VMEM_BYTES = 60 << 20
F32 = jnp.float32
BF16 = jnp.bfloat16


def remote(src, dst, send_sem, recv_sem, device):
    return pltpu.make_async_remote_copy(
        src_ref=src,
        dst_ref=dst,
        send_sem=send_sem,
        recv_sem=recv_sem,
        device_id=device,
        device_id_type=MESH,
    )


class Place:
    def __init__(self, dp_size, line):
        self.dp_size, self.line, self.chips = dp_size, line, dp_size // 2
        self.dp = lax.axis_index("dp")
        self.z = lax.axis_index("tensor")
        self.core = lax.rem(self.dp, 2)
        self.chip = lax.div(self.dp, 2)
        self.sibling = (2 * self.chip + 1 - self.core, self.z)

    def chip_at(self, k):
        return lax.rem(self.chip + k + self.chips, self.chips)

    def peer(self, k):
        return (2 * self.chip_at(k) + self.core, self.z)

    def along(self, k):
        return (self.dp, lax.rem(self.z + k + self.line, self.line))

    def enter(self, across=True, line=True):
        barrier = pltpu.get_barrier_semaphore()
        devices = []
        if across:
            devices += [self.peer(k) for k in range(1, self.chips)] + [self.sibling]
        if line:
            devices += [self.along(k) for k in range(1, self.line)]
        for device in devices:
            pl.semaphore_signal(barrier, inc=1, device_id=device, device_id_type=MESH)
        pl.semaphore_wait(barrier, len(devices))


class DpGather:
    @staticmethod
    def sems(chips):
        return [DMA((chips,)), DMA((chips,)), DMA((2 * chips,)), DMA(())]

    def __init__(self, place, src, dst, sems, at=None):
        self.p, self.src, self.dst = place, src, dst
        self.across, self.inside, self.recv, self.local = sems
        self.at = at if at is not None else (lambda slot: dst.at[slot])

    def start(self):
        p = self.p
        mine = self.at(p.dp)
        for k in range(1, p.chips):
            remote(self.src, mine, self.across.at[k], self.recv.at[p.dp], p.peer(k)).start()
        remote(self.src, mine, self.inside.at[0], self.recv.at[p.dp], p.sibling).start()
        pltpu.make_async_copy(self.src, mine, self.local).start()

    def forward(self):
        p = self.p
        for k in range(1, p.chips):
            slot = 2 * p.chip_at(-k) + p.core
            block = self.at(slot)
            remote(block, block, self.across.at[k], self.recv.at[slot], p.sibling).wait_recv()
            remote(block, block, self.inside.at[k], self.recv.at[slot], p.sibling).start()

    def finish(self):
        p = self.p
        mine = self.at(p.dp)
        for k in range(p.chips):
            slot = 2 * p.chip_at(-k) + 1 - p.core
            block = self.at(slot)
            remote(block, block, self.inside.at[k], self.recv.at[slot], p.sibling).wait_recv()
        for k in range(p.chips):
            remote(self.src, mine, self.inside.at[k], self.recv.at[0], p.sibling).wait_send()
            if k > 0:
                remote(self.src, mine, self.across.at[k], self.recv.at[0], p.sibling).wait_send()
        pltpu.make_async_copy(self.src, mine, self.local).wait()


class LineGather:
    @staticmethod
    def sems(line):
        return [DMA((line,)), DMA((line,)), DMA((line,)), DMA(())]

    def __init__(self, place, src, dst, sems, rows=None):
        self.p, self.src, self.dst = place, src, dst
        self.right, self.left, self.recv, self.local = sems
        self.at = (lambda slot: dst.at[slot]) if rows is None else (lambda slot: dst.at[slot, pl.ds(0, rows)])

    def send(self, src, slot, step):
        p = self.p

        @pl.when(p.z < p.line - 1)
        def _():
            remote(src, self.at(slot), self.right.at[step], self.recv.at[slot], (p.dp, p.z + 1)).start()

    def send_left(self, src, slot, step):
        p = self.p

        @pl.when(p.z > 0)
        def _():
            remote(src, self.at(slot), self.left.at[step], self.recv.at[slot], (p.dp, p.z - 1)).start()

    def start(self):
        p = self.p
        src = self.at(p.z) if self.src is None else self.src
        self.send(src, p.z, 0)
        self.send_left(src, p.z, 0)
        if self.src is not None:
            pltpu.make_async_copy(self.src, self.at(p.z), self.local).start()

    def arrive(self, slot):
        block = self.at(slot)
        remote(block, block, self.right.at[0], self.recv.at[slot], self.p.sibling).wait_recv()

    def step(self, s):
        p = self.p

        @pl.when(p.z >= s)
        def _():
            self.arrive(p.z - s)
            self.send(self.at(p.z - s), p.z - s, s)

        @pl.when(p.z + s < p.line)
        def _():
            self.arrive(p.z + s)
            self.send_left(self.at(p.z + s), p.z + s, s)

    def finish(self):
        p = self.p
        block = self.at(0)
        for s in range(p.line):

            @pl.when(jnp.logical_and(p.z >= s, p.z < p.line - 1))
            def _():
                remote(block, block, self.right.at[s], self.recv.at[0], p.sibling).wait_send()

            @pl.when(jnp.logical_and(p.z + s < p.line, p.z > 0))
            def _():
                remote(block, block, self.left.at[s], self.recv.at[0], p.sibling).wait_send()

        if self.src is not None:
            pltpu.make_async_copy(self.src, self.at(p.z), self.local).wait()


class LineExchange:
    @staticmethod
    def sems(line):
        return [DMA((line,)), DMA((line,)), DMA(())]

    def __init__(self, place, src, dst, sems):
        self.p, self.src, self.dst = place, src, dst
        self.sent, self.recv, self.local = sems

    def start(self):
        p = self.p
        for k in range(1, p.line):
            to = p.along(k)
            remote(self.src.at[to[1]], self.dst.at[p.z], self.sent.at[k], self.recv.at[p.z], to).start()
        pltpu.make_async_copy(self.src.at[p.z], self.dst.at[p.z], self.local).start()

    def finish(self):
        p = self.p
        for k in range(1, p.line):
            slot = p.along(k)[1]
            block = self.dst.at[slot]
            remote(block, block, self.sent.at[k], self.recv.at[slot], p.sibling).wait_recv()
        for k in range(1, p.line):
            block = self.src.at[0]
            remote(block, block, self.sent.at[k], self.recv.at[0], p.sibling).wait_send()
        pltpu.make_async_copy(self.src.at[p.z], self.dst.at[p.z], self.local).wait()


class LineSum:
    @staticmethod
    def sems(line):
        return [DMA((line,)), DMA((line,)), DMA((line,))]

    def __init__(self, place, part, from_left, from_right, sems):
        self.p, self.part, self.from_left, self.from_right = place, part, from_left, from_right
        self.sent, self.recv_left, self.recv_right = sems

    def add(self, d, got):
        self.part[d] = (self.part[d].astype(F32) + got[d].astype(F32)).astype(BF16)

    def wait(self, got, recv, d):
        remote(got.at[d], got.at[d], self.sent.at[d], recv.at[d], self.p.sibling).wait_recv()

    def move(self, i):
        p = self.p
        d = p.line - 1 - i

        @pl.when(p.z < d)
        def _():
            @pl.when(p.z > 0)
            def _():
                self.wait(self.from_left, self.recv_left, d)
                self.add(d, self.from_left)

            remote(self.part.at[d], self.from_left.at[d], self.sent.at[d], self.recv_left.at[d], (p.dp, p.z + 1)).start()

        @pl.when(p.z > i)
        def _():
            @pl.when(p.z < p.line - 1)
            def _():
                self.wait(self.from_right, self.recv_right, i)
                self.add(i, self.from_right)

            remote(self.part.at[i], self.from_right.at[i], self.sent.at[i], self.recv_right.at[i], (p.dp, p.z - 1)).start()

    def finish(self, out):
        p = self.p
        out[...] = self.part[p.z].astype(F32)

        @pl.when(p.z > 0)
        def _():
            self.wait(self.from_left, self.recv_left, p.z)
            out[...] += self.from_left[p.z].astype(F32)

        @pl.when(p.z < p.line - 1)
        def _():
            self.wait(self.from_right, self.recv_right, p.z)
            out[...] += self.from_right[p.z].astype(F32)

        for d in range(p.line):

            @pl.when(p.z != d)
            def _():
                block = self.part.at[d]
                remote(block, block, self.sent.at[d], self.recv_left.at[d], p.sibling).wait_send()


class DpSum:
    @staticmethod
    def sems(chips):
        return [DMA((chips,)), DMA((chips,)), DMA((chips,)), DMA((chips,))]

    def __init__(self, place, part, near, far, sems):
        self.p, self.part, self.near, self.far = place, part, near, far
        self.sent, self.recv, self.sent_far, self.recv_far = sems

    def start(self):
        p = self.p
        for k in [*range(1, p.chips), 0]:
            chip = p.chip_at(k)
            remote(self.part.at[2 * chip + 1 - p.core], self.near.at[k], self.sent.at[k], self.recv.at[k], p.sibling).start()

    def wait_near(self, k):
        block = self.near.at[k]
        remote(block, block, self.sent.at[k], self.recv.at[k], self.p.sibling).wait_recv()

    def move(self):
        p = self.p
        for k in range(1, p.chips):
            slot = 2 * p.chip_at(k) + p.core
            self.wait_near(k)
            self.part[slot] = (self.part[slot].astype(F32) + self.near[k].astype(F32)).astype(BF16)
            remote(self.part.at[slot], self.far.at[k], self.sent_far.at[k], self.recv_far.at[k], p.peer(k)).start()

    def finish(self):
        p = self.p
        self.wait_near(0)
        total = self.part[p.dp].astype(F32) + self.near[0].astype(F32)
        for k in range(1, p.chips):
            block = self.far.at[k]
            remote(block, block, self.sent_far.at[k], self.recv_far.at[k], p.sibling).wait_recv()
            total += self.far[k].astype(F32)
        for k in range(p.chips):
            block = self.near.at[0]
            remote(block, block, self.sent.at[k], self.recv.at[0], p.sibling).wait_send()
            if k > 0:
                remote(block, block, self.sent_far.at[k], self.recv.at[0], p.sibling).wait_send()
        return total


def params(collective_id):
    return pltpu.CompilerParams(
        collective_id=collective_id, has_side_effects=True, vmem_limit_bytes=VMEM_BYTES
    )


def shape(*dims, dtype=BF16):
    return jax.ShapeDtypeStruct(dims, dtype)


def gather_all(sizes, across, chained, along):
    n, t = sizes
    count = (len(across), len(chained), len(along))

    def kernel(*refs):
        refs = list(refs)
        take = lambda m: [refs.pop(0) for _ in range(m)]
        a_in, c_in, l_in = take(count[0]), take(count[1]), take(count[2])
        a_out, c_out, l_out = take(count[0]), take(count[1]), take(count[2])
        c_mid = take(count[1])
        place = Place(n, t)
        dp_ops = [DpGather(place, s, d, take(4)) for s, d in zip(a_in, a_out)]
        mid_ops = [LineGather(place, s, d, take(4)) for s, d in zip(c_in, c_mid)]
        tail_ops = [DpGather(place, s, d, take(4)) for s, d in zip(c_mid, c_out)]
        line_ops = [LineGather(place, s, d, take(4)) for s, d in zip(l_in, l_out)]
        place.enter()
        for op in mid_ops + line_ops + dp_ops:
            op.start()
        for s in range(1, t):
            for op in mid_ops:
                op.step(s)
        for op in mid_ops:
            op.finish()
        for op in tail_ops:
            op.start()
        for s in range(1, t):
            for op in line_ops:
                op.step(s)
        for op in dp_ops + tail_ops:
            op.forward()
        for op in line_ops + dp_ops + tail_ops:
            op.finish()

    outs = (
        [shape(n, *a.shape, dtype=a.dtype) for a in across]
        + [shape(n, t, *a.shape, dtype=a.dtype) for a in chained]
        + [shape(t, *a.shape, dtype=a.dtype) for a in along]
    )
    scratch = [pltpu.VMEM((t, *a.shape), a.dtype) for a in chained]
    for _ in across:
        scratch += DpGather.sems(n // 2)
    for _ in chained:
        scratch += LineGather.sems(t)
    for _ in chained:
        scratch += DpGather.sems(n // 2)
    for _ in along:
        scratch += LineGather.sems(t)
    return pl.pallas_call(
        kernel,
        out_shape=outs,
        in_specs=[ANY] * sum(count),
        out_specs=[ANY] * sum(count),
        scratch_shapes=scratch,
        compiler_params=params(0),
        name="gather_all",
    )(*across, *chained, *along)


def line_gather(sizes, block, collective_id):
    n, t = sizes

    def kernel(src, dst, *sems):
        place = Place(n, t)
        op = LineGather(place, src, dst, sems)
        place.enter(across=False)
        op.start()
        for s in range(1, t):
            op.step(s)
        op.finish()

    return pl.pallas_call(
        kernel,
        out_shape=shape(t, *block.shape),
        in_specs=[ANY],
        out_specs=ANY,
        scratch_shapes=LineGather.sems(t),
        compiler_params=params(collective_id),
        name="line_gather",
    )(block)


def line_exchange(sizes, blocks, collective_id):
    n, t = sizes

    def kernel(src, dst, *sems):
        place = Place(n, t)
        op = LineExchange(place, src, dst, sems)
        place.enter(across=False)
        op.start()
        op.finish()

    return pl.pallas_call(
        kernel,
        out_shape=shape(*blocks.shape),
        in_specs=[ANY],
        out_specs=ANY,
        scratch_shapes=LineExchange.sems(t),
        compiler_params=params(collective_id),
        name="line_exchange",
    )(blocks)


def line_sum(sizes, parts, collective_id):
    n, t = sizes
    m = len(parts)

    def kernel(*refs):
        refs = list(refs)
        take = lambda c: [refs.pop(0) for _ in range(c)]
        ins, outs, work, left, right = take(m), take(m), take(m), take(m), take(m)
        place = Place(n, t)
        ops = [LineSum(place, *r, take(3)) for r in zip(work, left, right)]
        place.enter(across=False)
        for op, src in zip(ops, ins):
            op.part[...] = src[...]
        for op in ops:
            for i in range(t - 1):
                op.move(i)
        for op, out in zip(ops, outs):
            op.finish(out)

    scratch = [pltpu.VMEM(p.shape, BF16) for _ in range(3) for p in parts]
    for _ in parts:
        scratch += LineSum.sems(t)
    return pl.pallas_call(
        kernel,
        out_shape=[shape(*p.shape[1:], dtype=F32) for p in parts],
        in_specs=[VM] * m,
        out_specs=[VM] * m,
        scratch_shapes=scratch,
        compiler_params=params(collective_id),
        name="line_sum",
    )(*parts)


def sum_all(sizes, across, chained, collective_id):
    n, t = sizes
    chips = n // 2
    m, c = len(across), len(chained)

    def kernel(*refs):
        refs = list(refs)
        take = lambda q: [refs.pop(0) for _ in range(q)]
        ins, outs = take(m + c), take(m + c)
        work, near, far = take(m + c), take(m + c), take(m + c)
        mid, got = take(c), take(c)
        place = Place(n, t)
        ops = [DpSum(place, *r, take(4)) for r in zip(work, near, far)]
        tails = [LineExchange(place, s, d, take(3)) for s, d in zip(mid, got)]
        place.enter()
        order = ops[m:] + ops[:m]
        sources = ins[m:] + ins[:m]
        for op, src in zip(order, sources):
            op.part[...] = src[...]
            op.start()
        for op in order:
            op.move()
        for op, s, tail in zip(ops[m:], mid, tails):
            s[...] = op.finish().astype(BF16)
            tail.start()
        for op, out in zip(ops[:m], outs[:m]):
            out[...] = op.finish()
        for tail, d, out in zip(tails, got, outs[m:]):
            tail.finish()
            out[...] = jnp.sum(d[...].astype(F32), axis=0)

    every = [*across, *chained]
    scratch = [pltpu.VMEM(p.shape, BF16) for p in every]
    scratch += [pltpu.VMEM((chips, *p.shape[1:]), BF16) for _ in range(2) for p in every]
    scratch += [pltpu.VMEM(p.shape[1:], BF16) for _ in range(2) for p in chained]
    for _ in every:
        scratch += DpSum.sems(chips)
    for _ in chained:
        scratch += LineExchange.sems(t)
    outs = [shape(*p.shape[1:], dtype=F32) for p in across] + [shape(*p.shape[2:], dtype=F32) for p in chained]
    return pl.pallas_call(
        kernel,
        out_shape=outs,
        in_specs=[VM] * len(every),
        out_specs=[VM] * len(every),
        scratch_shapes=scratch,
        compiler_params=params(collective_id),
        name="sum_all",
    )(*every)


def vector_sum(sizes, parts, collective_id):
    n, t = sizes

    def kernel(src, out, got, mid, got_line, sent, recv, sent_line, recv_line):
        place = Place(n, t)
        barrier = pltpu.get_barrier_semaphore()
        others = [lax.rem(place.dp + k, n) for k in range(1, n)]
        devices = [(d, place.z) for d in others] + [place.along(k) for k in range(1, t)]
        for device in devices:
            pl.semaphore_signal(barrier, inc=1, device_id=device, device_id_type=MESH)
        pl.semaphore_wait(barrier, len(devices))
        for k in range(1, n):
            remote(src.at[others[k - 1]], got.at[k], sent.at[k], recv.at[k], (others[k - 1], place.z)).start()
        total = src[place.dp]
        for k in range(1, n):
            remote(got.at[k], got.at[k], sent.at[k], recv.at[k], place.sibling).wait()
            total += got[k]
        mid[...] = total
        for k in range(1, t):
            remote(mid, got_line.at[k], sent_line.at[k], recv_line.at[k], place.along(k)).start()
        for k in range(1, t):
            remote(mid, got_line.at[k], sent_line.at[k], recv_line.at[k], place.sibling).wait()
            total += got_line[k]
        out[...] = total

    block = parts.shape[1:]
    return pl.pallas_call(
        kernel,
        out_shape=shape(*block, dtype=F32),
        in_specs=[VM],
        out_specs=VM,
        scratch_shapes=[
            pltpu.VMEM((n, *block), F32),
            pltpu.VMEM(block, F32),
            pltpu.VMEM((t, *block), F32),
            DMA((n,)),
            DMA((n,)),
            DMA((t,)),
            DMA((t,)),
        ],
        compiler_params=params(collective_id),
        name="vector_sum",
    )(parts)


def pad_to(count, unit):
    return -(-count // unit) * unit


def normalize(x):
    centred = x - jnp.mean(x, axis=-1, keepdims=True)
    inv_std = lax.rsqrt(jnp.mean(centred * centred, axis=-1, keepdims=True) + EPSILON)
    return centred * inv_std, inv_std


def dot(left, right, contract):
    return lax.dot_general(left, right, ((contract[:1], contract[1:]), ((), ())), preferred_element_type=F32)


NN, NT, TN = (1, 0), (1, 1), (0, 0)


class Dims:
    def __init__(self, sizes, rows, width, share, cols, hidden, up_share):
        self.n, self.t = sizes
        self.rows, self.width, self.share, self.cols = rows, width, share, cols
        self.hidden, self.up_share = hidden, up_share
        self.heads = cols // HD
        self.block = pad_to(rows, 16)
        self.sent_rows = rows if rows % 8 == 0 else self.block
        self.seq = self.t * self.block
        self.hidden_pad = pad_to(hidden, 128)
        self.vec_lanes = pad_to(max(up_share, share), 128)
        self.packed = self.block // self.t
        self.chunk = 32 if self.block % 32 == 0 else 16


def both_sides(place, s, work):
    def side(i, carry):
        slot = place.z - s + 2 * s * i

        @pl.when(jnp.logical_and(slot >= 0, slot < place.line))
        def _():
            work(slot)

        return carry

    lax.fori_loop(0, 2, side, 0)


def chunks(d, work):
    def one(i, carry):
        work(pl.ds(pl.multiple_of(i * d.chunk, d.chunk), d.chunk))
        return carry

    lax.fori_loop(0, d.block // d.chunk, one, 0)


def attention_forward(d, args):
    n, t, R, D = d.n, d.t, d.block, d.width
    chips = n // 2
    per_line = n // t
    scale_factor = 1.0 / math.sqrt(HD)

    def kernel(*refs):
        refs = list(refs)
        take = lambda m: [refs.pop(0) for _ in range(m)]
        tok, cot, mask, wq, wk, wv, wo, wu, wd = take(9)
        vecs = take(9)
        qh, kh, vh, mix, lse, first, mixed_rows, hidden, second, wqkv, out_t, vec, upb = take(13)
        cot_all, up_all, down_all = take(3)
        tokbuf, w_st, o_mid, o_pack, u_st, d_st, v_st, v_all, c_st, send, got = take(11)
        place = Place(n, t)
        z, dp = place.z, place.dp
        rows_of = lambda ref: (lambda slot: ref.at[pl.ds(pl.multiple_of(slot * d.share, 8), d.share)])
        g_vec = DpGather(place, v_st, v_all, take(4))
        g_qkv = DpGather(place, w_st, wqkv, take(4), rows_of(wqkv))
        g_up = DpGather(place, u_st, up_all, take(4), rows_of(up_all))
        g_down = DpGather(place, d_st, down_all, take(4), rows_of(down_all))
        g_out = DpGather(place, o_pack, out_t, take(4), rows_of(out_t))
        l_tok = LineGather(place, None, tokbuf, take(4), d.sent_rows)
        l_out = LineGather(place, None, o_mid, take(4))
        l_cot = LineGather(place, c_st.at[pl.ds(0, d.sent_rows)], cot_all, take(4), d.sent_rows)
        x_sent, x_recv = take(2)

        def stage_rows(value, store, dtype):
            store(slice(0, d.rows), value)
            if R > d.rows:
                store(slice(d.rows, R), jnp.zeros((R - d.rows, D), dtype))

        if R > d.rows:
            for i in range(t):
                tokbuf[i, d.rows :, :] = jnp.zeros((R - d.rows, D), BF16)
        tokbuf[z, : d.rows, :] = tok[...]
        for i, w in enumerate((wq, wk, wv)):
            w_st[:, i * d.cols : (i + 1) * d.cols] = w[...]
        v_st[...] = jnp.zeros_like(v_st)
        for i, v in enumerate(vecs):
            m = v.shape[0]
            v_st[i : i + 1, :m] = jnp.reshape(v[...].astype(F32), (1, m))
        place.enter()
        l_tok.start()
        g_vec.start()
        g_qkv.start()
        o_mid[z] = wo[...].T
        u_st[...] = jnp.zeros_like(u_st)
        u_st[:, : d.hidden] = wu[...]
        d_st[...] = jnp.zeros_like(d_st)
        d_st[:, : d.hidden] = wd[...].T
        c_st[: d.rows, :] = cot[...]
        if R > d.rows:
            c_st[d.rows :, :] = jnp.zeros((R - d.rows, D), BF16)
        g_vec.forward()
        g_vec.finish()
        for i in range(8):
            vec[i : i + 1, :] = jnp.concatenate([v_all[j, i : i + 1, : d.share] for j in range(n)], axis=1)
        upb[...] = jnp.zeros_like(upb)
        upb[0:1, : d.hidden] = jnp.concatenate(
            [v_all[z * per_line + j, 8:9, : d.up_share] for j in range(per_line)], axis=1
        )
        local = lambda i: jnp.concatenate(
            [v_all[z * per_line + j, i : i + 1, : d.share] for j in range(per_line)], axis=1
        )
        bias_row = jnp.concatenate([local(2), jnp.zeros((1, d.cols), F32), local(3)], axis=1)
        scale_row = jnp.concatenate(
            [jnp.full((1, d.cols), scale_factor, F32), jnp.ones((1, 2 * d.cols), F32)], axis=1
        )
        gain, shift = vec[0:1, :], vec[1:2, :]

        def norm_block(slot):
            def one(r):
                normed = normalize(tokbuf[slot, r, :].astype(F32))[0]
                first[slot, r, :] = (normed * gain + shift).astype(BF16)

            chunks(d, one)

        def project_block(slot):
            y = (dot(first[slot], wqkv[...], NN) + bias_row) * scale_row
            y = y.astype(BF16)
            at = pl.ds(pl.multiple_of(slot * R, R), R)
            for i, ref in enumerate((qh, kh, vh)):
                for j in range(d.heads):
                    start = i * d.cols + j * HD
                    ref[j, at, :] = y[:, start : start + HD]

        norm_block(z)
        l_tok.step(1)
        l_out.start()
        both_sides(place, 1, norm_block)
        g_qkv.forward()
        g_qkv.finish()
        g_up.start()
        project_block(z)
        both_sides(place, 1, project_block)
        for s in range(2, t):
            l_tok.step(s)

            def do(slot):
                norm_block(slot)
                project_block(slot)

            both_sides(place, s, do)
        for s in range(1, t):
            l_out.step(s)
        o_pack[...] = jnp.concatenate([o_mid[i] for i in range(t)], axis=1)
        g_out.start()
        l_cot.start()
        g_up.forward()
        g_down.start()

        count = jnp.sum(mask[...].astype(F32), axis=1, keepdims=True)
        lane = lax.broadcasted_iota(jnp.int32, (1, d.seq), 1)
        blk = sum([(lane >= R * i).astype(jnp.int32) for i in range(1, t)], jnp.zeros((1, d.seq), jnp.int32))
        off = lane - blk * R
        place_of = (off + blk * d.rows).astype(F32)
        valid = jnp.logical_and(off < d.rows, place_of < count)
        valid = jnp.where(valid, 1.0, 0.0)
        head_lane = lax.broadcasted_iota(jnp.int32, (1, 128), 1)

        def attend_rows(r):
            at = pl.ds(pl.multiple_of(r * R, R), R)

            def head(j, carry):
                scores = dot(qh[j, at, :], kh[j], NT)
                scores = jnp.where(valid > 0, scores, MASK_FILL)
                highest = jnp.max(scores, axis=-1, keepdims=True)
                raised = jnp.exp(scores - highest)
                total = jnp.sum(raised, axis=-1, keepdims=True)
                lse[at, :] = jnp.where(head_lane == j, highest + jnp.log(total), lse[at, :])
                probs = (raised * (1.0 / total)).astype(BF16)
                mix[j, at, :] = dot(probs, vh[j], NN).astype(BF16)
                return carry

            lax.fori_loop(0, d.heads, head, 0)
            own = [mix[j, at, :] for j in range(d.heads)]
            piece = lambda i, j: own[j][i * d.packed : (i + 1) * d.packed]
            send[r] = jnp.concatenate([piece(i, j) for i in range(t) for j in range(d.heads)], axis=1)

        lse[...] = jnp.zeros_like(lse)
        for k in range(1, t):
            to = place.along(k)
            attend_rows(to[1])
            remote(send.at[to[1]], got.at[z], x_sent.at[k], x_recv.at[z], to).start()
            if k == 1:
                l_cot.step(1)
            if k == 2:
                g_out.forward()
        attend_rows(z)
        got[z] = send[z]
        g_out.finish()
        for k in range(1, t):
            slot = place.along(k)[1]
            remote(got.at[slot], got.at[slot], x_sent.at[k], x_recv.at[slot], place.sibling).wait_recv()
        for i in range(t):
            mixed_rows[i * d.packed : (i + 1) * d.packed, :] = jnp.concatenate(
                [got[j, :, i * d.cols : (i + 1) * d.cols] for j in range(t)], axis=1
            )
        inputs = tokbuf[z].astype(F32)
        hidden[...] = inputs + dot(mixed_rows[...], out_t[...], NT) + vec[4:5, :]

        def norm_two(r):
            normed = normalize(hidden[r, :])[0]
            second[r, :] = (normed * vec[5:6, :] + vec[6:7, :]).astype(BF16)

        chunks(d, norm_two)
        for s in range(2, t):
            l_cot.step(s)
        g_down.forward()
        for op in (g_up, g_down, l_cot, l_tok, l_out):
            op.finish()
        for k in range(1, t):
            remote(send.at[0], got.at[0], x_sent.at[k], x_recv.at[0], place.sibling).wait_send()

    heads = (d.heads, d.seq, HD)
    outs = [
        shape(*heads),
        shape(*heads),
        shape(*heads),
        shape(*heads),
        shape(d.seq, 128, dtype=F32),
        shape(t, R, D),
        shape(R, D),
        shape(R, D, dtype=F32),
        shape(R, D),
        shape(D, 3 * d.cols),
        shape(D, D),
        shape(16, D, dtype=F32),
        shape(8, d.hidden_pad, dtype=F32),
    ]
    far = [shape(t, R, D), shape(D, d.hidden_pad), shape(D, d.hidden_pad)]
    scratch = [
        pltpu.VMEM((t, R, D), BF16),
        pltpu.VMEM((d.share, 3 * d.cols), BF16),
        pltpu.VMEM((t, d.share, d.cols), BF16),
        pltpu.VMEM((d.share, D), BF16),
        pltpu.VMEM((d.share, d.hidden_pad), BF16),
        pltpu.VMEM((d.share, d.hidden_pad), BF16),
        pltpu.VMEM((16, d.vec_lanes), F32),
        pltpu.VMEM((n, 16, d.vec_lanes), F32),
        pltpu.VMEM((R, D), BF16),
        pltpu.VMEM((t, d.packed, D), BF16),
        pltpu.VMEM((t, d.packed, D), BF16),
    ]
    for _ in range(5):
        scratch += DpGather.sems(chips)
    for _ in range(3):
        scratch += LineGather.sems(t)
    scratch += [DMA((t,)), DMA((t,))]
    return pl.pallas_call(
        kernel,
        out_shape=outs + far,
        in_specs=[VM] * len(args),
        out_specs=[VM] * len(outs) + [ANY] * len(far),
        scratch_shapes=scratch,
        compiler_params=params(0),
        name="attention_forward",
    )(*args)


class LineChain:
    @staticmethod
    def sems(line):
        return [DMA((line,)), DMA((line + 1,))]

    def __init__(self, place, part, inbox, sems):
        self.p, self.part, self.inbox = place, part, inbox
        self.sent, self.recv = sems

    def wait(self, slot):
        block = self.inbox.at[slot]
        remote(block, block, self.sent.at[0], self.recv.at[slot], self.p.sibling).wait_recv()

    def right(self, src, d):
        p = self.p
        remote(src.at[d], self.inbox.at[d], self.sent.at[d], self.recv.at[d], (p.dp, p.z + 1)).start()

    def left(self, src, d):
        p = self.p
        slot = jnp.where(d == p.z - 1, p.line, d)
        remote(src.at[d], self.inbox.at[slot], self.sent.at[d], self.recv.at[slot], (p.dp, p.z - 1)).start()

    def launch_right(self, d):
        @pl.when(self.p.z == 0)
        def _():
            self.right(self.part, d)

    def launch_left(self, d):
        @pl.when(self.p.z == self.p.line - 1)
        def _():
            self.left(self.part, d)

    def relay_right(self, d):
        p = self.p

        @pl.when((p.z > 0) & (p.z < d) & (d < p.line))
        def _():
            self.wait(d)
            self.inbox[d] = (self.inbox[d].astype(F32) + self.part[d].astype(F32)).astype(BF16)
            self.right(self.inbox, d)

    def relay_left(self, d):
        p = self.p

        @pl.when((p.z < p.line - 1) & (p.z > d) & (d >= 0))
        def _():
            self.wait(d)
            self.inbox[d] = (self.inbox[d].astype(F32) + self.part[d].astype(F32)).astype(BF16)
            self.left(self.inbox, d)

    def tick(self, i):
        p = self.p
        self.relay_right(i - p.z)
        self.relay_left(2 * (p.line - 1) - p.z - i)

    def finish(self, out, rows):
        p = self.p
        out[rows, :] = self.part[p.z].astype(F32)

        @pl.when(p.z > 0)
        def _():
            self.wait(p.z)
            out[rows, :] += self.inbox[p.z].astype(F32)

        @pl.when(p.z < p.line - 1)
        def _():
            self.wait(p.line)
            out[rows, :] += self.inbox[p.line].astype(F32)

        for d in range(p.line):

            @pl.when(p.z != d)
            def _():
                block = self.part.at[d]
                remote(block, block, self.sent.at[d], self.recv.at[d], p.sibling).wait_send()


def halves(d):
    cut = pad_to(d.sent_rows // 2, 16)
    return ((0, cut), (cut, d.sent_rows - cut))


def gelu_both(u):
    square = u * u
    tanh_val = jnp.tanh(GELU_COEF * (u + 0.044715 * u * square))
    half = 0.5 * (1.0 + tanh_val)
    slope = half + 0.5 * u * (1.0 - tanh_val * tanh_val) * (GELU_COEF * (1.0 + 3.0 * 0.044715 * square))
    return u * half, slope


def mlp(d, args):
    n, t, R, D, HP = d.n, d.t, d.block, d.width, d.hidden_pad

    def kernel(*refs):
        refs = list(refs)
        take = lambda m: [refs.pop(0) for _ in range(m)]
        second, upb, cot_in, up_in, down_in = take(5)
        grad_second, out_part, up_grad, down_grad, bias_part = take(5)
        sec, cot, up, down, act, pre_grad, part, inbox = take(8)
        place = Place(n, t)
        z = place.z
        gather = LineGather(place, None, sec, take(4), d.sent_rows)
        chains = [
            LineChain(place, part.at[:, pl.ds(lo, m)], inbox.at[:, pl.ds(lo, m)], take(2)) for lo, m in halves(d)
        ]
        (load,) = take(1)
        loads = [
            pltpu.make_async_copy(src, dst, load.at[i])
            for i, (src, dst) in enumerate(((up_in, up), (cot_in, cot), (down_in, down)))
        ]
        for copy in loads:
            copy.start()
        if R > d.rows:
            for i in range(t):
                sec[i, d.rows :, :] = jnp.zeros((R - d.rows, D), BF16)
        sec[z, : d.rows, :] = second[: d.rows, :]
        bias_part[...] = jnp.zeros_like(bias_part)
        place.enter(across=False)
        gather.start()
        for copy in loads:
            copy.wait()
        if R > d.rows:
            for i in range(t):
                cot[i, d.rows :, :] = jnp.zeros((R - d.rows, D), BF16)

        def block(slot):
            pre = dot(sec[slot], up[...], NN) + upb[0:1, :]
            value, slope = gelu_both(pre)
            act[slot] = value.astype(BF16)
            grad = dot(cot[slot], down[...], NN) * slope
            bias_part[0:1, :] += jnp.sum(grad, axis=0, keepdims=True)
            pre_grad[slot] = grad.astype(BF16)
            part[slot] = dot(pre_grad[slot], up[...], NT).astype(BF16)

        block(z)
        for s in range(1, t):
            gather.step(s)
            both_sides(place, s, block)
            for chain in chains:
                chain.launch_right(s)
                chain.launch_left(t - 1 - s)

        def out_block(i):
            out_part[i] = dot(act[i], down[...], NT).astype(BF16)

        def weight_grad(out, left, right, i):
            at = pl.ds(i * width, width)
            value = left[:, :, i * width : (i + 1) * width].reshape(d.seq, width)
            out[at, :] = dot(value, right[...].reshape(d.seq, HP), TN).astype(BF16)

        width = D // 3
        work = [partial(weight_grad, up_grad, sec, pre_grad, i) for i in range(3)]
        work += [partial(weight_grad, down_grad, cot, act, i) for i in range(3)]
        work += [partial(out_block, i) for i in range(t)]
        ticks = [(i, chain) for i in range(3, 2 * t - 2) for chain in chains]
        for i, chain in ticks:
            chain.tick(i)
            if work:
                work.pop(0)()
        for item in work:
            item()
        for (lo, m), chain in zip(halves(d), chains):
            chain.finish(grad_second, pl.ds(lo, m))
        if R > d.sent_rows:
            grad_second[d.sent_rows :, :] = jnp.zeros((R - d.sent_rows, D), F32)
        gather.finish()

    outs = [shape(R, D, dtype=F32), shape(t, R, D), shape(D, HP), shape(D, HP), shape(8, HP, dtype=F32)]
    scratch = [
        pltpu.VMEM((t, R, D), BF16),
        pltpu.VMEM((t, R, D), BF16),
        pltpu.VMEM((D, HP), BF16),
        pltpu.VMEM((D, HP), BF16),
        pltpu.VMEM((t, R, HP), BF16),
        pltpu.VMEM((t, R, HP), BF16),
        pltpu.VMEM((t, R, D), BF16),
        pltpu.VMEM((t + 1, R, D), BF16),
    ]
    scratch += LineGather.sems(t) + LineChain.sems(t) * 2 + [DMA((3,))]
    return pl.pallas_call(
        kernel,
        out_shape=outs,
        in_specs=[VM, VM, ANY, ANY, ANY],
        out_specs=[VM] * len(outs),
        scratch_shapes=scratch,
        compiler_params=params(2),
        name="mlp",
    )(*args)


def norm_forward(inputs, gain_vec, shift_vec):
    centred = inputs - jnp.mean(inputs, axis=-1, keepdims=True)
    inv_std = lax.rsqrt(jnp.mean(centred * centred, axis=-1, keepdims=True) + EPSILON)
    normed = centred * inv_std
    return (normed * gain_vec + shift_vec, normed, inv_std)


def norm_backward(grad_in, normed, inv_std, gain_vec):
    scaled = grad_in * gain_vec
    return inv_std * (
        scaled
        - jnp.mean(scaled, axis=-1, keepdims=True)
        - normed * jnp.mean(scaled * normed, axis=-1, keepdims=True)
    )


def gelu_pair(pre_act):
    tanh_val = jnp.tanh(GELU_COEF * (pre_act + 0.044715 * pre_act * pre_act * pre_act))
    gelu_value = 0.5 * pre_act * (1.0 + tanh_val)
    gelu_slope = 0.5 * (1.0 + tanh_val) + 0.5 * pre_act * (
        1.0 - tanh_val * tanh_val
    ) * GELU_COEF * (1.0 + 3.0 * 0.044715 * pre_act * pre_act)
    return (gelu_value, gelu_slope)


def mat_dot(left, right):
    return jnp.dot(left, right, preferred_element_type=jnp.float32)


def attend(query, keys, values, valid):
    scores = jnp.einsum("qhd,khd->hqk", query, keys, preferred_element_type=jnp.float32)
    scores = jnp.where(valid[None, None, :] > 0, scores, MASK_FILL)
    highest = jnp.max(scores, axis=-1, keepdims=True)
    logsum = highest + jnp.log(jnp.sum(jnp.exp(scores - highest), axis=-1, keepdims=True))
    probs = jnp.exp(scores - logsum).astype(jnp.bfloat16)
    mixed = jnp.einsum("hqk,khd->qhd", probs, values, preferred_element_type=jnp.float32)
    return (mixed.astype(jnp.bfloat16), logsum[..., 0])


def attend_back(scale_factor, query, keys, values, valid, logsum, mixed, grad):
    scores = jnp.einsum("qhd,khd->hqk", query, keys, preferred_element_type=jnp.float32)
    scores = jnp.where(valid[None, None, :] > 0, scores, MASK_FILL)
    probs_full = jnp.exp(scores - logsum[:, :, None])
    probs = probs_full.astype(jnp.bfloat16)
    grad_values = jnp.einsum("hqk,qhd->khd", probs, grad, preferred_element_type=jnp.float32)
    grad_probs = jnp.einsum("qhd,khd->hqk", grad, values, preferred_element_type=jnp.float32)
    delta = jnp.sum(grad.astype(jnp.float32) * mixed.astype(jnp.float32), axis=-1).T
    grad_scores = (probs_full * (grad_probs - delta[:, :, None])).astype(jnp.bfloat16)
    grad_query = (
        jnp.einsum("hqk,khd->qhd", grad_scores, keys, preferred_element_type=jnp.float32)
        * scale_factor
    )
    grad_keys = jnp.einsum("hqk,qhd->khd", grad_scores, query, preferred_element_type=jnp.float32)
    return (grad_query, grad_keys, grad_values)


def shards(
    sizes,
    tokens,
    key_mask,
    query_weight,
    key_weight,
    value_weight,
    out_weight,
    up_weight,
    down_weight,
    first_gain,
    first_shift,
    query_bias,
    value_bias,
    out_bias,
    second_gain,
    second_shift,
    up_bias,
    down_bias,
    cotangent,
):
    n, t = sizes
    z = lax.axis_index("tensor")
    images, rows, width = tokens.shape
    share = first_gain.shape[0]
    up_share = up_bias.shape[0]
    cols = query_weight.shape[1]
    hidden_cols = up_weight.shape[1]
    heads = cols // HD
    seq = t * rows
    scale_factor = 1.0 / math.sqrt(HD)
    d = Dims(sizes, rows, width, share, cols, hidden_cols, up_share)
    small = [first_gain, first_shift, query_bias, value_bias, out_bias, second_gain, second_shift, down_bias]
    (
        qh, kh, vh, mix, lse, first, mixed_rows, hidden, second, wqkv, out_t, vec, upb, cot_all, up_all, down_all,
    ) = attention_forward(
        d,
        [tokens[0], cotangent[0], key_mask, query_weight, key_weight, value_weight, out_weight, up_weight, down_weight]
        + small + [up_bias],
    )
    tight = lambda a: a.reshape(t, d.block, -1)[:, :rows].reshape(seq, -1)
    by_head = lambda a: a.reshape(heads, t, d.block, HD)[:, :, :rows].reshape(heads, seq, HD).transpose(1, 0, 2)
    query, keys, values, mixed = by_head(qh), by_head(kh), by_head(vh), by_head(mix)
    logsum = tight(lse)[:, :heads].T
    first = tight(first)
    mixed_rows = mixed_rows[:rows].reshape(rows, t, cols).transpose(1, 0, 2)
    grad_second, out_part, up_grad, down_grad, bias_part = mlp(d, [second, upb, cot_all, up_all, down_all])
    hidden = hidden[:rows]
    grad_second = grad_second[:rows]
    up_bias_part = bias_part[0, :hidden_cols]
    up_grad = up_grad[:, :hidden_cols]
    down_grad = down_grad[:, :hidden_cols]
    qkv_full = wqkv
    out_full = out_t.reshape(width, t, cols).transpose(1, 0, 2)
    up_full, down_full = up_all[:, :hidden_cols], down_all[:, :hidden_cols]
    gain_one, shift_one, query_bias_all, value_bias_all, out_bias_all, gain_two, shift_two, down_bias_all = [
        vec[i] for i in range(8)
    ]
    up_bias_all = jnp.zeros((n * up_share,), F32)
    up_bias_local = upb[0, :hidden_cols]
    head_shape = (seq, heads, HD)
    grad_rows = cot_all[:, :rows]
    inputs = tokens[0].astype(F32)
    normed_one, inv_one = norm_forward(inputs, gain_one, shift_one)[1:]
    normed_two, inv_two = norm_forward(hidden, gain_two, shift_two)[1:]
    (mlp_out,) = line_sum(sizes, [out_part[:, :rows]], 3)
    output = (hidden + mlp_out + down_bias_all).astype(BF16)
    grad_out = cotangent[0].astype(F32)
    down_bias_grad = jnp.sum(grad_out, axis=0)
    second_gain_grad = jnp.sum(grad_second * normed_two, axis=0)
    second_shift_grad = jnp.sum(grad_second, axis=0)
    grad_hidden = grad_out + norm_backward(grad_second, normed_two, inv_two, gain_two)
    out_bias_grad = jnp.sum(grad_hidden, axis=0)
    hidden_low = grad_hidden.astype(BF16)
    grad_mixed_rows = jnp.einsum("rd,tdc->trc", hidden_low, out_full, preferred_element_type=F32).astype(BF16)
    out_grad = jnp.einsum("rd,trc->tdc", hidden_low, mixed_rows, preferred_element_type=F32).astype(BF16)
    grad_mixed = line_exchange(sizes, grad_mixed_rows, 4).reshape(head_shape)
    grad_query_f, grad_keys_f, grad_values_f = attend_back(
        scale_factor, query, keys, values, key_mask[0], logsum, mixed, grad_mixed
    )
    grad_query_f = grad_query_f.reshape(seq, cols)
    grad_keys_f = grad_keys_f.reshape(seq, cols)
    grad_values_f = grad_values_f.reshape(seq, cols)
    query_bias_part = jnp.sum(grad_query_f, axis=0)
    value_bias_part = jnp.sum(grad_values_f, axis=0)
    grad_qkv = jnp.concatenate([g.astype(BF16) for g in (grad_query_f, grad_keys_f, grad_values_f)], axis=1)
    first_part = mat_dot(grad_qkv, qkv_full.T).astype(BF16)
    (grad_first,) = line_sum(sizes, [first_part.reshape(t, rows, width)], 5)
    qkv_grad = mat_dot(first.T, grad_qkv).astype(BF16)
    qkv_share, up_grad_share, down_share, out_share = sum_all(
        sizes,
        [
            qkv_grad.reshape(n, share, 3 * cols),
            up_grad.reshape(n, share, hidden_cols),
            down_grad.reshape(n, share, hidden_cols),
        ],
        [out_grad.reshape(t, n, share, cols).transpose(1, 0, 2, 3)],
        6,
    )
    first_gain_grad = jnp.sum(grad_first * normed_one, axis=0)
    first_shift_grad = jnp.sum(grad_first, axis=0)
    input_grad = grad_hidden + norm_backward(grad_first, normed_one, inv_one, gain_one)
    placed = lambda part, full: lax.dynamic_update_slice_in_dim(
        jnp.zeros((full,), F32), part, z * part.shape[0], 0
    )
    wide = jnp.stack(
        [
            first_gain_grad,
            first_shift_grad,
            placed(query_bias_part, width),
            placed(value_bias_part, width),
            out_bias_grad,
            second_gain_grad,
            second_shift_grad,
            down_bias_grad,
        ]
    ).reshape(8, n, share)
    wide = jnp.pad(wide, ((0, 0), (0, 0), (0, up_share - share)))
    last = placed(up_bias_part, up_bias_all.shape[0]).reshape(1, n, up_share)
    wide = jnp.pad(jnp.concatenate([wide, last]), ((0, 7), (0, 0), (0, 0))).transpose(1, 0, 2)
    vectors = vector_sum(sizes, wide, 7)
    outs = [vectors[i, :share] for i in range(8)]
    return (
        output[None],
        input_grad[None],
        qkv_share[:, :cols],
        qkv_share[:, cols : 2 * cols],
        qkv_share[:, 2 * cols :],
        out_share.T,
        up_grad_share,
        down_share.T,
        outs[0],
        outs[1],
        outs[2],
        outs[3],
        outs[4],
        outs[5],
        outs[6],
        vectors[8, :],
        outs[7],
    )


def solution(mesh):
    sizes = (mesh.shape["dp"], mesh.shape["tensor"])
    split = P("dp", "tensor")
    return jax.shard_map(
        partial(shards, sizes),
        mesh=mesh,
        in_specs=(P("dp", "tensor", None), P("dp", None), split, split, split, P("tensor", "dp"), split, P("tensor", "dp"))
        + (P("dp"),) * 9
        + (P("dp", "tensor", None),),
        out_specs=(P("dp", "tensor", None), P("dp", "tensor", None), split, split, split, P("tensor", "dp"), split, P("tensor", "dp"))
        + (P("dp"),) * 9,
        check_vma=False,
    )
```

```python
from functools import partial
import math

import jax
import jax.numpy as jnp
from jax import lax
from jax.experimental import pallas as pl
from jax.experimental.pallas import tpu as pltpu
from jax.sharding import PartitionSpec as P

HD = 72
EPSILON = 1e-06
GELU_COEF = 0.7978845608028654
MASK_FILL = -1e30
MESH = pl.DeviceIdType.MESH
ANY = pl.BlockSpec(memory_space=pl.ANY)
VM = pl.BlockSpec(memory_space=pltpu.VMEM)
DMA = pltpu.SemaphoreType.DMA
VMEM_BYTES = 60 << 20
F32 = jnp.float32
BF16 = jnp.bfloat16


def remote(src, dst, send_sem, recv_sem, device):
    return pltpu.make_async_remote_copy(
        src_ref=src,
        dst_ref=dst,
        send_sem=send_sem,
        recv_sem=recv_sem,
        device_id=device,
        device_id_type=MESH,
    )


class Place:
    def __init__(self, dp_size, line):
        self.dp_size, self.line, self.chips = dp_size, line, dp_size // 2
        self.dp = lax.axis_index("dp")
        self.z = lax.axis_index("tensor")
        self.core = lax.rem(self.dp, 2)
        self.chip = lax.div(self.dp, 2)
        self.sibling = (2 * self.chip + 1 - self.core, self.z)

    def chip_at(self, k):
        return lax.rem(self.chip + k + self.chips, self.chips)

    def peer(self, k):
        return (2 * self.chip_at(k) + self.core, self.z)

    def along(self, k):
        return (self.dp, lax.rem(self.z + k + self.line, self.line))

    def enter(self, across=True, line=True, every=False):
        barrier = pltpu.get_barrier_semaphore()
        devices = []
        if every:
            devices += [(lax.rem(self.dp + k, self.dp_size), self.z) for k in range(1, self.dp_size)]
        elif across:
            devices += [self.peer(k) for k in range(1, self.chips)] + [self.sibling]
        if line:
            devices += [self.along(k) for k in range(1, self.line)]
        for device in devices:
            pl.semaphore_signal(barrier, inc=1, device_id=device, device_id_type=MESH)
        pl.semaphore_wait(barrier, len(devices))


class DpGather:
    @staticmethod
    def sems(chips):
        return [DMA((chips,)), DMA((chips,)), DMA((2 * chips,)), DMA(())]

    def __init__(self, place, src, dst, sems, at=None):
        self.p, self.src, self.dst = place, src, dst
        self.across, self.inside, self.recv, self.local = sems
        self.at = at if at is not None else (lambda slot: dst.at[slot])

    def start(self):
        p = self.p
        mine = self.at(p.dp)
        for k in range(1, p.chips):
            remote(self.src, mine, self.across.at[k], self.recv.at[p.dp], p.peer(k)).start()
        remote(self.src, mine, self.inside.at[0], self.recv.at[p.dp], p.sibling).start()
        pltpu.make_async_copy(self.src, mine, self.local).start()

    def forward(self):
        p = self.p
        for k in range(1, p.chips):
            slot = 2 * p.chip_at(-k) + p.core
            block = self.at(slot)
            remote(block, block, self.across.at[k], self.recv.at[slot], p.sibling).wait_recv()
            remote(block, block, self.inside.at[k], self.recv.at[slot], p.sibling).start()

    def finish(self):
        p = self.p
        mine = self.at(p.dp)
        for k in range(p.chips):
            slot = 2 * p.chip_at(-k) + 1 - p.core
            block = self.at(slot)
            remote(block, block, self.inside.at[k], self.recv.at[slot], p.sibling).wait_recv()
        for k in range(p.chips):
            remote(self.src, mine, self.inside.at[k], self.recv.at[0], p.sibling).wait_send()
            if k > 0:
                remote(self.src, mine, self.across.at[k], self.recv.at[0], p.sibling).wait_send()
        pltpu.make_async_copy(self.src, mine, self.local).wait()


class LineGather:
    @staticmethod
    def sems(line, many=()):
        return [DMA((*many, line)), DMA((*many, line)), DMA((*many, line))]

    def __init__(self, place, dst, sems, rows=None):
        self.p, self.dst = place, dst
        self.right, self.left, self.recv = sems
        self.at = (lambda slot: dst.at[slot]) if rows is None else (lambda slot: dst.at[slot, pl.ds(0, rows)])

    def send_right(self, slot):
        p = self.p
        block = self.at(slot)

        @pl.when(p.z < p.line - 1)
        def _():
            remote(block, block, self.right.at[slot], self.recv.at[slot], (p.dp, p.z + 1)).start()

    def send_left(self, slot):
        p = self.p
        block = self.at(slot)

        @pl.when(p.z > 0)
        def _():
            remote(block, block, self.left.at[slot], self.recv.at[slot], (p.dp, p.z - 1)).start()

    def start(self):
        self.send_right(self.p.z)
        self.send_left(self.p.z)

    def arrive(self, slot):
        block = self.at(slot)
        remote(block, block, self.right.at[slot], self.recv.at[slot], self.p.sibling).wait_recv()

    def relay(self, slot):
        p = self.p

        @pl.when(jnp.logical_and(p.z > slot, slot >= 0))
        def _():
            self.arrive(slot)
            self.send_right(slot)

        @pl.when(jnp.logical_and(p.z < slot, slot < p.line))
        def _():
            self.arrive(slot)
            self.send_left(slot)

    def step(self, s):
        self.relay(self.p.z - s)
        self.relay(self.p.z + s)

    def finish(self):
        p = self.p
        for slot in range(p.line):
            block = self.at(slot)

            @pl.when(jnp.logical_and(p.z >= slot, p.z < p.line - 1))
            def _():
                remote(block, block, self.right.at[slot], self.recv.at[slot], p.sibling).wait_send()

            @pl.when(jnp.logical_and(p.z <= slot, p.z > 0))
            def _():
                remote(block, block, self.left.at[slot], self.recv.at[slot], p.sibling).wait_send()


class DirectGather:
    @staticmethod
    def sems(line, many=()):
        return [DMA((*many, line)), DMA((*many, line))]

    def __init__(self, place, dst, sems):
        self.p, self.dst = place, dst
        self.sent, self.recv = sems

    def start(self):
        p = self.p
        block = self.dst.at[p.z]
        for k in range(1, p.line):
            remote(block, block, self.sent.at[k], self.recv.at[p.z], p.along(k)).start()

    def finish(self):
        p = self.p
        for k in range(1, p.line):
            slot = p.along(k)[1]
            block = self.dst.at[slot]
            remote(block, block, self.sent.at[k], self.recv.at[slot], p.sibling).wait()


class LineExchange:
    @staticmethod
    def sems(line):
        return [DMA((line,)), DMA((line,)), DMA(())]

    def __init__(self, place, src, dst, sems):
        self.p, self.src, self.dst = place, src, dst
        self.sent, self.recv, self.local = sems

    def start(self):
        p = self.p
        for k in range(1, p.line):
            to = p.along(k)
            remote(self.src.at[to[1]], self.dst.at[p.z], self.sent.at[k], self.recv.at[p.z], to).start()
        pltpu.make_async_copy(self.src.at[p.z], self.dst.at[p.z], self.local).start()

    def finish(self):
        p = self.p
        for k in range(1, p.line):
            slot = p.along(k)[1]
            block = self.dst.at[slot]
            remote(block, block, self.sent.at[k], self.recv.at[slot], p.sibling).wait_recv()
        for k in range(1, p.line):
            block = self.src.at[0]
            remote(block, block, self.sent.at[k], self.recv.at[0], p.sibling).wait_send()
        pltpu.make_async_copy(self.src.at[p.z], self.dst.at[p.z], self.local).wait()


def params(collective_id):
    return pltpu.CompilerParams(
        collective_id=collective_id, has_side_effects=True, vmem_limit_bytes=VMEM_BYTES
    )


def shape(*dims, dtype=BF16):
    return jax.ShapeDtypeStruct(dims, dtype)


def pad_to(count, unit):
    return -(-count // unit) * unit


def normalize(x):
    centred = x - jnp.mean(x, axis=-1, keepdims=True)
    inv_std = lax.rsqrt(jnp.mean(centred * centred, axis=-1, keepdims=True) + EPSILON)
    return centred * inv_std, inv_std


def dot(left, right, contract):
    return lax.dot_general(left, right, ((contract[:1], contract[1:]), ((), ())), preferred_element_type=F32)


NN, NT, TN = (1, 0), (1, 1), (0, 0)


class Dims:
    def __init__(self, sizes, rows, width, share, cols, hidden, up_share):
        self.n, self.t = sizes
        self.rows, self.width, self.share, self.cols = rows, width, share, cols
        self.hidden, self.up_share = hidden, up_share
        self.heads = cols // HD
        self.block = pad_to(rows, 16)
        self.sent_rows = rows if rows % 8 == 0 else self.block
        self.seq = self.t * self.block
        self.hidden_pad = pad_to(hidden, 128)
        self.vec_lanes = pad_to(max(up_share, share), 128)
        self.packed = self.block // self.t
        self.chunk = 32 if self.block % 32 == 0 else 16


def both_sides(place, s, work):
    def side(i, carry):
        slot = place.z - s + 2 * s * i

        @pl.when(jnp.logical_and(slot >= 0, slot < place.line))
        def _():
            work(slot)

        return carry

    lax.fori_loop(0, 2, side, 0)


def chunks(d, work):
    def one(i, carry):
        work(pl.ds(pl.multiple_of(i * d.chunk, d.chunk), d.chunk))
        return carry

    lax.fori_loop(0, d.block // d.chunk, one, 0)


def valid_keys(d, count):
    lane = lax.broadcasted_iota(jnp.int32, (1, d.seq), 1)
    zero = jnp.zeros((1, d.seq), jnp.int32)
    blk = sum([(lane >= d.block * i).astype(jnp.int32) for i in range(1, d.t)], zero)
    off = lane - blk * d.block
    inside = jnp.logical_and(off < d.rows, (off + blk * d.rows).astype(F32) < count)
    return jnp.where(inside, 1.0, 0.0)


class LineChain:
    @staticmethod
    def sems(line):
        return [DMA((line,)), DMA((line + 1,))]

    def __init__(self, place, part, inbox, sems):
        self.p, self.part, self.inbox = place, part, inbox
        self.sent, self.recv = sems

    def wait(self, slot):
        block = self.inbox.at[slot]
        remote(block, block, self.sent.at[0], self.recv.at[slot], self.p.sibling).wait_recv()

    def right(self, src, d):
        p = self.p
        remote(src.at[d], self.inbox.at[d], self.sent.at[d], self.recv.at[d], (p.dp, p.z + 1)).start()

    def left(self, src, d):
        p = self.p
        slot = jnp.where(d == p.z - 1, p.line, d)
        remote(src.at[d], self.inbox.at[slot], self.sent.at[d], self.recv.at[slot], (p.dp, p.z - 1)).start()

    def launch_right(self, d):
        @pl.when(self.p.z == 0)
        def _():
            self.right(self.part, d)

    def launch_left(self, d):
        @pl.when(self.p.z == self.p.line - 1)
        def _():
            self.left(self.part, d)

    def relay_right(self, d):
        p = self.p

        @pl.when((p.z > 0) & (p.z < d) & (d < p.line))
        def _():
            self.wait(d)
            self.inbox[d] = (self.inbox[d].astype(F32) + self.part[d].astype(F32)).astype(BF16)
            self.right(self.inbox, d)

    def relay_left(self, d):
        p = self.p

        @pl.when((p.z < p.line - 1) & (p.z > d) & (d >= 0))
        def _():
            self.wait(d)
            self.inbox[d] = (self.inbox[d].astype(F32) + self.part[d].astype(F32)).astype(BF16)
            self.left(self.inbox, d)

    def hop(self, h, d):
        p = self.p

        @pl.when(p.z == h)
        def _():
            self.relay_right(d)

        @pl.when(p.z == p.line - 1 - h)
        def _():
            self.relay_left(d)

    def tick_far(self, i):
        p = self.p
        self.relay_right(p.line - 1 + p.z - i)
        self.relay_left(i - p.line + 1 + p.z)

    def finish(self, out, rows):
        p = self.p
        out[rows, :] = self.part[p.z].astype(F32)

        @pl.when(p.z > 0)
        def _():
            self.wait(p.z)
            out[rows, :] += self.inbox[p.z].astype(F32)

        @pl.when(p.z < p.line - 1)
        def _():
            self.wait(p.line)
            out[rows, :] += self.inbox[p.line].astype(F32)

        for d in range(p.line):

            @pl.when(p.z != d)
            def _():
                block = self.part.at[d]
                remote(block, block, self.sent.at[d], self.recv.at[d], p.sibling).wait_send()


def halves(d):
    cut = pad_to(d.sent_rows // 2, 16)
    return ((0, cut), (cut, d.sent_rows - cut))


def gelu_both(u):
    square = u * u
    tanh_val = jnp.tanh(GELU_COEF * (u + 0.044715 * u * square))
    half = 0.5 * (1.0 + tanh_val)
    slope = half + 0.5 * u * (1.0 - tanh_val * tanh_val) * (GELU_COEF * (1.0 + 3.0 * 0.044715 * square))
    return u * half, slope


def forward(d, args):
    n, t, R, D, HP = d.n, d.t, d.block, d.width, d.hidden_pad
    chips = n // 2
    per_line = n // t
    scale_factor = 1.0 / math.sqrt(HD)
    split = halves(d)

    def kernel(*refs):
        refs = list(refs)
        take = lambda m: [refs.pop(0) for _ in range(m)]
        tok, cot_in, mask, wq, wk, wv, wo, wu, wd = take(9)
        vecs = take(9)
        vec, hidden, mixed_rows, grad_second, bias_part = take(5)
        kept_out = take(10)
        kept = take(10)
        qh, kh, vh, mix, probs, first, wqkv, out_t, grads, o_part = kept
        tokbuf, w_st, o_mid, o_pack, u_st, d_st, v_st, v_all = take(8)
        mixbuf, second, cot, up, down, act, pre_grad, part, inbox, upb, total = take(11)
        place = Place(n, t)
        z = place.z
        rows_of = lambda ref: (lambda slot: ref.at[pl.ds(pl.multiple_of(slot * d.share, 8), d.share)])
        g_vec = DpGather(place, v_st, v_all, take(4))
        g_qkv = DpGather(place, w_st, wqkv, take(4), rows_of(wqkv))
        g_up = DpGather(place, u_st, up, take(4), rows_of(up))
        g_down = DpGather(place, d_st, down, take(4), rows_of(down))
        g_out = DpGather(place, o_pack, out_t, take(4), rows_of(out_t))
        l_tok = LineGather(place, tokbuf, take(3), d.sent_rows)
        l_out = DirectGather(place, o_mid, take(2))
        l_cot = LineGather(place, cot, take(3), d.sent_rows)
        mix_sems = take(2)
        l_mix = lambda r: DirectGather(place, mixbuf.at[r], [sem.at[r] for sem in mix_sems])
        view = lambda ref, lo, m: ref.at[:, pl.ds(lo, m)]
        chains = [LineChain(place, view(part, *h), view(inbox, *h), take(2)) for h in split]
        (kept_sems,) = take(1)

        def keep(*names):
            for i in names:
                pltpu.make_async_copy(kept[i], kept_out[i], kept_sems.at[i]).start()

        if R > d.rows:
            for i in range(t):
                tokbuf[i, d.rows :, :] = jnp.zeros((R - d.rows, D), BF16)
                cot[i, d.rows :, :] = jnp.zeros((R - d.rows, D), BF16)
        tokbuf[z, : d.rows, :] = tok[...]
        cot[z, : d.rows, :] = cot_in[...]
        for i, w in enumerate((wq, wk, wv)):
            w_st[:, i * d.cols : (i + 1) * d.cols] = w[...]
        v_st[...] = jnp.zeros_like(v_st)
        for i, v in enumerate(vecs):
            m = v.shape[0]
            v_st[i : i + 1, :m] = jnp.reshape(v[...].astype(F32), (1, m))
        o_mid[z] = wo[...]
        place.enter()
        l_out.start()
        g_vec.start()
        g_qkv.start()
        l_tok.start()
        at_end = jnp.logical_or(z == 0, z == t - 1)

        @pl.when(at_end)
        def _():
            l_cot.start()

        u_st[...] = jnp.zeros_like(u_st)
        u_st[:, : d.hidden] = wu[...]
        d_st[...] = jnp.zeros_like(d_st)
        d_st[:, : d.hidden] = wd[...]
        bias_part[...] = jnp.zeros_like(bias_part)
        g_vec.forward()
        g_vec.finish()
        for i in range(8):
            vec[i : i + 1, :] = jnp.concatenate([v_all[j, i : i + 1, : d.share] for j in range(n)], axis=1)
        upb[...] = jnp.zeros_like(upb)
        upb[0:1, : d.hidden] = jnp.concatenate(
            [v_all[z * per_line + j, 8:9, : d.up_share] for j in range(per_line)], axis=1
        )
        local = lambda i: jnp.concatenate(
            [v_all[z * per_line + j, i : i + 1, : d.share] for j in range(per_line)], axis=1
        )
        bias_row = jnp.concatenate([local(2), jnp.zeros((1, d.cols), F32), local(3)], axis=1)
        scale_row = jnp.concatenate(
            [jnp.full((1, d.cols), scale_factor, F32), jnp.ones((1, 2 * d.cols), F32)], axis=1
        )
        gain, shift = vec[0:1, :], vec[1:2, :]

        def norm_block(slot):
            def one(r):
                normed = normalize(tokbuf[slot, r, :].astype(F32))[0]
                first[slot, r, :] = (normed * gain + shift).astype(BF16)

            chunks(d, one)

        def project_block(slot):
            y = (dot(first[slot], wqkv[...], NN) + bias_row) * scale_row
            y = y.astype(BF16)
            at = pl.ds(pl.multiple_of(slot * R, R), R)
            for i, ref in enumerate((qh, kh, vh)):
                for j in range(d.heads):
                    start = i * d.cols + j * HD
                    ref[j, at, :] = y[:, start : start + HD]

        norm_block(z)
        l_out.finish()
        o_pack[...] = jnp.concatenate([o_mid[i] for i in range(t)], axis=1)
        g_out.start()
        l_tok.step(1)
        g_qkv.forward()
        g_up.start()
        g_down.start()
        both_sides(place, 1, norm_block)
        g_qkv.finish()
        project_block(z)
        both_sides(place, 1, project_block)

        def norm_and_project(slot):
            norm_block(slot)
            project_block(slot)

        for s in range(2, t):
            l_tok.step(s)

            @pl.when(z == s - 1)
            def _():
                l_cot.relay(0)

            @pl.when(z == t - s)
            def _():
                l_cot.relay(t - 1)

            if s == 2:

                @pl.when(jnp.logical_not(at_end))
                def _():
                    l_cot.start()

            if s == 2:
                g_out.forward()
            both_sides(place, s, norm_and_project)
        g_up.forward()
        keep(0, 1, 2, 5, 6)

        count = jnp.sum(mask[...].astype(F32), axis=1, keepdims=True)
        valid = valid_keys(d, count)
        order = lambda i: jnp.where(lax.rem(i, 2) == 0, lax.div(i, 2), t - 1 - lax.div(i, 2))

        def attend_rows(i, carry):
            r = order(i)
            at = pl.ds(pl.multiple_of(r * R, R), R)

            def head(j, carry):
                scores = dot(qh[j, at, :], kh[j], NT)
                scores = jnp.where(valid > 0, scores, MASK_FILL)
                highest = jnp.max(scores, axis=-1, keepdims=True)
                raised = jnp.exp(scores - highest)
                share = 1.0 / jnp.sum(raised, axis=-1, keepdims=True)
                probs[j, at, :] = (raised * share).astype(BF16)
                mix[j, at, :] = dot(probs[j, at, :], vh[j], NN).astype(BF16)
                return carry

            lax.fori_loop(0, d.heads, head, 0)
            own = [mix[j, at, :] for j in range(d.heads)]
            piece = lambda i, j: own[j][i * d.packed : (i + 1) * d.packed]
            mixbuf[r, z] = jnp.concatenate([piece(i, j) for i in range(t) for j in range(d.heads)], axis=1)
            l_mix(r).start()

            @pl.when(jnp.logical_and(i == 1, jnp.logical_not(at_end)))
            def _():
                for slot in range(1, t - 1):
                    l_cot.relay(slot)

            return carry

        lax.fori_loop(0, t, attend_rows, 0)
        keep(3, 4)
        g_up.finish()
        g_out.finish()
        keep(7)

        def block(i, carry):
            r = order(i)
            l_mix(r).finish()

            rows = jnp.concatenate(
                [
                    jnp.concatenate([mixbuf[r, j, :, k * d.cols : (k + 1) * d.cols] for j in range(t)], axis=1)
                    for k in range(t)
                ],
                axis=0,
            )
            total[...] = tokbuf[r].astype(F32) + dot(rows, out_t[...], NT) + vec[4:5, :]

            @pl.when(r == z)
            def _():
                hidden[...] = total[...]
                mixed_rows[...] = rows

            def norm_two(c):
                normed = normalize(total[c, :])[0]
                second[r, c, :] = (normed * vec[5:6, :] + vec[6:7, :]).astype(BF16)

            chunks(d, norm_two)
            pre = dot(second[r], up[...], NN) + upb[0:1, :]
            value, slope = gelu_both(pre)
            act[r] = value.astype(BF16)

            @pl.when(at_end)
            def _():
                l_cot.relay(r)

            @pl.when(i == 0)
            def _():
                g_down.forward()
                g_down.finish()

            grad = dot(cot[r], down[...], NN) * slope
            bias_part[0:1, :] += jnp.sum(grad, axis=0, keepdims=True)
            pre_grad[r] = grad.astype(BF16)
            part[r] = dot(pre_grad[r], up[...], NT).astype(BF16)

            def launch(these):
                for chain in these:

                    @pl.when(r > 0)
                    def _():
                        chain.launch_right(r)

                    @pl.when(r < t - 1)
                    def _():
                        chain.launch_left(r)

            launch(chains)
            o_part[r] = dot(act[r], down[...], NT).astype(BF16)
            for h in range(1, t - 1):

                @pl.when(i >= h)
                def _():
                    for chain in chains:
                        chain.hop(h, order(i - h))

            return carry

        lax.fori_loop(0, t, block, 0)

        width = D // 3

        def weight_grad(k, left, right, i):
            value = left[:, :, i * width : (i + 1) * width].reshape(d.seq, width)
            grads[k, i * width : (i + 1) * width, :] = dot(value, right[...].reshape(d.seq, HP), TN).astype(BF16)

        work = [partial(weight_grad, 0, second, pre_grad, i) for i in range(3)]
        work += [partial(weight_grad, 1, cot, act, i) for i in range(3)]
        for i in range(t, 2 * t - 2):
            work.pop(0)()
            for h in range(i - t + 1, t - 1):
                for chain in chains:
                    chain.hop(h, order(i - h))
        for item in work:
            item()
        keep(8, 9)
        for (lo, m), chain in zip(split, chains):
            chain.finish(grad_second, pl.ds(lo, m))
        if R > d.sent_rows:
            grad_second[d.sent_rows :, :] = jnp.zeros((R - d.sent_rows, D), F32)
        for op in (l_tok, l_cot):
            op.finish()
        for i in range(10):
            pltpu.make_async_copy(kept[i], kept_out[i], kept_sems.at[i]).wait()

    heads = (d.heads, d.seq, HD)
    outs = [
        shape(16, D, dtype=F32),
        shape(R, D, dtype=F32),
        shape(R, D),
        shape(R, D, dtype=F32),
        shape(8, HP, dtype=F32),
    ]
    kept = [
        shape(*heads),
        shape(*heads),
        shape(*heads),
        shape(*heads),
        shape(d.heads, d.seq, d.seq),
        shape(t, R, D),
        shape(D, 3 * d.cols),
        shape(D, D),
        shape(2, D, HP),
        shape(t, R, D),
    ]
    scratch = [pltpu.VMEM(a.shape, a.dtype) for a in kept]
    scratch += [
        pltpu.VMEM((t, R, D), BF16),
        pltpu.VMEM((d.share, 3 * d.cols), BF16),
        pltpu.VMEM((t, d.share, d.cols), BF16),
        pltpu.VMEM((d.share, D), BF16),
        pltpu.VMEM((d.share, HP), BF16),
        pltpu.VMEM((d.share, HP), BF16),
        pltpu.VMEM((16, d.vec_lanes), F32),
        pltpu.VMEM((n, 16, d.vec_lanes), F32),
        pltpu.VMEM((t, t, d.packed, D), BF16),
        pltpu.VMEM((t, R, D), BF16),
        pltpu.VMEM((t, R, D), BF16),
        pltpu.VMEM((D, HP), BF16),
        pltpu.VMEM((D, HP), BF16),
        pltpu.VMEM((t, R, HP), BF16),
        pltpu.VMEM((t, R, HP), BF16),
        pltpu.VMEM((t, R, D), BF16),
        pltpu.VMEM((t + 1, R, D), BF16),
        pltpu.VMEM((8, HP), F32),
        pltpu.VMEM((R, D), F32),
    ]
    for _ in range(5):
        scratch += DpGather.sems(chips)
    scratch += LineGather.sems(t) + DirectGather.sems(t) + LineGather.sems(t) + DirectGather.sems(t, (t,))
    scratch += LineChain.sems(t) * 2 + [DMA((10,))]
    return pl.pallas_call(
        kernel,
        out_shape=outs + kept,
        in_specs=[VM] * len(args),
        out_specs=[VM] * len(outs) + [ANY] * len(kept),
        scratch_shapes=scratch,
        compiler_params=params(0),
        name="forward",
    )(*args)


class DpAdd:
    @staticmethod
    def sems(chips):
        return [DMA((chips,)), DMA((chips,)), DMA((chips,)), DMA((chips,))]

    def __init__(self, place, part, rows, near, far, sems):
        self.p, self.part, self.rows, self.near, self.far = place, part, rows, near, far
        self.sent, self.recv, self.sent_far, self.recv_far = sems

    def at(self, slot):
        return pl.ds(pl.multiple_of(slot * self.rows, 8), self.rows)

    def start(self):
        p = self.p
        for k in [*range(1, p.chips), 0]:
            src = self.part.at[self.at(2 * p.chip_at(k) + 1 - p.core)]
            remote(src, self.near.at[k], self.sent.at[k], self.recv.at[k], p.sibling).start()

    def wait_near(self, k):
        block = self.near.at[k]
        remote(block, block, self.sent.at[k], self.recv.at[k], self.p.sibling).wait_recv()

    def move(self):
        p = self.p
        for k in range(1, p.chips):
            self.wait_near(k)
            mine = self.part[self.at(2 * p.chip_at(k) + p.core), :]
            self.near[k] = (mine.astype(F32) + self.near[k].astype(F32)).astype(BF16)
            remote(self.near.at[k], self.far.at[k - 1], self.sent_far.at[k], self.recv_far.at[k], p.peer(k)).start()

    def finish(self):
        p = self.p
        self.wait_near(0)
        total = self.part[self.at(p.dp), :].astype(F32) + self.near[0].astype(F32)
        for k in range(1, p.chips):
            block = self.far.at[k - 1]
            remote(block, block, self.sent_far.at[k], self.recv_far.at[k], p.sibling).wait_recv()
            total += self.far[k - 1].astype(F32)
        for k in range(p.chips):
            block = self.near.at[0]
            remote(block, block, self.sent.at[k], self.recv.at[0], p.sibling).wait_send()
            if k > 0:
                remote(block, block, self.sent_far.at[k], self.recv.at[0], p.sibling).wait_send()
        return total


def backward(d, args):
    n, t, R, D, HP = d.n, d.t, d.block, d.width, d.hidden_pad
    chips, per_line, share = n // 2, n // t, d.share
    scale_factor = 1.0 / math.sqrt(HD)
    wide = 3 * d.cols

    def kernel(*refs):
        refs = list(refs)
        take = lambda m: [refs.pop(0) for _ in range(m)]
        tok, cot, hidden, grad_second, vec, mixed_rows, bias_part = take(7)
        far = take(10)
        output, input_grad, g_qkv, g_out, g_up, g_down, g_vec = take(7)
        near = take(10)
        qh, kh, vh, mix, probs, first, wqkv, out_t, grads_mlp, p_part = near
        tok_p, cot_p, gh, low, send, got, dq, dk, dv, q_sum, grads = take(11)
        o_part, w_part, f_part, f_inbox, p_inbox, f_sum, acc = take(7)
        o_mid, o_got, v_send, v_got, v_mid, v_line = take(6)
        place = Place(n, t)
        z, dp = place.z, place.dp

        def adder(part):
            near, far = take(2)
            return part, near, far

        up_grad, down_grad = grads_mlp.at[0], grads_mlp.at[1]
        spaces = [adder(part) for part in (up_grad, down_grad, o_part, w_part)]
        sum_up, sum_down, sum_out, sum_qkv = [
            DpAdd(place, part, share, near, far, take(4)) for part, near, far in spaces
        ]
        split = halves(d)
        view = lambda ref, lo, m: ref.at[:, pl.ds(lo, m)]
        f_chains = [LineChain(place, view(f_part, *h), view(f_inbox, *h), take(2)) for h in split]
        p_chains = [LineChain(place, view(p_part, *h), view(p_inbox, *h), take(2)) for h in split]
        exchange = LineExchange(place, o_mid, o_got, take(3))
        x_sent, x_recv, v_sent, v_recv, v_sent_line, v_recv_line, far_sems = take(7)
        load = lambda i: pltpu.make_async_copy(far[i], near[i], far_sems.at[i])
        for i in (7, 9, 8, 4, 0, 1, 2, 3, 6, 5):
            load(i).start()
        place.enter(every=True)
        for ref, src in ((tok_p, tok), (cot_p, cot)):
            ref[: d.rows, :] = src[...]
            if R > d.rows:
                ref[d.rows :, :] = jnp.zeros((R - d.rows, D), BF16)
        acc[...] = jnp.zeros_like(acc)

        def add_row(i, value):
            acc[i : i + 1, :] += jnp.sum(value, axis=0, keepdims=True)

        def norm_two(r):
            normed, inv = normalize(hidden[r, :])
            grad = grad_second[r, :]
            scaled = grad * vec[5:6, :]
            cots = cot_p[r, :].astype(F32)
            mean = jnp.mean(scaled, axis=-1, keepdims=True)
            pull = jnp.mean(scaled * normed, axis=-1, keepdims=True)
            total = cots + inv * (scaled - mean - normed * pull)
            gh[r, :] = total
            low[r, :] = total.astype(BF16)
            add_row(5, grad * normed)
            add_row(6, grad)
            add_row(4, total)
            add_row(7, cots)

        chunks(d, norm_two)
        load(7).wait()
        mixed_grad = dot(low[...], out_t[...], NN).astype(BF16)
        for i in range(t):
            own = mixed_grad[:, i * d.cols : (i + 1) * d.cols]
            send[i] = jnp.concatenate([own[j * d.packed : (j + 1) * d.packed] for j in range(t)], axis=1)
        for k in range(1, t):
            to = place.along(k)
            remote(send.at[to[1]], got.at[z], x_sent.at[k], x_recv.at[z], to).start()
        got[z] = send[z]
        load(9).wait()
        for i in range(t - 1, 0, -1):
            for chain in p_chains:
                chain.launch_right(i)
                chain.launch_left(t - 1 - i)
        load(8).wait()
        sum_up.start()
        sum_down.start()
        third = D // 3
        for i in range(3):
            o_part[i * third : (i + 1) * third, :] = dot(
                low[:, i * third : (i + 1) * third], mixed_rows[...], TN
            ).astype(BF16)
        sum_out.start()
        for i in range(5):
            load(i).wait()

        for ref in (dk, dv, q_sum):
            ref[...] = jnp.zeros_like(ref)

        def attend_rows(r):
            at = pl.ds(pl.multiple_of(r * R, R), R)
            for j in range(d.heads):
                pieces = [got[r, :, i * d.cols + j * HD : i * d.cols + (j + 1) * HD] for i in range(t)]
                dq[j, at, :] = jnp.concatenate(pieces, axis=0)

            def head(j, carry):
                grad = dq[j, at, :]
                full = probs[j, at, :]
                dv[j] += dot(full, grad, TN)
                delta = jnp.sum(grad.astype(F32) * mix[j, at, :].astype(F32), axis=-1, keepdims=True)
                grad_scores = (full.astype(F32) * (dot(grad, vh[j], NT) - delta)).astype(BF16)
                dk[j] += dot(grad_scores, qh[j, at, :], TN)
                query = dot(grad_scores, kh[j], NN) * scale_factor
                q_sum[j, 0:1, :] += jnp.sum(query, axis=0, keepdims=True)
                dq[j, at, :] = query.astype(BF16)
                return carry

            lax.fori_loop(0, d.heads, head, 0)

        attend_rows(z)
        sum_up.move()
        for k in range(1, t):
            slot = place.along(k)[1]
            remote(got.at[slot], got.at[slot], x_sent.at[k], x_recv.at[slot], place.sibling).wait_recv()
            attend_rows(slot)
            if k == 1:
                sum_down.move()
            if k == 2:
                sum_out.move()
        load(6).wait()
        load(5).wait()

        def part_block(i):
            slot = jnp.where(z < t // 2, t - 1 - i, i)
            at = pl.ds(pl.multiple_of(slot * R, R), R)
            values = [dq[j, at, :] for j in range(d.heads)]
            values += [ref[j, at, :].astype(BF16) for ref in (dk, dv) for j in range(d.heads)]
            grads[at, :] = jnp.concatenate(values, axis=1)
            f_part[slot] = dot(grads[at, :], wqkv[...], NT).astype(BF16)
            for chain in f_chains:

                @pl.when(slot > 0)
                def _():
                    chain.launch_right(slot)

                @pl.when(slot < t - 1)
                def _():
                    chain.launch_left(slot)

        for i in range(1, t - 1):
            for chain in p_chains:
                chain.tick_far(i)
        for i in range(t):
            part_block(i)

        def weight_block(i):
            value = first[:, :, i * third : (i + 1) * third].reshape(d.seq, third)
            w_part[i * third : (i + 1) * third, :] = dot(value, grads[...], TN).astype(BF16)

        for i in range(3):
            weight_block(i)
        sum_qkv.start()
        for i in range(1, t - 1):
            for chain in f_chains:
                chain.tick_far(i)
        for (lo, m), chain in zip(split, p_chains):
            chain.finish(f_sum, pl.ds(lo, m))
        if R > d.sent_rows:
            f_sum[d.sent_rows :, :] = jnp.zeros((R - d.sent_rows, D), F32)
        output[...] = (hidden[...] + f_sum[...] + vec[7:8, :]).astype(BF16)
        g_up[...] = sum_up.finish()
        sum_qkv.move()
        g_down[...] = sum_down.finish()
        out_total = sum_out.finish().astype(BF16)
        for i in range(t):
            o_mid[i] = out_total[:, i * d.cols : (i + 1) * d.cols]
        exchange.start()
        for (lo, m), chain in zip(split, f_chains):
            chain.finish(f_sum, pl.ds(lo, m))
        if R > d.sent_rows:
            f_sum[d.sent_rows :, :] = jnp.zeros((R - d.sent_rows, D), F32)

        def norm_one(r):
            normed, inv = normalize(tok_p[r, :].astype(F32))
            grad = f_sum[r, :]
            scaled = grad * vec[0:1, :]
            mean = jnp.mean(scaled, axis=-1, keepdims=True)
            pull = jnp.mean(scaled * normed, axis=-1, keepdims=True)
            input_grad[r, :] = gh[r, :] + inv * (scaled - mean - normed * pull)
            add_row(0, grad * normed)
            add_row(1, grad)

        chunks(d, norm_one)
        v_send[...] = jnp.zeros_like(v_send)
        for i in (0, 1, 4, 5, 6, 7):
            for j in range(n):
                v_send[j, i : i + 1, :share] = acc[i : i + 1, j * share : (j + 1) * share]
        q_row = jnp.concatenate([q_sum[j, 0:1, :] for j in range(d.heads)], axis=1)
        v_row = jnp.concatenate([jnp.sum(dv[j], axis=0, keepdims=True) for j in range(d.heads)], axis=1)
        for j in range(per_line):
            slot = z * per_line + j
            v_send[slot, 2:3, :share] = q_row[:, j * share : (j + 1) * share]
            v_send[slot, 3:4, :share] = v_row[:, j * share : (j + 1) * share]
            v_send[slot, 8:9, : d.up_share] = bias_part[0:1, j * d.up_share : (j + 1) * d.up_share]
        others = [lax.rem(dp + k, n) for k in range(1, n)]
        for k in range(1, n):
            to = others[k - 1]
            remote(v_send.at[to], v_got.at[k], v_sent.at[k], v_recv.at[k], (to, z)).start()
        g_qkv[...] = sum_qkv.finish()
        total = v_send[dp]
        for k in range(1, n):
            remote(v_got.at[k], v_got.at[k], v_sent.at[k], v_recv.at[k], place.sibling).wait()
            total += v_got[k]
        v_mid[...] = total
        for k in range(1, t):
            remote(v_mid, v_line.at[k], v_sent_line.at[k], v_recv_line.at[k], place.along(k)).start()
        exchange.finish()
        g_out[...] = jnp.sum(o_got[...].astype(F32), axis=0)
        for k in range(1, t):
            remote(v_mid, v_line.at[k], v_sent_line.at[k], v_recv_line.at[k], place.sibling).wait()
            total += v_line[k]
        g_vec[...] = total
        for k in range(1, t):
            remote(send.at[0], got.at[0], x_sent.at[k], x_recv.at[0], place.sibling).wait_send()

    outs = [
        shape(R, D),
        shape(R, D, dtype=F32),
        shape(share, wide, dtype=F32),
        shape(share, d.cols, dtype=F32),
        shape(share, HP, dtype=F32),
        shape(share, HP, dtype=F32),
        shape(16, d.vec_lanes, dtype=F32),
    ]
    heads = (d.heads, d.seq, HD)
    scratch = [pltpu.VMEM(a.shape, a.dtype) for a in args[7:]]
    scratch += [
        pltpu.VMEM((R, D), BF16),
        pltpu.VMEM((R, D), BF16),
        pltpu.VMEM((R, D), F32),
        pltpu.VMEM((R, D), BF16),
        pltpu.VMEM((t, d.packed, D), BF16),
        pltpu.VMEM((t, d.packed, D), BF16),
        pltpu.VMEM(heads, BF16),
        pltpu.VMEM(heads, F32),
        pltpu.VMEM(heads, F32),
        pltpu.VMEM((d.heads, 8, HD), F32),
        pltpu.VMEM((d.seq, wide), BF16),
        pltpu.VMEM((D, D), BF16),
        pltpu.VMEM((D, wide), BF16),
        pltpu.VMEM((t, R, D), BF16),
        pltpu.VMEM((t + 1, R, D), BF16),
        pltpu.VMEM((t + 1, R, D), BF16),
        pltpu.VMEM((R, D), F32),
        pltpu.VMEM((16, D), F32),
        pltpu.VMEM((t, share, d.cols), BF16),
        pltpu.VMEM((t, share, d.cols), BF16),
        pltpu.VMEM((n, 16, d.vec_lanes), F32),
        pltpu.VMEM((n, 16, d.vec_lanes), F32),
        pltpu.VMEM((16, d.vec_lanes), F32),
        pltpu.VMEM((t, 16, d.vec_lanes), F32),
    ]
    for width in (HP, HP, D, wide):
        scratch += [pltpu.VMEM((chips, share, width), BF16), pltpu.VMEM((chips - 1, share, width), BF16)]
    scratch += DpAdd.sems(chips) * 4 + LineChain.sems(t) * 4 + LineExchange.sems(t)
    scratch += [DMA((t,)), DMA((t,)), DMA((n,)), DMA((n,)), DMA((t,)), DMA((t,)), DMA((10,))]
    return pl.pallas_call(
        kernel,
        out_shape=outs,
        in_specs=[VM] * 7 + [ANY] * 10,
        out_specs=[VM] * len(outs),
        scratch_shapes=scratch,
        compiler_params=params(1),
        name="backward",
    )(*args)


def finalize(d, args):
    rows, share, cols = d.rows, d.share, d.cols

    def kernel(out_p, grad_p, g_qkv, g_out, g_up, g_down, g_vec, *outs):
        output, input_grad, q, k, v, o, up, down = outs[:8]
        output[...] = out_p[:rows, :]
        input_grad[...] = grad_p[:rows, :]
        for i, ref in enumerate((q, k, v)):
            ref[...] = g_qkv[:, i * cols : (i + 1) * cols]
        o[...] = g_out[...]
        up[...] = g_up[:, : d.hidden]
        down[...] = g_down[:, : d.hidden]
        for i, ref in enumerate(outs[8:]):
            m = ref.shape[0]
            ref[...] = jnp.reshape(g_vec[i : i + 1, :m], (m,))

    f32 = partial(shape, dtype=F32)
    outs = [shape(rows, d.width), f32(rows, d.width)] + [f32(share, cols)] * 3
    outs += [f32(share, cols), f32(share, d.hidden), f32(share, d.hidden)] + [f32(share)] * 8 + [f32(d.up_share)]
    return pl.pallas_call(
        kernel,
        out_shape=outs,
        in_specs=[VM] * len(args),
        out_specs=[VM] * len(outs),
        compiler_params=pltpu.CompilerParams(vmem_limit_bytes=VMEM_BYTES),
        name="finalize",
    )(*args)


def shards(
    sizes,
    tokens,
    key_mask,
    query_weight,
    key_weight,
    value_weight,
    out_weight,
    up_weight,
    down_weight,
    first_gain,
    first_shift,
    query_bias,
    value_bias,
    out_bias,
    second_gain,
    second_shift,
    up_bias,
    down_bias,
    cotangent,
):
    rows, width = tokens.shape[1:]
    share, up_share = first_gain.shape[0], up_bias.shape[0]
    cols, hidden_cols = query_weight.shape[1], up_weight.shape[1]
    d = Dims(sizes, rows, width, share, cols, hidden_cols, up_share)
    small = [first_gain, first_shift, query_bias, value_bias, out_bias, second_gain, second_shift, down_bias]
    vec, hidden, mixed_rows, grad_second, bias_part, *kept = forward(
        d,
        [tokens[0], cotangent[0], key_mask, query_weight, key_weight, value_weight, out_weight.T, up_weight, down_weight.T]
        + small
        + [up_bias],
    )
    parts = backward(d, [tokens[0], cotangent[0], hidden, grad_second, vec, mixed_rows, bias_part, *kept])
    outs = finalize(d, parts)
    vectors = outs[8:]
    return (outs[0][None], outs[1][None], *outs[2:5], outs[5].T, outs[6], outs[7].T, *vectors[:7], vectors[8], vectors[7])


def solution(mesh):
    sizes = (mesh.shape["dp"], mesh.shape["tensor"])
    split = P("dp", "tensor")
    return jax.shard_map(
        partial(shards, sizes),
        mesh=mesh,
        in_specs=(P("dp", "tensor", None), P("dp", None), split, split, split, P("tensor", "dp"), split, P("tensor", "dp"))
        + (P("dp"),) * 9
        + (P("dp", "tensor", None),),
        out_specs=(P("dp", "tensor", None), P("dp", "tensor", None), split, split, split, P("tensor", "dp"), split, P("tensor", "dp"))
        + (P("dp"),) * 9,
        check_vma=False,
    )
```

```python
from functools import partial
import math

import jax
import jax.numpy as jnp
from jax import lax
from jax.experimental import pallas as pl
from jax.experimental.pallas import tpu as pltpu
from jax.sharding import PartitionSpec as P

HD = 72
EPSILON = 1e-06
GELU_COEF = 0.7978845608028654
MASK_FILL = -1e30
MESH = pl.DeviceIdType.MESH
ANY = pl.BlockSpec(memory_space=pl.ANY)
VM = pl.BlockSpec(memory_space=pltpu.VMEM)
DMA = pltpu.SemaphoreType.DMA
VMEM_BYTES = 60 << 20
F32 = jnp.float32
BF16 = jnp.bfloat16


def remote(src, dst, send_sem, recv_sem, device):
    return pltpu.make_async_remote_copy(
        src_ref=src,
        dst_ref=dst,
        send_sem=send_sem,
        recv_sem=recv_sem,
        device_id=device,
        device_id_type=MESH,
    )


class Place:
    def __init__(self, dp_size, line):
        self.dp_size, self.line, self.chips = dp_size, line, dp_size // 2
        self.dp = lax.axis_index("dp")
        self.z = lax.axis_index("tensor")
        self.core = lax.rem(self.dp, 2)
        self.chip = lax.div(self.dp, 2)
        self.sibling = (2 * self.chip + 1 - self.core, self.z)

    def chip_at(self, k):
        return lax.rem(self.chip + k + self.chips, self.chips)

    def peer(self, k):
        return (2 * self.chip_at(k) + self.core, self.z)

    def along(self, k):
        return (self.dp, lax.rem(self.z + k + self.line, self.line))

    def greet(self, every=False):
        barrier = pltpu.get_barrier_semaphore()
        if every:
            devices = [(lax.rem(self.dp + k, self.dp_size), self.z) for k in range(1, self.dp_size)]
        else:
            devices = [self.peer(k) for k in range(1, self.chips)] + [self.sibling]
        devices += [self.along(k) for k in range(1, self.line)]
        for device in devices:
            pl.semaphore_signal(barrier, inc=1, device_id=device, device_id_type=MESH)
        self.partners = len(devices)

    def meet(self):
        pl.semaphore_wait(pltpu.get_barrier_semaphore(), self.partners)


class DpGather:
    @staticmethod
    def sems(chips):
        return [DMA((chips,)), DMA((chips,)), DMA((2 * chips,)), DMA(())]

    def __init__(self, place, src, dst, sems, at=None):
        self.p, self.src, self.dst = place, src, dst
        self.across, self.inside, self.recv, self.local = sems
        self.at = at if at is not None else (lambda slot: dst.at[slot])

    def start(self):
        p = self.p
        mine = self.at(p.dp)
        for k in range(1, p.chips):
            remote(self.src, mine, self.across.at[k], self.recv.at[p.dp], p.peer(k)).start()
        remote(self.src, mine, self.inside.at[0], self.recv.at[p.dp], p.sibling).start()
        pltpu.make_async_copy(self.src, mine, self.local).start()

    def forward(self):
        p = self.p
        for k in range(1, p.chips):
            slot = 2 * p.chip_at(-k) + p.core
            block = self.at(slot)
            remote(block, block, self.across.at[k], self.recv.at[slot], p.sibling).wait_recv()
            remote(block, block, self.inside.at[k], self.recv.at[slot], p.sibling).start()

    def finish(self):
        p = self.p
        mine = self.at(p.dp)
        for k in range(p.chips):
            slot = 2 * p.chip_at(-k) + 1 - p.core
            block = self.at(slot)
            remote(block, block, self.inside.at[k], self.recv.at[slot], p.sibling).wait_recv()
        for k in range(p.chips):
            remote(self.src, mine, self.inside.at[k], self.recv.at[0], p.sibling).wait_send()
            if k > 0:
                remote(self.src, mine, self.across.at[k], self.recv.at[0], p.sibling).wait_send()
        pltpu.make_async_copy(self.src, mine, self.local).wait()


class LineGather:
    @staticmethod
    def sems(line, many=()):
        return [DMA((*many, line)), DMA((*many, line)), DMA((*many, line))]

    def __init__(self, place, dst, sems, rows=None):
        self.p, self.dst = place, dst
        self.right, self.left, self.recv = sems
        self.at = (lambda slot: dst.at[slot]) if rows is None else (lambda slot: dst.at[slot, pl.ds(0, rows)])

    def send_right(self, slot):
        p = self.p
        block = self.at(slot)

        @pl.when(p.z < p.line - 1)
        def _():
            remote(block, block, self.right.at[slot], self.recv.at[slot], (p.dp, p.z + 1)).start()

    def send_left(self, slot):
        p = self.p
        block = self.at(slot)

        @pl.when(p.z > 0)
        def _():
            remote(block, block, self.left.at[slot], self.recv.at[slot], (p.dp, p.z - 1)).start()

    def start(self):
        self.send_right(self.p.z)
        self.send_left(self.p.z)

    def arrive(self, slot):
        block = self.at(slot)
        remote(block, block, self.right.at[slot], self.recv.at[slot], self.p.sibling).wait_recv()

    def relay(self, slot):
        p = self.p

        @pl.when(jnp.logical_and(p.z > slot, slot >= 0))
        def _():
            self.arrive(slot)
            self.send_right(slot)

        @pl.when(jnp.logical_and(p.z < slot, slot < p.line))
        def _():
            self.arrive(slot)
            self.send_left(slot)

    def step(self, s):
        self.relay(self.p.z - s)
        self.relay(self.p.z + s)

    def finish(self):
        p = self.p
        for slot in range(p.line):
            block = self.at(slot)

            @pl.when(jnp.logical_and(p.z >= slot, p.z < p.line - 1))
            def _():
                remote(block, block, self.right.at[slot], self.recv.at[slot], p.sibling).wait_send()

            @pl.when(jnp.logical_and(p.z <= slot, p.z > 0))
            def _():
                remote(block, block, self.left.at[slot], self.recv.at[slot], p.sibling).wait_send()


class DirectGather:
    @staticmethod
    def sems(line, many=()):
        return [DMA((*many, line)), DMA((*many, line))]

    def __init__(self, place, dst, sems):
        self.p, self.dst = place, dst
        self.sent, self.recv = sems

    def start(self):
        p = self.p
        block = self.dst.at[p.z]
        for k in range(1, p.line):
            remote(block, block, self.sent.at[k], self.recv.at[p.z], p.along(k)).start()

    def finish(self):
        p = self.p
        for k in range(1, p.line):
            slot = p.along(k)[1]
            block = self.dst.at[slot]
            remote(block, block, self.sent.at[k], self.recv.at[slot], p.sibling).wait()


class LineExchange:
    @staticmethod
    def sems(line):
        return [DMA((line,)), DMA((line,)), DMA(())]

    def __init__(self, place, src, dst, sems):
        self.p, self.src, self.dst = place, src, dst
        self.sent, self.recv, self.local = sems

    def start(self):
        p = self.p
        for k in range(1, p.line):
            to = p.along(k)
            remote(self.src.at[to[1]], self.dst.at[p.z], self.sent.at[k], self.recv.at[p.z], to).start()
        pltpu.make_async_copy(self.src.at[p.z], self.dst.at[p.z], self.local).start()

    def finish(self):
        p = self.p
        for k in range(1, p.line):
            slot = p.along(k)[1]
            block = self.dst.at[slot]
            remote(block, block, self.sent.at[k], self.recv.at[slot], p.sibling).wait_recv()
        for k in range(1, p.line):
            block = self.src.at[0]
            remote(block, block, self.sent.at[k], self.recv.at[0], p.sibling).wait_send()
        pltpu.make_async_copy(self.src.at[p.z], self.dst.at[p.z], self.local).wait()


def params(collective_id):
    return pltpu.CompilerParams(
        collective_id=collective_id, has_side_effects=True, vmem_limit_bytes=VMEM_BYTES
    )


def shape(*dims, dtype=BF16):
    return jax.ShapeDtypeStruct(dims, dtype)


def pad_to(count, unit):
    return -(-count // unit) * unit


def normalize(x):
    centred = x - jnp.mean(x, axis=-1, keepdims=True)
    inv_std = lax.rsqrt(jnp.mean(centred * centred, axis=-1, keepdims=True) + EPSILON)
    return centred * inv_std, inv_std


def dot(left, right, contract):
    return lax.dot_general(left, right, ((contract[:1], contract[1:]), ((), ())), preferred_element_type=F32)


NN, NT, TN = (1, 0), (1, 1), (0, 0)


class Dims:
    def __init__(self, sizes, rows, width, share, cols, hidden, up_share):
        self.n, self.t = sizes
        self.rows, self.width, self.share, self.cols = rows, width, share, cols
        self.hidden, self.up_share = hidden, up_share
        self.heads = cols // HD
        self.block = pad_to(rows, 16)
        self.sent_rows = rows if rows % 8 == 0 else self.block
        self.seq = self.t * self.block
        self.hidden_pad = pad_to(hidden, 128)
        self.vec_lanes = pad_to(max(up_share, share), 128)
        self.packed = self.block // self.t
        self.folds = 3 if share % 3 == 0 else 1
        self.fold = share // self.folds
        self.chunk = 32 if self.block % 32 == 0 else 16


def both_sides(place, s, work):
    def side(i, carry):
        slot = place.z - s + 2 * s * i

        @pl.when(jnp.logical_and(slot >= 0, slot < place.line))
        def _():
            work(slot)

        return carry

    lax.fori_loop(0, 2, side, 0)


def chunks(d, work):
    def one(i, carry):
        work(pl.ds(pl.multiple_of(i * d.chunk, d.chunk), d.chunk))
        return carry

    lax.fori_loop(0, d.block // d.chunk, one, 0)


def valid_keys(d, count):
    lane = lax.broadcasted_iota(jnp.int32, (1, d.seq), 1)
    zero = jnp.zeros((1, d.seq), jnp.int32)
    blk = sum([(lane >= d.block * i).astype(jnp.int32) for i in range(1, d.t)], zero)
    off = lane - blk * d.block
    inside = jnp.logical_and(off < d.rows, (off + blk * d.rows).astype(F32) < count)
    return jnp.where(inside, 1.0, 0.0)


class LineChain:
    @staticmethod
    def sems(line):
        return [DMA((line,)), DMA((line + 1,))]

    def __init__(self, place, part, inbox, sems):
        self.p, self.part, self.inbox = place, part, inbox
        self.sent, self.recv = sems

    def wait(self, slot):
        block = self.inbox.at[slot]
        remote(block, block, self.sent.at[0], self.recv.at[slot], self.p.sibling).wait_recv()

    def right(self, src, d):
        p = self.p
        remote(src.at[d], self.inbox.at[d], self.sent.at[d], self.recv.at[d], (p.dp, p.z + 1)).start()

    def left(self, src, d):
        p = self.p
        slot = jnp.where(d == p.z - 1, p.line, d)
        remote(src.at[d], self.inbox.at[slot], self.sent.at[d], self.recv.at[slot], (p.dp, p.z - 1)).start()

    def launch_right(self, d):
        @pl.when(self.p.z == 0)
        def _():
            self.right(self.part, d)

    def launch_left(self, d):
        @pl.when(self.p.z == self.p.line - 1)
        def _():
            self.left(self.part, d)

    def relay_right(self, d):
        p = self.p

        @pl.when((p.z > 0) & (p.z < d) & (d < p.line))
        def _():
            self.wait(d)
            self.inbox[d] = (self.inbox[d].astype(F32) + self.part[d].astype(F32)).astype(BF16)
            self.right(self.inbox, d)

    def relay_left(self, d):
        p = self.p

        @pl.when((p.z < p.line - 1) & (p.z > d) & (d >= 0))
        def _():
            self.wait(d)
            self.inbox[d] = (self.inbox[d].astype(F32) + self.part[d].astype(F32)).astype(BF16)
            self.left(self.inbox, d)

    def hop(self, h, d):
        p = self.p

        @pl.when(p.z == h)
        def _():
            self.relay_right(d)

        @pl.when(p.z == p.line - 1 - h)
        def _():
            self.relay_left(d)

    def tick_far(self, i):
        p = self.p
        self.relay_right(p.line - 1 + p.z - i)
        self.relay_left(i - p.line + 1 + p.z)

    def finish(self, out, rows):
        p = self.p
        out[rows, :] = self.part[p.z].astype(F32)

        @pl.when(p.z > 0)
        def _():
            self.wait(p.z)
            out[rows, :] += self.inbox[p.z].astype(F32)

        @pl.when(p.z < p.line - 1)
        def _():
            self.wait(p.line)
            out[rows, :] += self.inbox[p.line].astype(F32)

        for d in range(p.line):

            @pl.when(p.z != d)
            def _():
                block = self.part.at[d]
                remote(block, block, self.sent.at[d], self.recv.at[d], p.sibling).wait_send()


def halves(d):
    cut = pad_to(d.sent_rows // 2, 16)
    return ((0, cut), (cut, d.sent_rows - cut))


def gelu_both(u):
    square = u * u
    tanh_val = jnp.tanh(GELU_COEF * (u + 0.044715 * u * square))
    half = 0.5 * (1.0 + tanh_val)
    slope = half + 0.5 * u * (1.0 - tanh_val * tanh_val) * (GELU_COEF * (1.0 + 3.0 * 0.044715 * square))
    return u * half, slope


def forward(d, args):
    n, t, R, D, HP = d.n, d.t, d.block, d.width, d.hidden_pad
    chips = n // 2
    per_line = n // t
    scale_factor = 1.0 / math.sqrt(HD)
    split = halves(d)

    def kernel(*refs):
        refs = list(refs)
        take = lambda m: [refs.pop(0) for _ in range(m)]
        tok, cot_in, mask, wq, wk, wv, wo, wu, wd = take(9)
        vecs = take(9)
        vec, hidden, mixed_rows, grad_second, bias_part = take(5)
        kept_out = take(10)
        kept = take(10)
        qh, kh, vh, mix, probs, first, wqkv, out_t, grads, o_part = kept
        tokbuf, w_st, o_mid, o_pack, u_st, d_st, v_st, v_all = take(8)
        mixbuf, second, cot, up, down, act, pre_grad, part, inbox, upb, total = take(11)
        place = Place(n, t)
        place.greet()
        z = place.z
        rows_of = lambda ref: (lambda slot: ref.at[pl.ds(pl.multiple_of(slot * d.share, 8), d.share)])
        g_vec = DpGather(place, v_st, v_all, take(4))
        g_qkv = DpGather(place, w_st, wqkv, take(4), rows_of(wqkv))
        g_up = DpGather(place, u_st, up, take(4), rows_of(up))
        g_down = DpGather(place, d_st, down, take(4), rows_of(down))
        g_out = DpGather(place, o_pack, out_t, take(4), rows_of(out_t))
        l_tok = LineGather(place, tokbuf, take(3), d.sent_rows)
        l_out = DirectGather(place, o_mid, take(2))
        l_cot = LineGather(place, cot, take(3), d.sent_rows)
        mix_sems = take(2)
        l_mix = lambda r: DirectGather(place, mixbuf.at[r], [sem.at[r] for sem in mix_sems])
        view = lambda ref, lo, m: ref.at[:, pl.ds(lo, m)]
        chains = [LineChain(place, view(part, *h), view(inbox, *h), take(2)) for h in split]
        (kept_sems,) = take(1)

        def keep(*names):
            for i in names:
                pltpu.make_async_copy(kept[i], kept_out[i], kept_sems.at[i]).start()

        if R > d.rows:
            for i in range(t):
                tokbuf[i, d.rows :, :] = jnp.zeros((R - d.rows, D), BF16)
                cot[i, d.rows :, :] = jnp.zeros((R - d.rows, D), BF16)
        tokbuf[z, : d.rows, :] = tok[...]
        cot[z, : d.rows, :] = cot_in[...]
        for i, w in enumerate((wq, wk, wv)):
            w_st[:, i * d.cols : (i + 1) * d.cols] = w[...]
        v_st[...] = jnp.zeros_like(v_st)
        for i, v in enumerate(vecs):
            m = v.shape[0]
            v_st[i : i + 1, :m] = jnp.reshape(v[...].astype(F32), (1, m))
        o_mid[z] = jnp.concatenate([wo[i * d.fold : (i + 1) * d.fold, :] for i in range(d.folds)], axis=1)
        place.meet()
        l_out.start()
        g_vec.start()
        g_qkv.start()
        l_tok.start()
        at_end = jnp.logical_or(z == 0, z == t - 1)

        @pl.when(at_end)
        def _():
            l_cot.start()

        u_st[...] = jnp.zeros_like(u_st)
        u_st[:, : d.hidden] = wu[...]
        d_st[...] = jnp.zeros_like(d_st)
        d_st[:, : d.hidden] = wd[...]
        bias_part[...] = jnp.zeros_like(bias_part)
        g_vec.forward()
        g_vec.finish()
        for i in range(8):
            vec[i : i + 1, :] = jnp.concatenate([v_all[j, i : i + 1, : d.share] for j in range(n)], axis=1)
        upb[...] = jnp.zeros_like(upb)
        upb[0:1, : d.hidden] = jnp.concatenate(
            [v_all[z * per_line + j, 8:9, : d.up_share] for j in range(per_line)], axis=1
        )
        local = lambda i: jnp.concatenate(
            [v_all[z * per_line + j, i : i + 1, : d.share] for j in range(per_line)], axis=1
        )
        bias_row = jnp.concatenate([local(2), jnp.zeros((1, d.cols), F32), local(3)], axis=1)
        scale_row = jnp.concatenate(
            [jnp.full((1, d.cols), scale_factor, F32), jnp.ones((1, 2 * d.cols), F32)], axis=1
        )
        gain, shift = vec[0:1, :], vec[1:2, :]

        def norm_block(slot):
            def one(r):
                normed = normalize(tokbuf[slot, r, :].astype(F32))[0]
                first[slot, r, :] = (normed * gain + shift).astype(BF16)

            chunks(d, one)

        def project_block(slot):
            y = (dot(first[slot], wqkv[...], NN) + bias_row) * scale_row
            y = y.astype(BF16)
            at = pl.ds(pl.multiple_of(slot * R, R), R)
            for i, ref in enumerate((qh, kh, vh)):
                for j in range(d.heads):
                    start = i * d.cols + j * HD
                    ref[j, at, :] = y[:, start : start + HD]

        norm_block(z)
        l_out.finish()
        for i in range(d.folds):
            o_pack[i * d.fold : (i + 1) * d.fold, :] = jnp.concatenate(
                [o_mid[j, :, i * d.cols : (i + 1) * d.cols] for j in range(t)], axis=1
            )
        g_out.start()
        l_tok.step(1)
        g_qkv.forward()
        g_up.start()
        g_down.start()
        both_sides(place, 1, norm_block)
        g_qkv.finish()
        project_block(z)
        both_sides(place, 1, project_block)

        def norm_and_project(slot):
            norm_block(slot)
            project_block(slot)

        for s in range(2, t):
            l_tok.step(s)

            @pl.when(z == s - 1)
            def _():
                l_cot.relay(0)

            @pl.when(z == t - s)
            def _():
                l_cot.relay(t - 1)

            if s == 2:

                @pl.when(jnp.logical_not(at_end))
                def _():
                    l_cot.start()

            if s == 2:
                g_out.forward()
            both_sides(place, s, norm_and_project)
        g_up.forward()
        keep(0, 1, 2, 5, 6)

        count = jnp.sum(mask[...].astype(F32), axis=1, keepdims=True)
        valid = valid_keys(d, count)


        def order(i):
            pair = lax.div(i, 2)
            return jnp.where(lax.rem(i + pair, 2) == 0, pair, t - 1 - pair)

        def attend_rows(i, carry):
            r = order(i)
            at = pl.ds(pl.multiple_of(r * R, R), R)

            def head(j, carry):
                scores = dot(qh[j, at, :], kh[j], NT)
                scores = jnp.where(valid > 0, scores, MASK_FILL)
                highest = jnp.max(scores, axis=-1, keepdims=True)
                raised = jnp.exp(scores - highest)
                share = 1.0 / jnp.sum(raised, axis=-1, keepdims=True)
                probs[j, at, :] = (raised * share).astype(BF16)
                mix[j, at, :] = dot(probs[j, at, :], vh[j], NN).astype(BF16)
                return carry

            lax.fori_loop(0, d.heads, head, 0)
            own = [mix[j, at, :] for j in range(d.heads)]
            piece = lambda i, j: own[j][i * d.packed : (i + 1) * d.packed]
            mixbuf[r, z] = jnp.concatenate([piece(i, j) for i in range(t) for j in range(d.heads)], axis=1)
            l_mix(r).start()

            return carry

        lax.fori_loop(0, t, attend_rows, 0)
        keep(3, 4)
        g_up.finish()
        g_out.finish()
        keep(7)

        def block(i, carry):
            r = order(i)
            l_mix(r).finish()

            @pl.when(jnp.logical_and(i == 2, jnp.logical_not(at_end)))
            def _():
                for slot in range(1, t - 1):
                    l_cot.relay(slot)

            rows = jnp.concatenate(
                [
                    jnp.concatenate([mixbuf[r, j, :, k * d.cols : (k + 1) * d.cols] for j in range(t)], axis=1)
                    for k in range(t)
                ],
                axis=0,
            )
            total[...] = tokbuf[r].astype(F32) + dot(rows, out_t[...], NT) + vec[4:5, :]

            @pl.when(r == z)
            def _():
                hidden[...] = total[...]
                mixed_rows[...] = rows

            def norm_two(c):
                normed = normalize(total[c, :])[0]
                second[r, c, :] = (normed * vec[5:6, :] + vec[6:7, :]).astype(BF16)

            chunks(d, norm_two)
            pre = dot(second[r], up[...], NN) + upb[0:1, :]
            value, slope = gelu_both(pre)
            act[r] = value.astype(BF16)

            @pl.when(at_end)
            def _():
                l_cot.relay(r)

            @pl.when(i == 0)
            def _():
                g_down.forward()
                g_down.finish()

            grad = dot(cot[r], down[...], NN) * slope
            bias_part[0:1, :] += jnp.sum(grad, axis=0, keepdims=True)
            pre_grad[r] = grad.astype(BF16)
            part[r] = dot(pre_grad[r], up[...], NT).astype(BF16)

            def launch(these):
                for chain in these:

                    @pl.when(r > 0)
                    def _():
                        chain.launch_right(r)

                    @pl.when(r < t - 1)
                    def _():
                        chain.launch_left(r)

            launch(chains)
            o_part[r] = dot(act[r], down[...], NT).astype(BF16)
            for h in range(1, t - 1):

                @pl.when(i >= h)
                def _():
                    for chain in chains:
                        chain.hop(h, order(i - h))

            return carry

        lax.fori_loop(0, t, block, 0)

        width = D // 3

        def weight_grad(k, left, right, i):
            value = left[:, :, i * width : (i + 1) * width].reshape(d.seq, width)
            grads[k, i * width : (i + 1) * width, :] = dot(value, right[...].reshape(d.seq, HP), TN).astype(BF16)

        work = [partial(weight_grad, 0, second, pre_grad, i) for i in range(3)]
        work += [partial(weight_grad, 1, cot, act, i) for i in range(3)]
        for i in range(t, 2 * t - 2):
            work.pop(0)()
            for h in range(i - t + 1, t - 1):
                for chain in chains:
                    chain.hop(h, order(i - h))
        for item in work:
            item()
        keep(8, 9)
        for (lo, m), chain in zip(split, chains):
            chain.finish(grad_second, pl.ds(lo, m))
        if R > d.sent_rows:
            grad_second[d.sent_rows :, :] = jnp.zeros((R - d.sent_rows, D), F32)
        for op in (l_tok, l_cot):
            op.finish()
        for i in range(10):
            pltpu.make_async_copy(kept[i], kept_out[i], kept_sems.at[i]).wait()

    heads = (d.heads, d.seq, HD)
    outs = [
        shape(16, D, dtype=F32),
        shape(R, D, dtype=F32),
        shape(R, D),
        shape(R, D, dtype=F32),
        shape(8, HP, dtype=F32),
    ]
    kept = [
        shape(*heads),
        shape(*heads),
        shape(*heads),
        shape(*heads),
        shape(d.heads, d.seq, d.seq),
        shape(t, R, D),
        shape(D, 3 * d.cols),
        shape(D, D),
        shape(2, D, HP),
        shape(t, R, D),
    ]
    scratch = [pltpu.VMEM(a.shape, a.dtype) for a in kept]
    scratch += [
        pltpu.VMEM((t, R, D), BF16),
        pltpu.VMEM((d.share, 3 * d.cols), BF16),
        pltpu.VMEM((t, d.fold, d.folds * d.cols), BF16),
        pltpu.VMEM((d.share, D), BF16),
        pltpu.VMEM((d.share, HP), BF16),
        pltpu.VMEM((d.share, HP), BF16),
        pltpu.VMEM((16, d.vec_lanes), F32),
        pltpu.VMEM((n, 16, d.vec_lanes), F32),
        pltpu.VMEM((t, t, d.packed, D), BF16),
        pltpu.VMEM((t, R, D), BF16),
        pltpu.VMEM((t, R, D), BF16),
        pltpu.VMEM((D, HP), BF16),
        pltpu.VMEM((D, HP), BF16),
        pltpu.VMEM((t, R, HP), BF16),
        pltpu.VMEM((t, R, HP), BF16),
        pltpu.VMEM((t, R, D), BF16),
        pltpu.VMEM((t + 1, R, D), BF16),
        pltpu.VMEM((8, HP), F32),
        pltpu.VMEM((R, D), F32),
    ]
    for _ in range(5):
        scratch += DpGather.sems(chips)
    scratch += LineGather.sems(t) + DirectGather.sems(t) + LineGather.sems(t) + DirectGather.sems(t, (t,))
    scratch += LineChain.sems(t) * 2 + [DMA((10,))]
    return pl.pallas_call(
        kernel,
        out_shape=outs + kept,
        in_specs=[VM] * len(args),
        out_specs=[VM] * len(outs) + [ANY] * len(kept),
        scratch_shapes=scratch,
        compiler_params=params(0),
        name="forward",
    )(*args)


class DpAdd:
    @staticmethod
    def sems(chips):
        return [DMA((chips,)), DMA((chips,)), DMA((chips,)), DMA((chips,))]

    def __init__(self, place, part, rows, near, far, sems):
        self.p, self.part, self.rows, self.near, self.far = place, part, rows, near, far
        self.sent, self.recv, self.sent_far, self.recv_far = sems

    def at(self, slot):
        return pl.ds(pl.multiple_of(slot * self.rows, 8), self.rows)

    def start(self):
        p = self.p
        for k in [*range(1, p.chips), 0]:
            src = self.part.at[self.at(2 * p.chip_at(k) + 1 - p.core)]
            remote(src, self.near.at[k], self.sent.at[k], self.recv.at[k], p.sibling).start()

    def wait_near(self, k):
        block = self.near.at[k]
        remote(block, block, self.sent.at[k], self.recv.at[k], self.p.sibling).wait_recv()

    def move(self):
        p = self.p
        for k in range(1, p.chips):
            self.wait_near(k)
            mine = self.part[self.at(2 * p.chip_at(k) + p.core), :]
            self.near[k] = (mine.astype(F32) + self.near[k].astype(F32)).astype(BF16)
            remote(self.near.at[k], self.far.at[k - 1], self.sent_far.at[k], self.recv_far.at[k], p.peer(k)).start()

    def finish(self):
        p = self.p
        self.wait_near(0)
        total = self.part[self.at(p.dp), :].astype(F32) + self.near[0].astype(F32)
        for k in range(1, p.chips):
            block = self.far.at[k - 1]
            remote(block, block, self.sent_far.at[k], self.recv_far.at[k], p.sibling).wait_recv()
            total += self.far[k - 1].astype(F32)
        for k in range(p.chips):
            block = self.near.at[0]
            remote(block, block, self.sent.at[k], self.recv.at[0], p.sibling).wait_send()
            if k > 0:
                remote(block, block, self.sent_far.at[k], self.recv.at[0], p.sibling).wait_send()
        return total


def backward(d, args):
    n, t, R, D, HP = d.n, d.t, d.block, d.width, d.hidden_pad
    chips, per_line, share = n // 2, n // t, d.share
    scale_factor = 1.0 / math.sqrt(HD)
    wide = 3 * d.cols

    def kernel(*refs):
        refs = list(refs)
        take = lambda m: [refs.pop(0) for _ in range(m)]
        tok, cot, hidden, grad_second, vec, mixed_rows, bias_part = take(7)
        far = take(10)
        output, input_grad, g_q, g_k, g_v, g_out, g_up, g_down, g_vec = take(9)
        near = take(10)
        qh, kh, vh, mix, probs, first, wqkv, out_t, grads_mlp, p_part = near
        tok_p, cot_p, gh, low, send, got, dq, dk, dv, q_sum, grads = take(11)
        o_part, w_part, f_part, f_inbox, p_inbox, f_sum, acc = take(7)
        o_mid, o_got, v_send, v_got, v_mid, v_line = take(6)
        place = Place(n, t)
        place.greet(every=True)
        z, dp = place.z, place.dp

        def adder(part):
            near, far = take(2)
            return part, near, far

        up_grad, down_grad = grads_mlp.at[0], grads_mlp.at[1]
        spaces = [adder(part) for part in (up_grad, down_grad, o_part, w_part)]
        sum_up, sum_down, sum_out, sum_qkv = [
            DpAdd(place, part, share, near, far, take(4)) for part, near, far in spaces
        ]
        split = halves(d)
        view = lambda ref, lo, m: ref.at[:, pl.ds(lo, m)]
        f_chains = [LineChain(place, view(f_part, *h), view(f_inbox, *h), take(2)) for h in split]
        p_chains = [LineChain(place, view(p_part, *h), view(p_inbox, *h), take(2)) for h in split]
        exchange = LineExchange(place, o_mid, o_got, take(3))
        x_sent, x_recv, v_sent, v_recv, v_sent_line, v_recv_line, far_sems = take(7)
        load = lambda i: pltpu.make_async_copy(far[i], near[i], far_sems.at[i])
        for i in (9, 8, 7, 4, 0, 1, 2, 3, 6, 5):
            load(i).start()
        place.meet()
        load(9).wait()
        for chain in p_chains:
            chain.launch_right(t - 1)
            chain.launch_left(0)
        load(8).wait()
        sum_up.start()
        sum_down.start()
        for ref, src in ((tok_p, tok), (cot_p, cot)):
            ref[: d.rows, :] = src[...]
            if R > d.rows:
                ref[d.rows :, :] = jnp.zeros((R - d.rows, D), BF16)
        acc[...] = jnp.zeros_like(acc)

        def add_row(i, value):
            acc[i : i + 1, :] += jnp.sum(value, axis=0, keepdims=True)

        def norm_two(r):
            normed, inv = normalize(hidden[r, :])
            grad = grad_second[r, :]
            scaled = grad * vec[5:6, :]
            cots = cot_p[r, :].astype(F32)
            mean = jnp.mean(scaled, axis=-1, keepdims=True)
            pull = jnp.mean(scaled * normed, axis=-1, keepdims=True)
            total = cots + inv * (scaled - mean - normed * pull)
            gh[r, :] = total
            low[r, :] = total.astype(BF16)
            add_row(5, grad * normed)
            add_row(6, grad)
            add_row(4, total)
            add_row(7, cots)

        chunks(d, norm_two)
        load(7).wait()
        mixed_grad = dot(low[...], out_t[...], NN).astype(BF16)
        for i in range(t):
            own = mixed_grad[:, i * d.cols : (i + 1) * d.cols]
            send[i] = jnp.concatenate([own[j * d.packed : (j + 1) * d.packed] for j in range(t)], axis=1)
        for k in range(1, t):
            to = place.along(k)
            remote(send.at[to[1]], got.at[z], x_sent.at[k], x_recv.at[z], to).start()
        got[z] = send[z]
        for i in range(t - 2, 1, -1):
            for chain in p_chains:
                chain.launch_right(i)
                chain.launch_left(t - 1 - i)
        p_chains[0].launch_right(1)
        p_chains[0].launch_left(t - 2)
        sum_up.move()
        third = D // 3
        for i in range(3):
            o_part[i * third : (i + 1) * third, :] = dot(
                low[:, i * third : (i + 1) * third], mixed_rows[...], TN
            ).astype(BF16)
        sum_out.start()
        for i in range(5):
            load(i).wait()

        for ref in (dk, dv, q_sum):
            ref[...] = jnp.zeros_like(ref)

        def attend_rows(r):
            at = pl.ds(pl.multiple_of(r * R, R), R)
            for j in range(d.heads):
                pieces = [got[r, :, i * d.cols + j * HD : i * d.cols + (j + 1) * HD] for i in range(t)]
                dq[j, at, :] = jnp.concatenate(pieces, axis=0)

            def head(j, carry):
                grad = dq[j, at, :]
                full = probs[j, at, :]
                dv[j] += dot(full, grad, TN)
                delta = jnp.sum(grad.astype(F32) * mix[j, at, :].astype(F32), axis=-1, keepdims=True)
                grad_scores = (full.astype(F32) * (dot(grad, vh[j], NT) - delta)).astype(BF16)
                dk[j] += dot(grad_scores, qh[j, at, :], TN)
                query = dot(grad_scores, kh[j], NN) * scale_factor
                q_sum[j, 0:1, :] += jnp.sum(query, axis=0, keepdims=True)
                dq[j, at, :] = query.astype(BF16)
                return carry

            lax.fori_loop(0, d.heads, head, 0)

        attend_rows(z)
        sum_down.move()
        for k in range(1, t):
            slot = place.along(k)[1]
            remote(got.at[slot], got.at[slot], x_sent.at[k], x_recv.at[slot], place.sibling).wait_recv()
            attend_rows(slot)
            if k == 1:
                sum_out.move()
                for chain in p_chains:
                    chain.tick_far(1)
        load(6).wait()
        load(5).wait()

        def part_block(i):
            slot = jnp.where(z < t // 2, t - 1 - i, i)
            at = pl.ds(pl.multiple_of(slot * R, R), R)
            values = [dq[j, at, :] for j in range(d.heads)]
            values += [ref[j, at, :].astype(BF16) for ref in (dk, dv) for j in range(d.heads)]
            grads[at, :] = jnp.concatenate(values, axis=1)
            f_part[slot] = dot(grads[at, :], wqkv[...], NT).astype(BF16)
            for chain in f_chains:

                @pl.when(slot > 0)
                def _():
                    chain.launch_right(slot)

                @pl.when(slot < t - 1)
                def _():
                    chain.launch_left(slot)

        for i in range(t):
            part_block(i)
        for chain in p_chains[1:]:
            chain.launch_right(1)
            chain.launch_left(t - 2)
        for i in range(2, t - 1):
            for chain in p_chains:
                chain.tick_far(i)

        def weight_block(i):
            value = first[:, :, i * third : (i + 1) * third].reshape(d.seq, third)
            w_part[i * third : (i + 1) * third, :] = dot(value, grads[...], TN).astype(BF16)

        for i in range(3):
            weight_block(i)
        sum_qkv.start()
        g_up[...] = sum_up.finish()[:, : d.hidden]
        for chain in f_chains:
            chain.tick_far(1)
        sum_qkv.move()
        g_down[...] = sum_down.finish()[:, : d.hidden]
        for i in range(2, t - 1):
            for chain in f_chains:
                chain.tick_far(i)
        out_total = sum_out.finish().astype(BF16)
        for i in range(t):
            o_mid[i] = jnp.concatenate(
                [out_total[j * d.fold : (j + 1) * d.fold, i * d.cols : (i + 1) * d.cols] for j in range(d.folds)], axis=1
            )
        exchange.start()
        v_send[...] = jnp.zeros_like(v_send)
        q_row = jnp.concatenate([q_sum[j, 0:1, :] for j in range(d.heads)], axis=1)
        v_row = jnp.concatenate([jnp.sum(dv[j], axis=0, keepdims=True) for j in range(d.heads)], axis=1)
        for j in range(per_line):
            slot = z * per_line + j
            v_send[slot, 2:3, :share] = q_row[:, j * share : (j + 1) * share]
            v_send[slot, 3:4, :share] = v_row[:, j * share : (j + 1) * share]
            v_send[slot, 8:9, : d.up_share] = bias_part[0:1, j * d.up_share : (j + 1) * d.up_share]
        for (lo, m), chain in zip(split, f_chains):
            chain.finish(f_sum, pl.ds(lo, m))
        if R > d.sent_rows:
            f_sum[d.sent_rows :, :] = jnp.zeros((R - d.sent_rows, D), F32)

        def norm_one_sums(r):
            normed = normalize(tok_p[r, :].astype(F32))[0]
            grad = f_sum[r, :]
            add_row(0, grad * normed)
            add_row(1, grad)

        def norm_one(r):
            normed, inv = normalize(tok_p[r, :].astype(F32))
            scaled = f_sum[r, :] * vec[0:1, :]
            mean = jnp.mean(scaled, axis=-1, keepdims=True)
            pull = jnp.mean(scaled * normed, axis=-1, keepdims=True)
            input_grad[r, :] = gh[r, :] + inv * (scaled - mean - normed * pull)

        chunks(d, norm_one_sums)
        for i in (0, 1, 4, 5, 6, 7):
            for j in range(n):
                v_send[j, i : i + 1, :share] = acc[i : i + 1, j * share : (j + 1) * share]
        others = [lax.rem(dp + k, n) for k in range(1, n)]
        for k in range(1, n):
            to = others[k - 1]
            remote(v_send.at[to], v_got.at[k], v_sent.at[k], v_recv.at[k], (to, z)).start()
        chunks(d, norm_one)
        total = v_send[dp]
        for k in range(1, n):
            remote(v_got.at[k], v_got.at[k], v_sent.at[k], v_recv.at[k], place.sibling).wait()
            total += v_got[k]
        v_mid[...] = total
        for k in range(1, t):
            remote(v_mid, v_line.at[k], v_sent_line.at[k], v_recv_line.at[k], place.along(k)).start()
        qkv_total = sum_qkv.finish()
        for i, ref in enumerate((g_q, g_k, g_v)):
            ref[...] = qkv_total[:, i * d.cols : (i + 1) * d.cols]
        exchange.finish()
        out_sum = jnp.sum(o_got[...].astype(F32), axis=0)
        for i in range(d.folds):
            g_out[i * d.fold : (i + 1) * d.fold, :] = out_sum[:, i * d.cols : (i + 1) * d.cols]
        for (lo, m), chain in zip(split, p_chains):
            chain.finish(f_sum, pl.ds(lo, m))
        if R > d.sent_rows:
            f_sum[d.sent_rows :, :] = jnp.zeros((R - d.sent_rows, D), F32)
        output[...] = (hidden[...] + f_sum[...] + vec[7:8, :]).astype(BF16)
        for k in range(1, t):
            remote(v_mid, v_line.at[k], v_sent_line.at[k], v_recv_line.at[k], place.sibling).wait()
            total += v_line[k]
        g_vec[...] = total
        for k in range(1, t):
            remote(send.at[0], got.at[0], x_sent.at[k], x_recv.at[0], place.sibling).wait_send()

    outs = [
        shape(R, D),
        shape(R, D, dtype=F32),
        shape(share, d.cols, dtype=F32),
        shape(share, d.cols, dtype=F32),
        shape(share, d.cols, dtype=F32),
        shape(share, d.cols, dtype=F32),
        shape(share, d.hidden, dtype=F32),
        shape(share, d.hidden, dtype=F32),
        shape(16, d.vec_lanes, dtype=F32),
    ]
    heads = (d.heads, d.seq, HD)
    scratch = [pltpu.VMEM(a.shape, a.dtype) for a in args[7:]]
    scratch += [
        pltpu.VMEM((R, D), BF16),
        pltpu.VMEM((R, D), BF16),
        pltpu.VMEM((R, D), F32),
        pltpu.VMEM((R, D), BF16),
        pltpu.VMEM((t, d.packed, D), BF16),
        pltpu.VMEM((t, d.packed, D), BF16),
        pltpu.VMEM(heads, BF16),
        pltpu.VMEM(heads, F32),
        pltpu.VMEM(heads, F32),
        pltpu.VMEM((d.heads, 8, HD), F32),
        pltpu.VMEM((d.seq, wide), BF16),
        pltpu.VMEM((D, D), BF16),
        pltpu.VMEM((D, wide), BF16),
        pltpu.VMEM((t, R, D), BF16),
        pltpu.VMEM((t + 1, R, D), BF16),
        pltpu.VMEM((t + 1, R, D), BF16),
        pltpu.VMEM((R, D), F32),
        pltpu.VMEM((16, D), F32),
        pltpu.VMEM((t, d.fold, d.folds * d.cols), BF16),
        pltpu.VMEM((t, d.fold, d.folds * d.cols), BF16),
        pltpu.VMEM((n, 16, d.vec_lanes), F32),
        pltpu.VMEM((n, 16, d.vec_lanes), F32),
        pltpu.VMEM((16, d.vec_lanes), F32),
        pltpu.VMEM((t, 16, d.vec_lanes), F32),
    ]
    for width in (HP, HP, D, wide):
        scratch += [pltpu.VMEM((chips, share, width), BF16), pltpu.VMEM((chips - 1, share, width), BF16)]
    scratch += DpAdd.sems(chips) * 4 + LineChain.sems(t) * 4 + LineExchange.sems(t)
    scratch += [DMA((t,)), DMA((t,)), DMA((n,)), DMA((n,)), DMA((t,)), DMA((t,)), DMA((10,))]
    return pl.pallas_call(
        kernel,
        out_shape=outs,
        in_specs=[VM] * 7 + [ANY] * 10,
        out_specs=[VM] * len(outs),
        scratch_shapes=scratch,
        compiler_params=params(1),
        name="backward",
    )(*args)


def finalize(d, args):
    names = len(args) - 1
    f32 = partial(shape, dtype=F32)
    outs = [shape(d.rows, d.width), f32(d.rows, d.width)] + [f32(*a.shape) for a in args[2:-1]]
    vectors = [f32(d.share)] * 8 + [f32(d.up_share)]

    def kernel(*refs):
        ins, g_vec, results = refs[:names], refs[names], refs[names + 1 :]
        for src, dst in zip(ins, results):
            dst[...] = src[: dst.shape[0], :]
        for i, ref in enumerate(results[names:]):
            m = ref.shape[0]
            ref[...] = jnp.reshape(g_vec[i : i + 1, :m], (m,))

    return pl.pallas_call(
        kernel,
        out_shape=outs + vectors,
        in_specs=[VM] * len(args),
        out_specs=[VM] * (names + 9),
        compiler_params=pltpu.CompilerParams(vmem_limit_bytes=VMEM_BYTES),
        name="finalize",
    )(*args)


def shards(
    sizes,
    tokens,
    key_mask,
    query_weight,
    key_weight,
    value_weight,
    out_weight,
    up_weight,
    down_weight,
    first_gain,
    first_shift,
    query_bias,
    value_bias,
    out_bias,
    second_gain,
    second_shift,
    up_bias,
    down_bias,
    cotangent,
):
    rows, width = tokens.shape[1:]
    share, up_share = first_gain.shape[0], up_bias.shape[0]
    cols, hidden_cols = query_weight.shape[1], up_weight.shape[1]
    d = Dims(sizes, rows, width, share, cols, hidden_cols, up_share)
    small = [first_gain, first_shift, query_bias, value_bias, out_bias, second_gain, second_shift, down_bias]
    vec, hidden, mixed_rows, grad_second, bias_part, *kept = forward(
        d,
        [tokens[0], cotangent[0], key_mask, query_weight, key_weight, value_weight, out_weight.T, up_weight, down_weight.T]
        + small
        + [up_bias],
    )
    parts = backward(d, [tokens[0], cotangent[0], hidden, grad_second, vec, mixed_rows, bias_part, *kept])
    outs = finalize(d, parts)
    vectors = outs[8:]
    return (outs[0][None], outs[1][None], *outs[2:5], outs[5].T, outs[6], outs[7].T, *vectors[:7], vectors[8], vectors[7])


def solution(mesh):
    sizes = (mesh.shape["dp"], mesh.shape["tensor"])
    split = P("dp", "tensor")
    return jax.shard_map(
        partial(shards, sizes),
        mesh=mesh,
        in_specs=(P("dp", "tensor", None), P("dp", None), split, split, split, P("tensor", "dp"), split, P("tensor", "dp"))
        + (P("dp"),) * 9
        + (P("dp", "tensor", None),),
        out_specs=(P("dp", "tensor", None), P("dp", "tensor", None), split, split, split, P("tensor", "dp"), split, P("tensor", "dp"))
        + (P("dp"),) * 9,
        check_vma=False,
    )
```

```python
from functools import partial
import math

import jax
import jax.numpy as jnp
from jax import lax
from jax.experimental import pallas as pl
from jax.experimental.pallas import tpu as pltpu
from jax.sharding import PartitionSpec as P

HD = 72
EPSILON = 1e-06
GELU_COEF = 0.7978845608028654
MASK_FILL = -1e30
MESH = pl.DeviceIdType.MESH
ANY = pl.BlockSpec(memory_space=pl.ANY)
VM = pl.BlockSpec(memory_space=pltpu.VMEM)
DMA = pltpu.SemaphoreType.DMA
VMEM_BYTES = 60 << 20
F32 = jnp.float32
BF16 = jnp.bfloat16


def remote(src, dst, send_sem, recv_sem, device):
    return pltpu.make_async_remote_copy(
        src_ref=src,
        dst_ref=dst,
        send_sem=send_sem,
        recv_sem=recv_sem,
        device_id=device,
        device_id_type=MESH,
    )


class Place:
    def __init__(self, dp_size, line):
        self.dp_size, self.line, self.chips = dp_size, line, dp_size // 2
        self.dp = lax.axis_index("dp")
        self.z = lax.axis_index("tensor")
        self.core = lax.rem(self.dp, 2)
        self.chip = lax.div(self.dp, 2)
        self.sibling = (2 * self.chip + 1 - self.core, self.z)

    def chip_at(self, k):
        return lax.rem(self.chip + k + self.chips, self.chips)

    def peer(self, k):
        return (2 * self.chip_at(k) + self.core, self.z)

    def along(self, k):
        return (self.dp, lax.rem(self.z + k + self.line, self.line))

    def greet(self, every=False):
        barrier = pltpu.get_barrier_semaphore()
        if every:
            devices = [(lax.rem(self.dp + k, self.dp_size), self.z) for k in range(1, self.dp_size)]
        else:
            devices = [self.peer(k) for k in range(1, self.chips)] + [self.sibling]
        devices += [self.along(k) for k in range(1, self.line)]
        for device in devices:
            pl.semaphore_signal(barrier, inc=1, device_id=device, device_id_type=MESH)
        self.partners = len(devices)

    def meet(self):
        pl.semaphore_wait(pltpu.get_barrier_semaphore(), self.partners)


class DpGather:
    @staticmethod
    def sems(chips):
        return [DMA((chips,)), DMA((chips,)), DMA((2 * chips,)), DMA(())]

    def __init__(self, place, src, dst, sems, at=None):
        self.p, self.src, self.dst = place, src, dst
        self.across, self.inside, self.recv, self.local = sems
        self.at = at if at is not None else (lambda slot: dst.at[slot])

    def start(self):
        p = self.p
        mine = self.at(p.dp)
        for k in range(1, p.chips):
            remote(self.src, mine, self.across.at[k], self.recv.at[p.dp], p.peer(k)).start()
        remote(self.src, mine, self.inside.at[0], self.recv.at[p.dp], p.sibling).start()
        pltpu.make_async_copy(self.src, mine, self.local).start()

    def forward(self):
        p = self.p
        for k in range(1, p.chips):
            slot = 2 * p.chip_at(-k) + p.core
            block = self.at(slot)
            remote(block, block, self.across.at[k], self.recv.at[slot], p.sibling).wait_recv()
            remote(block, block, self.inside.at[k], self.recv.at[slot], p.sibling).start()

    def finish(self):
        p = self.p
        mine = self.at(p.dp)
        for k in range(p.chips):
            slot = 2 * p.chip_at(-k) + 1 - p.core
            block = self.at(slot)
            remote(block, block, self.inside.at[k], self.recv.at[slot], p.sibling).wait_recv()
        for k in range(p.chips):
            remote(self.src, mine, self.inside.at[k], self.recv.at[0], p.sibling).wait_send()
            if k > 0:
                remote(self.src, mine, self.across.at[k], self.recv.at[0], p.sibling).wait_send()
        pltpu.make_async_copy(self.src, mine, self.local).wait()


class LineGather:
    @staticmethod
    def sems(line, many=()):
        return [DMA((*many, line)), DMA((*many, line)), DMA((*many, line))]

    def __init__(self, place, dst, sems, rows=None):
        self.p, self.dst = place, dst
        self.right, self.left, self.recv = sems
        self.at = (lambda slot: dst.at[slot]) if rows is None else (lambda slot: dst.at[slot, pl.ds(0, rows)])

    def send_right(self, slot):
        p = self.p
        block = self.at(slot)

        @pl.when(p.z < p.line - 1)
        def _():
            remote(block, block, self.right.at[slot], self.recv.at[slot], (p.dp, p.z + 1)).start()

    def send_left(self, slot):
        p = self.p
        block = self.at(slot)

        @pl.when(p.z > 0)
        def _():
            remote(block, block, self.left.at[slot], self.recv.at[slot], (p.dp, p.z - 1)).start()

    def start(self):
        self.send_right(self.p.z)
        self.send_left(self.p.z)

    def arrive(self, slot):
        block = self.at(slot)
        remote(block, block, self.right.at[slot], self.recv.at[slot], self.p.sibling).wait_recv()

    def relay(self, slot):
        p = self.p

        @pl.when(jnp.logical_and(p.z > slot, slot >= 0))
        def _():
            self.arrive(slot)
            self.send_right(slot)

        @pl.when(jnp.logical_and(p.z < slot, slot < p.line))
        def _():
            self.arrive(slot)
            self.send_left(slot)

    def step(self, s):
        self.relay(self.p.z - s)
        self.relay(self.p.z + s)

    def finish(self):
        p = self.p
        for slot in range(p.line):
            block = self.at(slot)

            @pl.when(jnp.logical_and(p.z >= slot, p.z < p.line - 1))
            def _():
                remote(block, block, self.right.at[slot], self.recv.at[slot], p.sibling).wait_send()

            @pl.when(jnp.logical_and(p.z <= slot, p.z > 0))
            def _():
                remote(block, block, self.left.at[slot], self.recv.at[slot], p.sibling).wait_send()


class DirectGather:
    @staticmethod
    def sems(line, many=()):
        return [DMA((*many, line)), DMA((*many, line))]

    def __init__(self, place, dst, sems):
        self.p, self.dst = place, dst
        self.sent, self.recv = sems

    def start(self):
        p = self.p
        block = self.dst.at[p.z]
        for k in range(1, p.line):
            step = jnp.where(p.z < p.line // 2, p.line - k, k)
            remote(block, block, self.sent.at[k], self.recv.at[p.z], p.along(step)).start()

    def finish(self):
        p = self.p
        for k in range(1, p.line):
            slot = p.along(k)[1]
            block = self.dst.at[slot]
            remote(block, block, self.sent.at[k], self.recv.at[slot], p.sibling).wait()


class LineExchange:
    @staticmethod
    def sems(line):
        return [DMA((line,)), DMA((line,)), DMA(())]

    def __init__(self, place, src, dst, sems):
        self.p, self.src, self.dst = place, src, dst
        self.sent, self.recv, self.local = sems

    def start(self):
        p = self.p
        for k in range(1, p.line):
            to = p.along(k)
            remote(self.src.at[to[1]], self.dst.at[p.z], self.sent.at[k], self.recv.at[p.z], to).start()
        pltpu.make_async_copy(self.src.at[p.z], self.dst.at[p.z], self.local).start()

    def finish(self):
        p = self.p
        for k in range(1, p.line):
            slot = p.along(k)[1]
            block = self.dst.at[slot]
            remote(block, block, self.sent.at[k], self.recv.at[slot], p.sibling).wait_recv()
        for k in range(1, p.line):
            block = self.src.at[0]
            remote(block, block, self.sent.at[k], self.recv.at[0], p.sibling).wait_send()
        pltpu.make_async_copy(self.src.at[p.z], self.dst.at[p.z], self.local).wait()


def params(collective_id):
    return pltpu.CompilerParams(
        collective_id=collective_id, has_side_effects=True, vmem_limit_bytes=VMEM_BYTES
    )


def shape(*dims, dtype=BF16):
    return jax.ShapeDtypeStruct(dims, dtype)


def pad_to(count, unit):
    return -(-count // unit) * unit


def normalize(x):
    centred = x - jnp.mean(x, axis=-1, keepdims=True)
    inv_std = lax.rsqrt(jnp.mean(centred * centred, axis=-1, keepdims=True) + EPSILON)
    return centred * inv_std, inv_std


def dot(left, right, contract):
    return lax.dot_general(left, right, ((contract[:1], contract[1:]), ((), ())), preferred_element_type=F32)


NN, NT, TN = (1, 0), (1, 1), (0, 0)


class Dims:
    def __init__(self, sizes, rows, width, share, cols, hidden, up_share):
        self.n, self.t = sizes
        self.rows, self.width, self.share, self.cols = rows, width, share, cols
        self.hidden, self.up_share = hidden, up_share
        self.heads = cols // HD
        self.block = pad_to(rows, 16)
        self.sent_rows = rows if rows % 8 == 0 else self.block
        self.seq = self.t * self.block
        self.hidden_pad = pad_to(hidden, 128)
        self.vec_lanes = pad_to(max(up_share, share), 128)
        self.packed = self.block // self.t
        self.folds = 3 if share % 3 == 0 else 1
        self.fold = share // self.folds
        self.chunk = 32 if self.block % 32 == 0 else 16


def both_sides(place, s, work):
    def side(i, carry):
        slot = place.z - s + 2 * s * i

        @pl.when(jnp.logical_and(slot >= 0, slot < place.line))
        def _():
            work(slot)

        return carry

    lax.fori_loop(0, 2, side, 0)


def chunks(d, work):
    def one(i, carry):
        work(pl.ds(pl.multiple_of(i * d.chunk, d.chunk), d.chunk))
        return carry

    lax.fori_loop(0, d.block // d.chunk, one, 0)


def valid_keys(d, count):
    lane = lax.broadcasted_iota(jnp.int32, (1, d.seq), 1)
    zero = jnp.zeros((1, d.seq), jnp.int32)
    blk = sum([(lane >= d.block * i).astype(jnp.int32) for i in range(1, d.t)], zero)
    off = lane - blk * d.block
    inside = jnp.logical_and(off < d.rows, (off + blk * d.rows).astype(F32) < count)
    return jnp.where(inside, 1.0, 0.0)


class LineChain:
    @staticmethod
    def sems(line):
        return [DMA((line,)), DMA((line + 1,))]

    def __init__(self, place, part, inbox, sems):
        self.p, self.part, self.inbox = place, part, inbox
        self.sent, self.recv = sems

    def wait(self, slot):
        block = self.inbox.at[slot]
        remote(block, block, self.sent.at[0], self.recv.at[slot], self.p.sibling).wait_recv()

    def right(self, src, d):
        p = self.p
        remote(src.at[d], self.inbox.at[d], self.sent.at[d], self.recv.at[d], (p.dp, p.z + 1)).start()

    def left(self, src, d):
        p = self.p
        slot = jnp.where(d == p.z - 1, p.line, d)
        remote(src.at[d], self.inbox.at[slot], self.sent.at[d], self.recv.at[slot], (p.dp, p.z - 1)).start()

    def launch_right(self, d):
        @pl.when(self.p.z == 0)
        def _():
            self.right(self.part, d)

    def launch_left(self, d):
        @pl.when(self.p.z == self.p.line - 1)
        def _():
            self.left(self.part, d)

    def relay_right(self, d):
        p = self.p

        @pl.when((p.z > 0) & (p.z < d) & (d < p.line))
        def _():
            self.wait(d)
            self.inbox[d] = (self.inbox[d].astype(F32) + self.part[d].astype(F32)).astype(BF16)
            self.right(self.inbox, d)

    def relay_left(self, d):
        p = self.p

        @pl.when((p.z < p.line - 1) & (p.z > d) & (d >= 0))
        def _():
            self.wait(d)
            self.inbox[d] = (self.inbox[d].astype(F32) + self.part[d].astype(F32)).astype(BF16)
            self.left(self.inbox, d)

    def hop(self, h, d):
        p = self.p

        @pl.when(p.z == h)
        def _():
            self.relay_right(d)

        @pl.when(p.z == p.line - 1 - h)
        def _():
            self.relay_left(d)

    def tick_far(self, i):
        p = self.p
        self.relay_right(p.line - 1 + p.z - i)
        self.relay_left(i - p.line + 1 + p.z)

    def finish(self, out, rows):
        p = self.p
        out[rows, :] = self.part[p.z].astype(F32)

        @pl.when(p.z > 0)
        def _():
            self.wait(p.z)
            out[rows, :] += self.inbox[p.z].astype(F32)

        @pl.when(p.z < p.line - 1)
        def _():
            self.wait(p.line)
            out[rows, :] += self.inbox[p.line].astype(F32)

        for d in range(p.line):

            @pl.when(p.z != d)
            def _():
                block = self.part.at[d]
                remote(block, block, self.sent.at[d], self.recv.at[d], p.sibling).wait_send()


def halves(d):
    cut = pad_to(d.sent_rows // 2, 16)
    return ((0, cut), (cut, d.sent_rows - cut))


def gelu_both(u):
    square = u * u
    tanh_val = jnp.tanh(GELU_COEF * (u + 0.044715 * u * square))
    half = 0.5 * (1.0 + tanh_val)
    slope = half + 0.5 * u * (1.0 - tanh_val * tanh_val) * (GELU_COEF * (1.0 + 3.0 * 0.044715 * square))
    return u * half, slope


def forward(d, args):
    n, t, R, D, HP = d.n, d.t, d.block, d.width, d.hidden_pad
    chips = n // 2
    per_line = n // t
    scale_factor = 1.0 / math.sqrt(HD)
    split = halves(d)

    def kernel(*refs):
        refs = list(refs)
        take = lambda m: [refs.pop(0) for _ in range(m)]
        tok, cot_in, mask, wq, wk, wv, wo, wu, wd = take(9)
        vecs = take(9)
        (grad_second,) = take(1)
        kept_out = take(14)
        kept = take(14)
        qh, kh, vh, mix, probs, first, wqkv, out_t, grads, o_part, vec, hidden, mixed_rows, bias_part = kept
        tokbuf, w_st, o_mid, o_pack, u_st, d_st, v_st, v_all = take(8)
        mixbuf, second, cot, up, down, act, pre_grad, part, inbox, upb, total, grad_act = take(12)
        place = Place(n, t)
        place.greet()
        z = place.z
        rows_of = lambda ref: (lambda slot: ref.at[pl.ds(pl.multiple_of(slot * d.share, 8), d.share)])
        g_vec = DpGather(place, v_st, v_all, take(4))
        g_qkv = DpGather(place, w_st, wqkv, take(4), rows_of(wqkv))
        g_up = DpGather(place, u_st, up, take(4), rows_of(up))
        g_down = DpGather(place, d_st, down, take(4), rows_of(down))
        g_out = DpGather(place, o_pack, out_t, take(4), rows_of(out_t))
        l_tok = LineGather(place, tokbuf, take(3), d.sent_rows)
        l_out = DirectGather(place, o_mid, take(2))
        l_cot = LineGather(place, cot, take(3), d.sent_rows)
        mix_sems = take(2)
        l_mix = lambda r: DirectGather(place, mixbuf.at[r], [sem.at[r] for sem in mix_sems])
        view = lambda ref, lo, m: ref.at[:, pl.ds(lo, m)]
        chains = [LineChain(place, view(part, *h), view(inbox, *h), take(2)) for h in split]
        (kept_sems,) = take(1)

        def keep(*names):
            for i in names:
                pltpu.make_async_copy(kept[i], kept_out[i], kept_sems.at[i]).start()

        if R > d.rows:
            for i in range(t):
                tokbuf[i, d.rows :, :] = jnp.zeros((R - d.rows, D), BF16)
                cot[i, d.rows :, :] = jnp.zeros((R - d.rows, D), BF16)
        tokbuf[z, : d.rows, :] = tok[...]
        cot[z, : d.rows, :] = cot_in[...]
        for i, w in enumerate((wq, wk, wv)):
            w_st[:, i * d.cols : (i + 1) * d.cols] = w[...]
        v_st[...] = jnp.zeros_like(v_st)
        for i, v in enumerate(vecs):
            m = v.shape[0]
            v_st[i : i + 1, :m] = jnp.reshape(v[...].astype(F32), (1, m))
        o_mid[z] = jnp.concatenate([wo[i * d.fold : (i + 1) * d.fold, :] for i in range(d.folds)], axis=1)
        place.meet()
        l_out.start()
        g_vec.start()
        g_qkv.start()
        l_tok.start()
        at_end = jnp.logical_or(z == 0, z == t - 1)

        @pl.when(at_end)
        def _():
            l_cot.start()

        u_st[...] = jnp.zeros_like(u_st)
        u_st[:, : d.hidden] = wu[...]
        d_st[...] = jnp.zeros_like(d_st)
        d_st[:, : d.hidden] = wd[...]
        bias_part[...] = jnp.zeros_like(bias_part)
        g_vec.forward()
        g_vec.finish()
        vec[8:, :] = jnp.zeros((8, D), F32)
        for i in range(8):
            vec[i : i + 1, :] = jnp.concatenate([v_all[j, i : i + 1, : d.share] for j in range(n)], axis=1)
        upb[...] = jnp.zeros_like(upb)
        upb[0:1, : d.hidden] = jnp.concatenate(
            [v_all[z * per_line + j, 8:9, : d.up_share] for j in range(per_line)], axis=1
        )
        local = lambda i: jnp.concatenate(
            [v_all[z * per_line + j, i : i + 1, : d.share] for j in range(per_line)], axis=1
        )
        bias_row = jnp.concatenate([local(2), jnp.zeros((1, d.cols), F32), local(3)], axis=1)
        scale_row = jnp.concatenate(
            [jnp.full((1, d.cols), scale_factor, F32), jnp.ones((1, 2 * d.cols), F32)], axis=1
        )
        gain, shift = vec[0:1, :], vec[1:2, :]

        def norm_block(slot):
            def one(r):
                normed = normalize(tokbuf[slot, r, :].astype(F32))[0]
                first[slot, r, :] = (normed * gain + shift).astype(BF16)

            chunks(d, one)

        def project_block(slot):
            y = (dot(first[slot], wqkv[...], NN) + bias_row) * scale_row
            y = y.astype(BF16)
            at = pl.ds(pl.multiple_of(slot * R, R), R)
            for i, ref in enumerate((qh, kh, vh)):
                for j in range(d.heads):
                    start = i * d.cols + j * HD
                    ref[j, at, :] = y[:, start : start + HD]

        norm_block(z)
        l_out.finish()
        for i in range(d.folds):
            o_pack[i * d.fold : (i + 1) * d.fold, :] = jnp.concatenate(
                [o_mid[j, :, i * d.cols : (i + 1) * d.cols] for j in range(t)], axis=1
            )
        g_out.start()
        l_tok.step(1)
        g_qkv.forward()
        g_up.start()
        g_down.start()
        both_sides(place, 1, norm_block)
        g_qkv.finish()
        project_block(z)
        both_sides(place, 1, project_block)

        def norm_and_project(slot):
            norm_block(slot)
            project_block(slot)

        for s in range(2, t):
            l_tok.step(s)

            @pl.when(z == s - 1)
            def _():
                l_cot.relay(0)

            @pl.when(z == t - s)
            def _():
                l_cot.relay(t - 1)

            if s == 2:

                @pl.when(jnp.logical_not(at_end))
                def _():
                    l_cot.start()

            if s == 2:
                g_out.forward()
            both_sides(place, s, norm_and_project)
        g_up.forward()
        keep(0, 1, 2, 5, 6, 10)

        count = jnp.sum(mask[...].astype(F32), axis=1, keepdims=True)
        valid = valid_keys(d, count)


        def order(i):
            pair = lax.div(i, 2)
            return jnp.where(lax.rem(i + pair, 2) == 0, pair, t - 1 - pair)

        def attend_rows(i, carry):
            r = order(i)
            at = pl.ds(pl.multiple_of(r * R, R), R)

            def head(j, carry):
                scores = dot(qh[j, at, :], kh[j], NT)
                scores = jnp.where(valid > 0, scores, MASK_FILL)
                highest = jnp.max(scores, axis=-1, keepdims=True)
                raised = jnp.exp(scores - highest)
                share = 1.0 / jnp.sum(raised, axis=-1, keepdims=True)
                probs[j, at, :] = (raised * share).astype(BF16)
                mix[j, at, :] = dot(probs[j, at, :], vh[j], NN).astype(BF16)
                return carry

            lax.fori_loop(0, d.heads, head, 0)
            own = [mix[j, at, :] for j in range(d.heads)]
            piece = lambda i, j: own[j][i * d.packed : (i + 1) * d.packed]
            mixbuf[r, z] = jnp.concatenate([piece(i, j) for i in range(t) for j in range(d.heads)], axis=1)
            l_mix(r).start()

            return carry

        lax.fori_loop(0, t, attend_rows, 0)
        keep(3, 4)
        g_up.finish()
        g_out.finish()
        keep(7)

        def block(i, carry):
            r = order(i)

            @pl.when(jnp.logical_and(i == 1, jnp.logical_not(at_end)))
            def _():
                for slot in range(1, t - 1):
                    l_cot.relay(slot)

            @pl.when(at_end)
            def _():
                l_cot.relay(r)

            @pl.when(i == 0)
            def _():
                g_down.forward()
                g_down.finish()

            grad_act[...] = dot(cot[r], down[...], NN)
            l_mix(r).finish()

            rows = jnp.concatenate(
                [
                    jnp.concatenate([mixbuf[r, j, :, k * d.cols : (k + 1) * d.cols] for j in range(t)], axis=1)
                    for k in range(t)
                ],
                axis=0,
            )
            total[...] = tokbuf[r].astype(F32) + dot(rows, out_t[...], NT) + vec[4:5, :]

            @pl.when(r == z)
            def _():
                hidden[...] = total[...]
                mixed_rows[...] = rows

            def norm_two(c):
                normed = normalize(total[c, :])[0]
                second[r, c, :] = (normed * vec[5:6, :] + vec[6:7, :]).astype(BF16)

            chunks(d, norm_two)
            pre = dot(second[r], up[...], NN) + upb[0:1, :]
            value, slope = gelu_both(pre)
            act[r] = value.astype(BF16)
            grad = grad_act[...] * slope
            bias_part[0:1, :] += jnp.sum(grad, axis=0, keepdims=True)
            pre_grad[r] = grad.astype(BF16)
            part[r] = dot(pre_grad[r], up[...], NT).astype(BF16)

            def launch(these):
                for chain in these:

                    @pl.when(r > 0)
                    def _():
                        chain.launch_right(r)

                    @pl.when(r < t - 1)
                    def _():
                        chain.launch_left(r)

            launch(chains)
            o_part[r] = dot(act[r], down[...], NT).astype(BF16)
            for h in range(1, t - 1):

                @pl.when(i >= h)
                def _():
                    for chain in chains:
                        chain.hop(h, order(i - h))

            return carry

        lax.fori_loop(0, t, block, 0)

        width = D // 3

        def weight_grad(k, left, right, i):
            value = left[:, :, i * width : (i + 1) * width].reshape(d.seq, width)
            grads[k, i * width : (i + 1) * width, :] = dot(value, right[...].reshape(d.seq, HP), TN).astype(BF16)

        work = [partial(weight_grad, 0, second, pre_grad, i) for i in range(3)]
        work += [partial(weight_grad, 1, cot, act, i) for i in range(3)]
        for i in range(t, 2 * t - 2):
            work.pop(0)()
            for h in range(i - t + 1, t - 1):
                for chain in chains:
                    chain.hop(h, order(i - h))
        for item in work:
            item()
        keep(8, 9, 11, 12, 13)
        for (lo, m), chain in zip(split, chains):
            chain.finish(grad_second, pl.ds(lo, m))
        if R > d.sent_rows:
            grad_second[d.sent_rows :, :] = jnp.zeros((R - d.sent_rows, D), F32)
        for op in (l_tok, l_cot):
            op.finish()
        for i in range(14):
            pltpu.make_async_copy(kept[i], kept_out[i], kept_sems.at[i]).wait()

    heads = (d.heads, d.seq, HD)
    outs = [shape(R, D, dtype=F32)]
    kept = [
        shape(*heads),
        shape(*heads),
        shape(*heads),
        shape(*heads),
        shape(d.heads, d.seq, d.seq),
        shape(t, R, D),
        shape(D, 3 * d.cols),
        shape(D, D),
        shape(2, D, HP),
        shape(t, R, D),
        shape(16, D, dtype=F32),
        shape(R, D, dtype=F32),
        shape(R, D),
        shape(8, HP, dtype=F32),
    ]
    scratch = [pltpu.VMEM(a.shape, a.dtype) for a in kept]
    scratch += [
        pltpu.VMEM((t, R, D), BF16),
        pltpu.VMEM((d.share, 3 * d.cols), BF16),
        pltpu.VMEM((t, d.fold, d.folds * d.cols), BF16),
        pltpu.VMEM((d.share, D), BF16),
        pltpu.VMEM((d.share, HP), BF16),
        pltpu.VMEM((d.share, HP), BF16),
        pltpu.VMEM((16, d.vec_lanes), F32),
        pltpu.VMEM((n, 16, d.vec_lanes), F32),
        pltpu.VMEM((t, t, d.packed, D), BF16),
        pltpu.VMEM((t, R, D), BF16),
        pltpu.VMEM((t, R, D), BF16),
        pltpu.VMEM((D, HP), BF16),
        pltpu.VMEM((D, HP), BF16),
        pltpu.VMEM((t, R, HP), BF16),
        pltpu.VMEM((t, R, HP), BF16),
        pltpu.VMEM((t, R, D), BF16),
        pltpu.VMEM((t + 1, R, D), BF16),
        pltpu.VMEM((8, HP), F32),
        pltpu.VMEM((R, D), F32),
        pltpu.VMEM((R, HP), F32),
    ]
    for _ in range(5):
        scratch += DpGather.sems(chips)
    scratch += LineGather.sems(t) + DirectGather.sems(t) + LineGather.sems(t) + DirectGather.sems(t, (t,))
    scratch += LineChain.sems(t) * 2 + [DMA((14,))]
    return pl.pallas_call(
        kernel,
        out_shape=outs + kept,
        in_specs=[VM] * len(args),
        out_specs=[VM] * len(outs) + [ANY] * len(kept),
        scratch_shapes=scratch,
        compiler_params=params(0),
        name="forward",
    )(*args)


class DpAdd:
    @staticmethod
    def sems(chips):
        return [DMA((chips,)), DMA((chips,)), DMA((chips,)), DMA((chips,))]

    def __init__(self, place, part, rows, near, far, sems):
        self.p, self.part, self.rows, self.near, self.far = place, part, rows, near, far
        self.sent, self.recv, self.sent_far, self.recv_far = sems

    def at(self, slot):
        return pl.ds(pl.multiple_of(slot * self.rows, 8), self.rows)

    def start(self):
        p = self.p
        for k in [*range(1, p.chips), 0]:
            src = self.part.at[self.at(2 * p.chip_at(k) + 1 - p.core)]
            remote(src, self.near.at[k], self.sent.at[k], self.recv.at[k], p.sibling).start()

    def wait_near(self, k):
        block = self.near.at[k]
        remote(block, block, self.sent.at[k], self.recv.at[k], self.p.sibling).wait_recv()

    def move(self):
        p = self.p
        for k in range(1, p.chips):
            self.wait_near(k)
            mine = self.part[self.at(2 * p.chip_at(k) + p.core), :]
            self.near[k] = (mine.astype(F32) + self.near[k].astype(F32)).astype(BF16)
            remote(self.near.at[k], self.far.at[k - 1], self.sent_far.at[k], self.recv_far.at[k], p.peer(k)).start()

    def finish(self):
        p = self.p
        self.wait_near(0)
        total = self.part[self.at(p.dp), :].astype(F32) + self.near[0].astype(F32)
        for k in range(1, p.chips):
            block = self.far.at[k - 1]
            remote(block, block, self.sent_far.at[k], self.recv_far.at[k], p.sibling).wait_recv()
            total += self.far[k - 1].astype(F32)
        for k in range(p.chips):
            block = self.near.at[0]
            remote(block, block, self.sent.at[k], self.recv.at[0], p.sibling).wait_send()
            if k > 0:
                remote(block, block, self.sent_far.at[k], self.recv.at[0], p.sibling).wait_send()
        return total


def backward(d, args):
    n, t, R, D, HP = d.n, d.t, d.block, d.width, d.hidden_pad
    chips, per_line, share = n // 2, n // t, d.share
    scale_factor = 1.0 / math.sqrt(HD)
    wide = 3 * d.cols

    def kernel(*refs):
        refs = list(refs)
        take = lambda m: [refs.pop(0) for _ in range(m)]
        tok, cot = take(2)
        far = take(15)
        output, input_grad, g_q, g_k, g_v, g_out, g_up, g_down, g_vec = take(9)
        near = take(15)
        grad_second, qh, kh, vh, mix, probs, first, wqkv, out_t, grads_mlp, p_part, vec, hidden, mixed_rows, bias_part = near
        tok_p, cot_p, gh, low, send, got, dq, dk, dv, q_sum, grads = take(11)
        o_part, w_part, f_part, f_inbox, p_inbox, f_sum, acc = take(7)
        o_mid, o_got, v_send, v_got, v_mid, v_line = take(6)
        place = Place(n, t)
        place.greet(every=True)
        z, dp = place.z, place.dp

        def adder(part):
            near, far = take(2)
            return part, near, far

        up_grad, down_grad = grads_mlp.at[0], grads_mlp.at[1]
        spaces = [adder(part) for part in (up_grad, down_grad, o_part, w_part)]
        sum_up, sum_down, sum_out, sum_qkv = [
            DpAdd(place, part, share, near, far, take(4)) for part, near, far in spaces
        ]
        split = halves(d)
        view = lambda ref, lo, m: ref.at[:, pl.ds(lo, m)]
        f_chains = [LineChain(place, view(f_part, *h), view(f_inbox, *h), take(2)) for h in split]
        p_chains = [LineChain(place, view(p_part, *h), view(p_inbox, *h), take(2)) for h in split]
        exchange = LineExchange(place, o_mid, o_got, take(3))
        x_sent, x_recv, v_sent, v_recv, v_sent_line, v_recv_line, far_sems = take(7)
        load = lambda i: pltpu.make_async_copy(far[i + 1], near[i + 1], far_sems.at[i + 1])
        for i in (9, 11, -1, 10, 8, 7, 12, 4, 0, 1, 2, 3, 6, 5, 13):
            load(i).start()
        place.meet()
        load(9).wait()
        for chain in p_chains:
            chain.launch_right(t - 1)
            chain.launch_left(0)
        load(8).wait()
        sum_up.start()
        sum_down.start()
        for ref, src in ((tok_p, tok), (cot_p, cot)):
            ref[: d.rows, :] = src[...]
            if R > d.rows:
                ref[d.rows :, :] = jnp.zeros((R - d.rows, D), BF16)
        acc[...] = jnp.zeros_like(acc)

        def add_row(i, value):
            acc[i : i + 1, :] += jnp.sum(value, axis=0, keepdims=True)

        def norm_two(r):
            normed, inv = normalize(hidden[r, :])
            grad = grad_second[r, :]
            scaled = grad * vec[5:6, :]
            cots = cot_p[r, :].astype(F32)
            mean = jnp.mean(scaled, axis=-1, keepdims=True)
            pull = jnp.mean(scaled * normed, axis=-1, keepdims=True)
            total = cots + inv * (scaled - mean - normed * pull)
            gh[r, :] = total
            low[r, :] = total.astype(BF16)
            add_row(5, grad * normed)
            add_row(6, grad)
            add_row(4, total)
            add_row(7, cots)

        for i in (11, -1, 10):
            load(i).wait()
        chunks(d, norm_two)
        load(7).wait()
        mixed_grad = dot(low[...], out_t[...], NN).astype(BF16)
        for i in range(t):
            own = mixed_grad[:, i * d.cols : (i + 1) * d.cols]
            send[i] = jnp.concatenate([own[j * d.packed : (j + 1) * d.packed] for j in range(t)], axis=1)
        for k in range(1, t):
            to = place.along(k)
            remote(send.at[to[1]], got.at[z], x_sent.at[k], x_recv.at[z], to).start()
        got[z] = send[z]
        for i in range(t - 2, 1, -1):
            for chain in p_chains:
                chain.launch_right(i)
                chain.launch_left(t - 1 - i)
        p_chains[0].launch_right(1)
        p_chains[0].launch_left(t - 2)
        sum_up.move()
        third = D // 3
        load(12).wait()
        for i in range(3):
            o_part[i * third : (i + 1) * third, :] = dot(
                low[:, i * third : (i + 1) * third], mixed_rows[...], TN
            ).astype(BF16)
        sum_out.start()
        for i in range(5):
            load(i).wait()

        for ref in (dk, dv, q_sum):
            ref[...] = jnp.zeros_like(ref)

        def attend_rows(r):
            at = pl.ds(pl.multiple_of(r * R, R), R)
            for j in range(d.heads):
                pieces = [got[r, :, i * d.cols + j * HD : i * d.cols + (j + 1) * HD] for i in range(t)]
                dq[j, at, :] = jnp.concatenate(pieces, axis=0)

            def head(j, carry):
                grad = dq[j, at, :]
                full = probs[j, at, :]
                dv[j] += dot(full, grad, TN)
                delta = jnp.sum(grad.astype(F32) * mix[j, at, :].astype(F32), axis=-1, keepdims=True)
                grad_scores = (full.astype(F32) * (dot(grad, vh[j], NT) - delta)).astype(BF16)
                dk[j] += dot(grad_scores, qh[j, at, :], TN)
                query = dot(grad_scores, kh[j], NN) * scale_factor
                q_sum[j, 0:1, :] += jnp.sum(query, axis=0, keepdims=True)
                dq[j, at, :] = query.astype(BF16)
                return carry

            lax.fori_loop(0, d.heads, head, 0)

        attend_rows(z)
        sum_down.move()
        for k in range(1, t):
            slot = place.along(k)[1]
            remote(got.at[slot], got.at[slot], x_sent.at[k], x_recv.at[slot], place.sibling).wait_recv()
            attend_rows(slot)
            if k == 1:
                sum_out.move()
                for chain in p_chains:
                    chain.tick_far(1)
        for i in (6, 5, 13):
            load(i).wait()

        def part_block(i):
            slot = jnp.where(z < t // 2, t - 1 - i, i)
            at = pl.ds(pl.multiple_of(slot * R, R), R)
            values = [dq[j, at, :] for j in range(d.heads)]
            values += [ref[j, at, :].astype(BF16) for ref in (dk, dv) for j in range(d.heads)]
            grads[at, :] = jnp.concatenate(values, axis=1)
            f_part[slot] = dot(grads[at, :], wqkv[...], NT).astype(BF16)
            for chain in f_chains:

                @pl.when(slot > 0)
                def _():
                    chain.launch_right(slot)

                @pl.when(slot < t - 1)
                def _():
                    chain.launch_left(slot)

        for i in range(t):
            part_block(i)
        for chain in p_chains[1:]:
            chain.launch_right(1)
            chain.launch_left(t - 2)
        for i in range(2, t - 1):
            for chain in p_chains:
                chain.tick_far(i)

        def weight_block(i):
            value = first[:, :, i * third : (i + 1) * third].reshape(d.seq, third)
            w_part[i * third : (i + 1) * third, :] = dot(value, grads[...], TN).astype(BF16)

        for i in range(3):
            weight_block(i)
        sum_qkv.start()
        g_up[...] = sum_up.finish()[:, : d.hidden]
        for chain in f_chains:
            chain.tick_far(1)
        sum_qkv.move()
        g_down[...] = sum_down.finish()[:, : d.hidden]
        for i in range(2, t - 1):
            for chain in f_chains:
                chain.tick_far(i)
        out_total = sum_out.finish().astype(BF16)
        for i in range(t):
            o_mid[i] = jnp.concatenate(
                [out_total[j * d.fold : (j + 1) * d.fold, i * d.cols : (i + 1) * d.cols] for j in range(d.folds)], axis=1
            )
        exchange.start()
        v_send[...] = jnp.zeros_like(v_send)
        q_row = jnp.concatenate([q_sum[j, 0:1, :] for j in range(d.heads)], axis=1)
        v_row = jnp.concatenate([jnp.sum(dv[j], axis=0, keepdims=True) for j in range(d.heads)], axis=1)
        for j in range(per_line):
            slot = z * per_line + j
            v_send[slot, 2:3, :share] = q_row[:, j * share : (j + 1) * share]
            v_send[slot, 3:4, :share] = v_row[:, j * share : (j + 1) * share]
            v_send[slot, 8:9, : d.up_share] = bias_part[0:1, j * d.up_share : (j + 1) * d.up_share]
        for (lo, m), chain in zip(split, f_chains):
            chain.finish(f_sum, pl.ds(lo, m))
        if R > d.sent_rows:
            f_sum[d.sent_rows :, :] = jnp.zeros((R - d.sent_rows, D), F32)

        def norm_one_sums(r):
            normed = normalize(tok_p[r, :].astype(F32))[0]
            grad = f_sum[r, :]
            add_row(0, grad * normed)
            add_row(1, grad)

        def norm_one(r):
            normed, inv = normalize(tok_p[r, :].astype(F32))
            scaled = f_sum[r, :] * vec[0:1, :]
            mean = jnp.mean(scaled, axis=-1, keepdims=True)
            pull = jnp.mean(scaled * normed, axis=-1, keepdims=True)
            input_grad[r, :] = gh[r, :] + inv * (scaled - mean - normed * pull)

        chunks(d, norm_one_sums)
        for i in (0, 1, 4, 5, 6, 7):
            for j in range(n):
                v_send[j, i : i + 1, :share] = acc[i : i + 1, j * share : (j + 1) * share]
        others = [lax.rem(dp + k, n) for k in range(1, n)]
        for k in range(1, n):
            to = others[k - 1]
            remote(v_send.at[to], v_got.at[k], v_sent.at[k], v_recv.at[k], (to, z)).start()
        chunks(d, norm_one)
        total = v_send[dp]
        for k in range(1, n):
            remote(v_got.at[k], v_got.at[k], v_sent.at[k], v_recv.at[k], place.sibling).wait()
            total += v_got[k]
        v_mid[...] = total
        for k in range(1, t):
            remote(v_mid, v_line.at[k], v_sent_line.at[k], v_recv_line.at[k], place.along(k)).start()
        qkv_total = sum_qkv.finish()
        for i, ref in enumerate((g_q, g_k, g_v)):
            ref[...] = qkv_total[:, i * d.cols : (i + 1) * d.cols]
        exchange.finish()
        out_sum = jnp.sum(o_got[...].astype(F32), axis=0)
        for i in range(d.folds):
            g_out[i * d.fold : (i + 1) * d.fold, :] = out_sum[:, i * d.cols : (i + 1) * d.cols]
        for (lo, m), chain in zip(split, p_chains):
            chain.finish(f_sum, pl.ds(lo, m))
        if R > d.sent_rows:
            f_sum[d.sent_rows :, :] = jnp.zeros((R - d.sent_rows, D), F32)
        output[...] = (hidden[...] + f_sum[...] + vec[7:8, :]).astype(BF16)
        for k in range(1, t):
            remote(v_mid, v_line.at[k], v_sent_line.at[k], v_recv_line.at[k], place.sibling).wait()
            total += v_line[k]
        g_vec[...] = total
        for k in range(1, t):
            remote(send.at[0], got.at[0], x_sent.at[k], x_recv.at[0], place.sibling).wait_send()

    outs = [
        shape(R, D),
        shape(R, D, dtype=F32),
        shape(share, d.cols, dtype=F32),
        shape(share, d.cols, dtype=F32),
        shape(share, d.cols, dtype=F32),
        shape(share, d.cols, dtype=F32),
        shape(share, d.hidden, dtype=F32),
        shape(share, d.hidden, dtype=F32),
        shape(16, d.vec_lanes, dtype=F32),
    ]
    heads = (d.heads, d.seq, HD)
    scratch = [pltpu.VMEM(a.shape, a.dtype) for a in args[2:]]
    scratch += [
        pltpu.VMEM((R, D), BF16),
        pltpu.VMEM((R, D), BF16),
        pltpu.VMEM((R, D), F32),
        pltpu.VMEM((R, D), BF16),
        pltpu.VMEM((t, d.packed, D), BF16),
        pltpu.VMEM((t, d.packed, D), BF16),
        pltpu.VMEM(heads, BF16),
        pltpu.VMEM(heads, F32),
        pltpu.VMEM(heads, F32),
        pltpu.VMEM((d.heads, 8, HD), F32),
        pltpu.VMEM((d.seq, wide), BF16),
        pltpu.VMEM((D, D), BF16),
        pltpu.VMEM((D, wide), BF16),
        pltpu.VMEM((t, R, D), BF16),
        pltpu.VMEM((t + 1, R, D), BF16),
        pltpu.VMEM((t + 1, R, D), BF16),
        pltpu.VMEM((R, D), F32),
        pltpu.VMEM((16, D), F32),
        pltpu.VMEM((t, d.fold, d.folds * d.cols), BF16),
        pltpu.VMEM((t, d.fold, d.folds * d.cols), BF16),
        pltpu.VMEM((n, 16, d.vec_lanes), F32),
        pltpu.VMEM((n, 16, d.vec_lanes), F32),
        pltpu.VMEM((16, d.vec_lanes), F32),
        pltpu.VMEM((t, 16, d.vec_lanes), F32),
    ]
    for width in (HP, HP, D, wide):
        scratch += [pltpu.VMEM((chips, share, width), BF16), pltpu.VMEM((chips - 1, share, width), BF16)]
    scratch += DpAdd.sems(chips) * 4 + LineChain.sems(t) * 4 + LineExchange.sems(t)
    scratch += [DMA((t,)), DMA((t,)), DMA((n,)), DMA((n,)), DMA((t,)), DMA((t,)), DMA((15,))]
    return pl.pallas_call(
        kernel,
        out_shape=outs,
        in_specs=[VM] * 2 + [ANY] * 15,
        out_specs=[VM] * len(outs),
        scratch_shapes=scratch,
        compiler_params=params(1),
        name="backward",
    )(*args)


def finalize(d, args):
    names = len(args) - 1
    f32 = partial(shape, dtype=F32)
    outs = [shape(d.rows, d.width), f32(d.rows, d.width)] + [f32(*a.shape) for a in args[2:-1]]
    vectors = [f32(d.share)] * 8 + [f32(d.up_share)]

    def kernel(*refs):
        ins, g_vec, results = refs[:names], refs[names], refs[names + 1 :]
        for src, dst in zip(ins, results):
            dst[...] = src[: dst.shape[0], :]
        for i, ref in enumerate(results[names:]):
            m = ref.shape[0]
            ref[...] = jnp.reshape(g_vec[i : i + 1, :m], (m,))

    return pl.pallas_call(
        kernel,
        out_shape=outs + vectors,
        in_specs=[VM] * len(args),
        out_specs=[VM] * (names + 9),
        compiler_params=pltpu.CompilerParams(vmem_limit_bytes=VMEM_BYTES),
        name="finalize",
    )(*args)


def shards(
    sizes,
    tokens,
    key_mask,
    query_weight,
    key_weight,
    value_weight,
    out_weight,
    up_weight,
    down_weight,
    first_gain,
    first_shift,
    query_bias,
    value_bias,
    out_bias,
    second_gain,
    second_shift,
    up_bias,
    down_bias,
    cotangent,
):
    rows, width = tokens.shape[1:]
    share, up_share = first_gain.shape[0], up_bias.shape[0]
    cols, hidden_cols = query_weight.shape[1], up_weight.shape[1]
    d = Dims(sizes, rows, width, share, cols, hidden_cols, up_share)
    small = [first_gain, first_shift, query_bias, value_bias, out_bias, second_gain, second_shift, down_bias]
    kept = forward(
        d,
        [tokens[0], cotangent[0], key_mask, query_weight, key_weight, value_weight, out_weight.T, up_weight, down_weight.T]
        + small
        + [up_bias],
    )
    parts = backward(d, [tokens[0], cotangent[0], *kept])
    outs = finalize(d, parts)
    vectors = outs[8:]
    return (outs[0][None], outs[1][None], *outs[2:5], outs[5].T, outs[6], outs[7].T, *vectors[:7], vectors[8], vectors[7])


def solution(mesh):
    sizes = (mesh.shape["dp"], mesh.shape["tensor"])
    split = P("dp", "tensor")
    return jax.shard_map(
        partial(shards, sizes),
        mesh=mesh,
        in_specs=(P("dp", "tensor", None), P("dp", None), split, split, split, P("tensor", "dp"), split, P("tensor", "dp"))
        + (P("dp"),) * 9
        + (P("dp", "tensor", None),),
        out_specs=(P("dp", "tensor", None), P("dp", "tensor", None), split, split, split, P("tensor", "dp"), split, P("tensor", "dp"))
        + (P("dp"),) * 9,
        check_vma=False,
    )
```

```python
from functools import partial
import math

import jax
import jax.numpy as jnp
from jax import lax
from jax.experimental import pallas as pl
from jax.experimental.pallas import tpu as pltpu
from jax.sharding import PartitionSpec as P

HD = 72
EPSILON = 1e-06
GELU_COEF = 0.7978845608028654
MASK_FILL = -1e30
MESH = pl.DeviceIdType.MESH
ANY = pl.BlockSpec(memory_space=pl.ANY)
VM = pl.BlockSpec(memory_space=pltpu.VMEM)
DMA = pltpu.SemaphoreType.DMA
VMEM_BYTES = 60 << 20
F32 = jnp.float32
BF16 = jnp.bfloat16


def remote(src, dst, send_sem, recv_sem, device):
    return pltpu.make_async_remote_copy(
        src_ref=src,
        dst_ref=dst,
        send_sem=send_sem,
        recv_sem=recv_sem,
        device_id=device,
        device_id_type=MESH,
    )


class Place:
    def __init__(self, dp_size, line):
        self.dp_size, self.line, self.chips = dp_size, line, dp_size // 2
        self.dp = lax.axis_index("dp")
        self.z = lax.axis_index("tensor")
        self.core = lax.rem(self.dp, 2)
        self.chip = lax.div(self.dp, 2)
        self.sibling = (2 * self.chip + 1 - self.core, self.z)

    def chip_at(self, k):
        return lax.rem(self.chip + k + self.chips, self.chips)

    def peer(self, k):
        return (2 * self.chip_at(k) + self.core, self.z)

    def along(self, k):
        return (self.dp, lax.rem(self.z + k + self.line, self.line))

    def greet(self, every=False):
        barrier = pltpu.get_barrier_semaphore()
        if every:
            devices = [(lax.rem(self.dp + k, self.dp_size), self.z) for k in range(1, self.dp_size)]
        else:
            devices = [self.peer(k) for k in range(1, self.chips)] + [self.sibling]
        devices += [self.along(k) for k in range(1, self.line)]
        for device in devices:
            pl.semaphore_signal(barrier, inc=1, device_id=device, device_id_type=MESH)
        self.partners = len(devices)

    def meet(self):
        pl.semaphore_wait(pltpu.get_barrier_semaphore(), self.partners)


class DpGather:
    @staticmethod
    def sems(chips):
        return [DMA((chips,)), DMA((chips,)), DMA((2 * chips,)), DMA(())]

    def __init__(self, place, src, dst, sems, at=None):
        self.p, self.src, self.dst = place, src, dst
        self.across, self.inside, self.recv, self.local = sems
        self.at = at if at is not None else (lambda slot: dst.at[slot])

    def start(self):
        p = self.p
        mine = self.at(p.dp)
        for k in range(1, p.chips):
            remote(self.src, mine, self.across.at[k], self.recv.at[p.dp], p.peer(k)).start()
        remote(self.src, mine, self.inside.at[0], self.recv.at[p.dp], p.sibling).start()
        pltpu.make_async_copy(self.src, mine, self.local).start()

    def forward(self):
        p = self.p
        for k in range(1, p.chips):
            slot = 2 * p.chip_at(-k) + p.core
            block = self.at(slot)
            remote(block, block, self.across.at[k], self.recv.at[slot], p.sibling).wait_recv()
            remote(block, block, self.inside.at[k], self.recv.at[slot], p.sibling).start()

    def finish(self):
        p = self.p
        mine = self.at(p.dp)
        for k in range(p.chips):
            slot = 2 * p.chip_at(-k) + 1 - p.core
            block = self.at(slot)
            remote(block, block, self.inside.at[k], self.recv.at[slot], p.sibling).wait_recv()
        for k in range(p.chips):
            remote(self.src, mine, self.inside.at[k], self.recv.at[0], p.sibling).wait_send()
            if k > 0:
                remote(self.src, mine, self.across.at[k], self.recv.at[0], p.sibling).wait_send()
        pltpu.make_async_copy(self.src, mine, self.local).wait()


class LineGather:
    @staticmethod
    def sems(line, many=()):
        return [DMA((*many, line)), DMA((*many, line)), DMA((*many, line))]

    def __init__(self, place, dst, sems, rows=None):
        self.p, self.dst = place, dst
        self.right, self.left, self.recv = sems
        self.at = (lambda slot: dst.at[slot]) if rows is None else (lambda slot: dst.at[slot, pl.ds(0, rows)])

    def send_right(self, slot):
        p = self.p
        block = self.at(slot)

        @pl.when(p.z < p.line - 1)
        def _():
            remote(block, block, self.right.at[slot], self.recv.at[slot], (p.dp, p.z + 1)).start()

    def send_left(self, slot):
        p = self.p
        block = self.at(slot)

        @pl.when(p.z > 0)
        def _():
            remote(block, block, self.left.at[slot], self.recv.at[slot], (p.dp, p.z - 1)).start()

    def start(self):
        self.send_right(self.p.z)
        self.send_left(self.p.z)

    def arrive(self, slot):
        block = self.at(slot)
        remote(block, block, self.right.at[slot], self.recv.at[slot], self.p.sibling).wait_recv()

    def relay(self, slot):
        p = self.p

        @pl.when(jnp.logical_and(p.z > slot, slot >= 0))
        def _():
            self.arrive(slot)
            self.send_right(slot)

        @pl.when(jnp.logical_and(p.z < slot, slot < p.line))
        def _():
            self.arrive(slot)
            self.send_left(slot)

    def step(self, s):
        self.relay(self.p.z - s)
        self.relay(self.p.z + s)

    def finish(self):
        p = self.p
        for slot in range(p.line):
            block = self.at(slot)

            @pl.when(jnp.logical_and(p.z >= slot, p.z < p.line - 1))
            def _():
                remote(block, block, self.right.at[slot], self.recv.at[slot], p.sibling).wait_send()

            @pl.when(jnp.logical_and(p.z <= slot, p.z > 0))
            def _():
                remote(block, block, self.left.at[slot], self.recv.at[slot], p.sibling).wait_send()


class DirectGather:
    @staticmethod
    def sems(line, many=()):
        return [DMA((*many, line)), DMA((*many, line))]

    def __init__(self, place, dst, sems):
        self.p, self.dst = place, dst
        self.sent, self.recv = sems

    def start(self):
        p = self.p
        block = self.dst.at[p.z]
        for k in range(1, p.line):
            step = jnp.where(p.z < p.line // 2, p.line - k, k)
            remote(block, block, self.sent.at[k], self.recv.at[p.z], p.along(step)).start()

    def finish(self):
        p = self.p
        for k in range(1, p.line):
            slot = p.along(k)[1]
            block = self.dst.at[slot]
            remote(block, block, self.sent.at[k], self.recv.at[slot], p.sibling).wait()


class LineExchange:
    @staticmethod
    def sems(line):
        return [DMA((line,)), DMA((line,)), DMA(())]

    def __init__(self, place, src, dst, sems):
        self.p, self.src, self.dst = place, src, dst
        self.sent, self.recv, self.local = sems

    def start(self):
        p = self.p
        for k in range(1, p.line):
            to = p.along(k)
            remote(self.src.at[to[1]], self.dst.at[p.z], self.sent.at[k], self.recv.at[p.z], to).start()
        pltpu.make_async_copy(self.src.at[p.z], self.dst.at[p.z], self.local).start()

    def finish(self):
        p = self.p
        for k in range(1, p.line):
            slot = p.along(k)[1]
            block = self.dst.at[slot]
            remote(block, block, self.sent.at[k], self.recv.at[slot], p.sibling).wait_recv()
        for k in range(1, p.line):
            block = self.src.at[0]
            remote(block, block, self.sent.at[k], self.recv.at[0], p.sibling).wait_send()
        pltpu.make_async_copy(self.src.at[p.z], self.dst.at[p.z], self.local).wait()


def params(collective_id):
    return pltpu.CompilerParams(
        collective_id=collective_id, has_side_effects=True, vmem_limit_bytes=VMEM_BYTES
    )


def shape(*dims, dtype=BF16):
    return jax.ShapeDtypeStruct(dims, dtype)


def pad_to(count, unit):
    return -(-count // unit) * unit


def normalize(x):
    centred = x - jnp.mean(x, axis=-1, keepdims=True)
    inv_std = lax.rsqrt(jnp.mean(centred * centred, axis=-1, keepdims=True) + EPSILON)
    return centred * inv_std, inv_std


def dot(left, right, contract):
    return lax.dot_general(left, right, ((contract[:1], contract[1:]), ((), ())), preferred_element_type=F32)


NN, NT, TN = (1, 0), (1, 1), (0, 0)


class Dims:
    def __init__(self, sizes, rows, width, share, cols, hidden, up_share):
        self.n, self.t = sizes
        self.rows, self.width, self.share, self.cols = rows, width, share, cols
        self.hidden, self.up_share = hidden, up_share
        self.heads = cols // HD
        self.block = pad_to(rows, 16)
        self.sent_rows = rows if rows % 8 == 0 else self.block
        self.seq = self.t * self.block
        self.hidden_pad = pad_to(hidden, 128)
        self.vec_lanes = pad_to(max(up_share, share), 128)
        self.packed = self.block // self.t
        self.folds = 3 if share % 3 == 0 else 1
        self.fold = share // self.folds
        self.chunk = 32 if self.block % 32 == 0 else 16


def both_sides(place, s, work):
    def side(i, carry):
        slot = place.z - s + 2 * s * i

        @pl.when(jnp.logical_and(slot >= 0, slot < place.line))
        def _():
            work(slot)

        return carry

    lax.fori_loop(0, 2, side, 0)


def chunks(d, work):
    def one(i, carry):
        work(pl.ds(pl.multiple_of(i * d.chunk, d.chunk), d.chunk))
        return carry

    lax.fori_loop(0, d.block // d.chunk, one, 0)


def valid_keys(d, count):
    lane = lax.broadcasted_iota(jnp.int32, (1, d.seq), 1)
    zero = jnp.zeros((1, d.seq), jnp.int32)
    blk = sum([(lane >= d.block * i).astype(jnp.int32) for i in range(1, d.t)], zero)
    off = lane - blk * d.block
    inside = jnp.logical_and(off < d.rows, (off + blk * d.rows).astype(F32) < count)
    return jnp.where(inside, 1.0, 0.0)


class LineChain:
    @staticmethod
    def sems(line):
        return [DMA((line,)), DMA((line + 1,))]

    def __init__(self, place, part, inbox, sems):
        self.p, self.part, self.inbox = place, part, inbox
        self.sent, self.recv = sems

    def wait(self, slot):
        block = self.inbox.at[slot]
        remote(block, block, self.sent.at[0], self.recv.at[slot], self.p.sibling).wait_recv()

    def right(self, src, d):
        p = self.p
        remote(src.at[d], self.inbox.at[d], self.sent.at[d], self.recv.at[d], (p.dp, p.z + 1)).start()

    def left(self, src, d):
        p = self.p
        slot = jnp.where(d == p.z - 1, p.line, d)
        remote(src.at[d], self.inbox.at[slot], self.sent.at[d], self.recv.at[slot], (p.dp, p.z - 1)).start()

    def launch_right(self, d):
        @pl.when(self.p.z == 0)
        def _():
            self.right(self.part, d)

    def launch_left(self, d):
        @pl.when(self.p.z == self.p.line - 1)
        def _():
            self.left(self.part, d)

    def relay_right(self, d):
        p = self.p

        @pl.when((p.z > 0) & (p.z < d) & (d < p.line))
        def _():
            self.wait(d)
            self.inbox[d] = (self.inbox[d].astype(F32) + self.part[d].astype(F32)).astype(BF16)
            self.right(self.inbox, d)

    def relay_left(self, d):
        p = self.p

        @pl.when((p.z < p.line - 1) & (p.z > d) & (d >= 0))
        def _():
            self.wait(d)
            self.inbox[d] = (self.inbox[d].astype(F32) + self.part[d].astype(F32)).astype(BF16)
            self.left(self.inbox, d)

    def hop(self, h, d):
        p = self.p

        @pl.when(p.z == h)
        def _():
            self.relay_right(d)

        @pl.when(p.z == p.line - 1 - h)
        def _():
            self.relay_left(d)

    def tick_far(self, i):
        p = self.p
        self.relay_right(p.line - 1 + p.z - i)
        self.relay_left(i - p.line + 1 + p.z)

    def finish(self, out, rows):
        p = self.p
        out[rows, :] = self.part[p.z].astype(F32)

        @pl.when(p.z > 0)
        def _():
            self.wait(p.z)
            out[rows, :] += self.inbox[p.z].astype(F32)

        @pl.when(p.z < p.line - 1)
        def _():
            self.wait(p.line)
            out[rows, :] += self.inbox[p.line].astype(F32)

        for d in range(p.line):

            @pl.when(p.z != d)
            def _():
                block = self.part.at[d]
                remote(block, block, self.sent.at[d], self.recv.at[d], p.sibling).wait_send()


def halves(d):
    cut = pad_to(d.sent_rows // 2, 16)
    return ((0, cut), (cut, d.sent_rows - cut))


def gelu_both(u):
    square = u * u
    tanh_val = jnp.tanh(GELU_COEF * (u + 0.044715 * u * square))
    half = 0.5 * (1.0 + tanh_val)
    slope = half + 0.5 * u * (1.0 - tanh_val * tanh_val) * (GELU_COEF * (1.0 + 3.0 * 0.044715 * square))
    return u * half, slope


def forward(d, args):
    n, t, R, D, HP = d.n, d.t, d.block, d.width, d.hidden_pad
    chips = n // 2
    per_line = n // t
    scale_factor = 1.0 / math.sqrt(HD)
    split = halves(d)

    def kernel(*refs):
        refs = list(refs)
        take = lambda m: [refs.pop(0) for _ in range(m)]
        tok, cot_in, mask, wq, wk, wv, wo, wu, wd = take(9)
        vecs = take(9)
        (grad_second,) = take(1)
        kept_out = take(14)
        kept = take(14)
        qh, kh, vh, mix, probs, first, wqkv, out_t, grads, o_part, vec, hidden, mixed_rows, bias_part = kept
        tokbuf, w_st, o_mid, o_pack, u_st, d_st, v_st, v_all = take(8)
        mixbuf, second, cot, up, down, act, pre_grad, part, inbox, upb, total, grad_act = take(12)
        place = Place(n, t)
        place.greet()
        z = place.z
        rows_of = lambda ref: (lambda slot: ref.at[pl.ds(pl.multiple_of(slot * d.share, 8), d.share)])
        g_vec = DpGather(place, v_st, v_all, take(4))
        g_qkv = DpGather(place, w_st, wqkv, take(4), rows_of(wqkv))
        g_up = DpGather(place, u_st, up, take(4), rows_of(up))
        g_down = DpGather(place, d_st, down, take(4), rows_of(down))
        g_out = DpGather(place, o_pack, out_t, take(4), rows_of(out_t))
        l_tok = LineGather(place, tokbuf, take(3), d.sent_rows)
        l_out = DirectGather(place, o_mid, take(2))
        l_cot = LineGather(place, cot, take(3), d.sent_rows)
        mix_sems = take(2)
        l_mix = lambda r: DirectGather(place, mixbuf.at[r], [sem.at[r] for sem in mix_sems])
        view = lambda ref, lo, m: ref.at[:, pl.ds(lo, m)]
        chains = [LineChain(place, view(part, *h), view(inbox, *h), take(2)) for h in split]
        (kept_sems,) = take(1)

        def keep(*names):
            for i in names:
                pltpu.make_async_copy(kept[i], kept_out[i], kept_sems.at[i]).start()

        if R > d.rows:
            for i in range(t):
                tokbuf[i, d.rows :, :] = jnp.zeros((R - d.rows, D), BF16)
                cot[i, d.rows :, :] = jnp.zeros((R - d.rows, D), BF16)
        tokbuf[z, : d.rows, :] = tok[...]
        cot[z, : d.rows, :] = cot_in[...]
        for i, w in enumerate((wq, wk, wv)):
            w_st[:, i * d.cols : (i + 1) * d.cols] = w[...]
        v_st[...] = jnp.zeros_like(v_st)
        for i, v in enumerate(vecs):
            m = v.shape[0]
            v_st[i : i + 1, :m] = jnp.reshape(v[...].astype(F32), (1, m))
        o_mid[z] = jnp.concatenate([wo[i * d.fold : (i + 1) * d.fold, :] for i in range(d.folds)], axis=1)
        place.meet()
        g_vec.start()
        g_qkv.start()
        l_tok.start()
        l_out.start()
        at_end = jnp.logical_or(z == 0, z == t - 1)

        @pl.when(at_end)
        def _():
            l_cot.start()

        u_st[...] = jnp.zeros_like(u_st)
        u_st[:, : d.hidden] = wu[...]
        g_up.start()
        d_st[...] = jnp.zeros_like(d_st)
        d_st[:, : d.hidden] = wd[...]
        bias_part[...] = jnp.zeros_like(bias_part)
        g_vec.forward()
        g_vec.finish()
        vec[8:, :] = jnp.zeros((8, D), F32)
        for i in range(8):
            vec[i : i + 1, :] = jnp.concatenate([v_all[j, i : i + 1, : d.share] for j in range(n)], axis=1)
        upb[...] = jnp.zeros_like(upb)
        upb[0:1, : d.hidden] = jnp.concatenate(
            [v_all[z * per_line + j, 8:9, : d.up_share] for j in range(per_line)], axis=1
        )
        local = lambda i: jnp.concatenate(
            [v_all[z * per_line + j, i : i + 1, : d.share] for j in range(per_line)], axis=1
        )
        bias_row = jnp.concatenate([local(2), jnp.zeros((1, d.cols), F32), local(3)], axis=1)
        scale_row = jnp.concatenate(
            [jnp.full((1, d.cols), scale_factor, F32), jnp.ones((1, 2 * d.cols), F32)], axis=1
        )
        gain, shift = vec[0:1, :], vec[1:2, :]

        def norm_block(slot):
            def one(r):
                normed = normalize(tokbuf[slot, r, :].astype(F32))[0]
                first[slot, r, :] = (normed * gain + shift).astype(BF16)

            chunks(d, one)

        def project_block(slot):
            y = (dot(first[slot], wqkv[...], NN) + bias_row) * scale_row
            y = y.astype(BF16)
            at = pl.ds(pl.multiple_of(slot * R, R), R)
            for i, ref in enumerate((qh, kh, vh)):
                for j in range(d.heads):
                    start = i * d.cols + j * HD
                    ref[j, at, :] = y[:, start : start + HD]

        norm_block(z)
        l_tok.step(1)
        l_out.finish()
        for i in range(d.folds):
            o_pack[i * d.fold : (i + 1) * d.fold, :] = jnp.concatenate(
                [o_mid[j, :, i * d.cols : (i + 1) * d.cols] for j in range(t)], axis=1
            )
        g_out.start()
        g_down.start()
        g_qkv.forward()
        both_sides(place, 1, norm_block)
        g_qkv.finish()
        project_block(z)
        both_sides(place, 1, project_block)

        def norm_and_project(slot):
            norm_block(slot)
            project_block(slot)

        for s in range(2, t):
            l_tok.step(s)

            @pl.when(z == s - 1)
            def _():
                l_cot.relay(0)

            @pl.when(z == t - s)
            def _():
                l_cot.relay(t - 1)

            if s == 2:

                @pl.when(jnp.logical_not(at_end))
                def _():
                    l_cot.start()

            if s == 2:
                g_up.forward()
            both_sides(place, s, norm_and_project)
        g_out.forward()
        keep(0, 1, 2, 5, 6, 10)

        count = jnp.sum(mask[...].astype(F32), axis=1, keepdims=True)
        valid = valid_keys(d, count)


        def order(i):
            pair = lax.div(i, 2)
            return jnp.where(lax.rem(i + pair, 2) == 0, pair, t - 1 - pair)

        def attend_rows(i, carry):
            r = order(i)
            at = pl.ds(pl.multiple_of(r * R, R), R)

            def head(j, carry):
                scores = dot(qh[j, at, :], kh[j], NT)
                scores = jnp.where(valid > 0, scores, MASK_FILL)
                highest = jnp.max(scores, axis=-1, keepdims=True)
                raised = jnp.exp(scores - highest)
                share = 1.0 / jnp.sum(raised, axis=-1, keepdims=True)
                probs[j, at, :] = (raised * share).astype(BF16)
                mix[j, at, :] = dot(probs[j, at, :], vh[j], NN).astype(BF16)
                return carry

            lax.fori_loop(0, d.heads, head, 0)
            own = [mix[j, at, :] for j in range(d.heads)]
            piece = lambda i, j: own[j][i * d.packed : (i + 1) * d.packed]
            mixbuf[r, z] = jnp.concatenate([piece(i, j) for i in range(t) for j in range(d.heads)], axis=1)
            l_mix(r).start()

            return carry

        lax.fori_loop(0, t, attend_rows, 0)
        keep(3, 4)
        g_up.finish()
        g_out.finish()
        keep(7)

        def block(i, carry):
            r = order(i)

            @pl.when(jnp.logical_and(i == 1, jnp.logical_not(at_end)))
            def _():
                for slot in range(1, t - 1):
                    l_cot.relay(slot)

            @pl.when(at_end)
            def _():
                l_cot.relay(r)

            @pl.when(i == 0)
            def _():
                g_down.forward()
                g_down.finish()

            grad_act[...] = dot(cot[r], down[...], NN)
            l_mix(r).finish()

            rows = jnp.concatenate(
                [
                    jnp.concatenate([mixbuf[r, j, :, k * d.cols : (k + 1) * d.cols] for j in range(t)], axis=1)
                    for k in range(t)
                ],
                axis=0,
            )
            total[...] = tokbuf[r].astype(F32) + dot(rows, out_t[...], NT) + vec[4:5, :]

            @pl.when(r == z)
            def _():
                hidden[...] = total[...]
                mixed_rows[...] = rows

            def norm_two(c):
                normed = normalize(total[c, :])[0]
                second[r, c, :] = (normed * vec[5:6, :] + vec[6:7, :]).astype(BF16)

            chunks(d, norm_two)
            pre = dot(second[r], up[...], NN) + upb[0:1, :]
            value, slope = gelu_both(pre)
            act[r] = value.astype(BF16)
            grad = grad_act[...] * slope
            bias_part[0:1, :] += jnp.sum(grad, axis=0, keepdims=True)
            pre_grad[r] = grad.astype(BF16)
            part[r] = dot(pre_grad[r], up[...], NT).astype(BF16)

            def launch(these):
                for chain in these:

                    @pl.when(r > 0)
                    def _():
                        chain.launch_right(r)

                    @pl.when(r < t - 1)
                    def _():
                        chain.launch_left(r)

            launch(chains)
            o_part[r] = dot(act[r], down[...], NT).astype(BF16)
            for h in range(1, t - 1):

                @pl.when(i >= h)
                def _():
                    for chain in chains:
                        chain.hop(h, order(i - h))

            return carry

        lax.fori_loop(0, t, block, 0)

        width = D // 3

        def weight_grad(k, left, right, i):
            value = left[:, :, i * width : (i + 1) * width].reshape(d.seq, width)
            grads[k, i * width : (i + 1) * width, :] = dot(value, right[...].reshape(d.seq, HP), TN).astype(BF16)

        work = [partial(weight_grad, 0, second, pre_grad, i) for i in range(3)]
        work += [partial(weight_grad, 1, cot, act, i) for i in range(3)]
        for i in range(t, 2 * t - 2):
            work.pop(0)()
            for h in range(i - t + 1, t - 1):
                for chain in chains:
                    chain.hop(h, order(i - h))
        for item in work:
            item()
        keep(8, 9, 11, 12, 13)
        for (lo, m), chain in zip(split, chains):
            chain.finish(grad_second, pl.ds(lo, m))
        if R > d.sent_rows:
            grad_second[d.sent_rows :, :] = jnp.zeros((R - d.sent_rows, D), F32)
        for op in (l_tok, l_cot):
            op.finish()
        for i in range(14):
            pltpu.make_async_copy(kept[i], kept_out[i], kept_sems.at[i]).wait()

    heads = (d.heads, d.seq, HD)
    outs = [shape(R, D, dtype=F32)]
    kept = [
        shape(*heads),
        shape(*heads),
        shape(*heads),
        shape(*heads),
        shape(d.heads, d.seq, d.seq),
        shape(t, R, D),
        shape(D, 3 * d.cols),
        shape(D, D),
        shape(2, D, HP),
        shape(t, R, D),
        shape(16, D, dtype=F32),
        shape(R, D, dtype=F32),
        shape(R, D),
        shape(8, HP, dtype=F32),
    ]
    scratch = [pltpu.VMEM(a.shape, a.dtype) for a in kept]
    scratch += [
        pltpu.VMEM((t, R, D), BF16),
        pltpu.VMEM((d.share, 3 * d.cols), BF16),
        pltpu.VMEM((t, d.fold, d.folds * d.cols), BF16),
        pltpu.VMEM((d.share, D), BF16),
        pltpu.VMEM((d.share, HP), BF16),
        pltpu.VMEM((d.share, HP), BF16),
        pltpu.VMEM((16, d.vec_lanes), F32),
        pltpu.VMEM((n, 16, d.vec_lanes), F32),
        pltpu.VMEM((t, t, d.packed, D), BF16),
        pltpu.VMEM((t, R, D), BF16),
        pltpu.VMEM((t, R, D), BF16),
        pltpu.VMEM((D, HP), BF16),
        pltpu.VMEM((D, HP), BF16),
        pltpu.VMEM((t, R, HP), BF16),
        pltpu.VMEM((t, R, HP), BF16),
        pltpu.VMEM((t, R, D), BF16),
        pltpu.VMEM((t + 1, R, D), BF16),
        pltpu.VMEM((8, HP), F32),
        pltpu.VMEM((R, D), F32),
        pltpu.VMEM((R, HP), F32),
    ]
    for _ in range(5):
        scratch += DpGather.sems(chips)
    scratch += LineGather.sems(t) + DirectGather.sems(t) + LineGather.sems(t) + DirectGather.sems(t, (t,))
    scratch += LineChain.sems(t) * 2 + [DMA((14,))]
    return pl.pallas_call(
        kernel,
        out_shape=outs + kept,
        in_specs=[VM] * len(args),
        out_specs=[VM] * len(outs) + [ANY] * len(kept),
        scratch_shapes=scratch,
        compiler_params=params(0),
        name="forward",
    )(*args)


class DpAdd:
    @staticmethod
    def sems(chips):
        return [DMA((chips,)), DMA((chips,)), DMA((chips,)), DMA((chips,))]

    def __init__(self, place, part, rows, near, far, sems):
        self.p, self.part, self.rows, self.near, self.far = place, part, rows, near, far
        self.sent, self.recv, self.sent_far, self.recv_far = sems

    def at(self, slot):
        return pl.ds(pl.multiple_of(slot * self.rows, 8), self.rows)

    def start(self):
        p = self.p
        for k in [*range(1, p.chips), 0]:
            src = self.part.at[self.at(2 * p.chip_at(k) + 1 - p.core)]
            remote(src, self.near.at[k], self.sent.at[k], self.recv.at[k], p.sibling).start()

    def wait_near(self, k):
        block = self.near.at[k]
        remote(block, block, self.sent.at[k], self.recv.at[k], self.p.sibling).wait_recv()

    def move(self):
        p = self.p
        for k in range(1, p.chips):
            self.wait_near(k)
            mine = self.part[self.at(2 * p.chip_at(k) + p.core), :]
            self.near[k] = (mine.astype(F32) + self.near[k].astype(F32)).astype(BF16)
            remote(self.near.at[k], self.far.at[k - 1], self.sent_far.at[k], self.recv_far.at[k], p.peer(k)).start()

    def finish(self):
        p = self.p
        self.wait_near(0)
        total = self.part[self.at(p.dp), :].astype(F32) + self.near[0].astype(F32)
        for k in range(1, p.chips):
            block = self.far.at[k - 1]
            remote(block, block, self.sent_far.at[k], self.recv_far.at[k], p.sibling).wait_recv()
            total += self.far[k - 1].astype(F32)
        for k in range(p.chips):
            block = self.near.at[0]
            remote(block, block, self.sent.at[k], self.recv.at[0], p.sibling).wait_send()
            if k > 0:
                remote(block, block, self.sent_far.at[k], self.recv.at[0], p.sibling).wait_send()
        return total


def backward(d, args):
    n, t, R, D, HP = d.n, d.t, d.block, d.width, d.hidden_pad
    chips, per_line, share = n // 2, n // t, d.share
    scale_factor = 1.0 / math.sqrt(HD)
    wide = 3 * d.cols

    def kernel(*refs):
        refs = list(refs)
        take = lambda m: [refs.pop(0) for _ in range(m)]
        tok, cot = take(2)
        far = take(15)
        output, input_grad, g_q, g_k, g_v, g_out, g_up, g_down, g_vec = take(9)
        near = take(15)
        grad_second, qh, kh, vh, mix, probs, first, wqkv, out_t, grads_mlp, p_part, vec, hidden, mixed_rows, bias_part = near
        tok_p, cot_p, gh, low, send, got, dq, dk, dv, q_sum, grads = take(11)
        o_part, w_part, f_part, f_inbox, p_inbox, f_sum, acc = take(7)
        o_mid, o_got, v_send, v_got, v_mid, v_line = take(6)
        place = Place(n, t)
        place.greet(every=True)
        z, dp = place.z, place.dp

        def adder(part):
            near, far = take(2)
            return part, near, far

        up_grad, down_grad = grads_mlp.at[0], grads_mlp.at[1]
        spaces = [adder(part) for part in (up_grad, down_grad, o_part, w_part)]
        sum_up, sum_down, sum_out, sum_qkv = [
            DpAdd(place, part, share, near, far, take(4)) for part, near, far in spaces
        ]
        split = halves(d)
        view = lambda ref, lo, m: ref.at[:, pl.ds(lo, m)]
        f_chains = [LineChain(place, view(f_part, *h), view(f_inbox, *h), take(2)) for h in split]
        p_chains = [LineChain(place, view(p_part, *h), view(p_inbox, *h), take(2)) for h in split]
        exchange = LineExchange(place, o_mid, o_got, take(3))
        x_sent, x_recv, v_sent, v_recv, v_sent_line, v_recv_line, far_sems = take(7)
        load = lambda i: pltpu.make_async_copy(far[i + 1], near[i + 1], far_sems.at[i + 1])
        for i in (9, 11, -1, 10, 8, 7, 12, 4, 0, 1, 2, 3, 6, 5, 13):
            load(i).start()
        place.meet()
        load(9).wait()
        p_chains[0].launch_right(t - 1)
        p_chains[0].launch_left(0)
        load(8).wait()
        sum_up.start()
        sum_down.start()
        for ref, src in ((tok_p, tok), (cot_p, cot)):
            ref[: d.rows, :] = src[...]
            if R > d.rows:
                ref[d.rows :, :] = jnp.zeros((R - d.rows, D), BF16)
        acc[...] = jnp.zeros_like(acc)

        def add_row(i, value):
            acc[i : i + 1, :] += jnp.sum(value, axis=0, keepdims=True)

        def norm_two(r):
            normed, inv = normalize(hidden[r, :])
            grad = grad_second[r, :]
            scaled = grad * vec[5:6, :]
            cots = cot_p[r, :].astype(F32)
            mean = jnp.mean(scaled, axis=-1, keepdims=True)
            pull = jnp.mean(scaled * normed, axis=-1, keepdims=True)
            total = cots + inv * (scaled - mean - normed * pull)
            gh[r, :] = total
            low[r, :] = total.astype(BF16)
            add_row(5, grad * normed)
            add_row(6, grad)
            add_row(4, total)
            add_row(7, cots)

        for i in (11, -1, 10):
            load(i).wait()
        chunks(d, norm_two)
        load(7).wait()
        mixed_grad = dot(low[...], out_t[...], NN).astype(BF16)
        for i in range(t):
            own = mixed_grad[:, i * d.cols : (i + 1) * d.cols]
            send[i] = jnp.concatenate([own[j * d.packed : (j + 1) * d.packed] for j in range(t)], axis=1)
        for k in range(1, t):
            to = place.along(k)
            remote(send.at[to[1]], got.at[z], x_sent.at[k], x_recv.at[z], to).start()
        got[z] = send[z]
        for chain in p_chains[1:]:
            chain.launch_right(t - 1)
            chain.launch_left(0)
        for i in range(t - 2, 1, -1):
            for chain in p_chains:
                chain.launch_right(i)
                chain.launch_left(t - 1 - i)
        p_chains[0].launch_right(1)
        p_chains[0].launch_left(t - 2)
        sum_up.move()
        third = D // 3
        load(12).wait()
        for i in range(3):
            o_part[i * third : (i + 1) * third, :] = dot(
                low[:, i * third : (i + 1) * third], mixed_rows[...], TN
            ).astype(BF16)
        sum_out.start()
        for i in range(5):
            load(i).wait()

        for ref in (dk, dv, q_sum):
            ref[...] = jnp.zeros_like(ref)

        def attend_rows(r):
            at = pl.ds(pl.multiple_of(r * R, R), R)
            for j in range(d.heads):
                pieces = [got[r, :, i * d.cols + j * HD : i * d.cols + (j + 1) * HD] for i in range(t)]
                dq[j, at, :] = jnp.concatenate(pieces, axis=0)

            def head(j, carry):
                grad = dq[j, at, :]
                full = probs[j, at, :]
                dv[j] += dot(full, grad, TN)
                delta = jnp.sum(grad.astype(F32) * mix[j, at, :].astype(F32), axis=-1, keepdims=True)
                grad_scores = (full.astype(F32) * (dot(grad, vh[j], NT) - delta)).astype(BF16)
                dk[j] += dot(grad_scores, qh[j, at, :], TN)
                query = dot(grad_scores, kh[j], NN) * scale_factor
                q_sum[j, 0:1, :] += jnp.sum(query, axis=0, keepdims=True)
                dq[j, at, :] = query.astype(BF16)
                return carry

            lax.fori_loop(0, d.heads, head, 0)

        attend_rows(z)
        sum_down.move()
        for k in range(1, t):
            slot = place.along(k)[1]
            remote(got.at[slot], got.at[slot], x_sent.at[k], x_recv.at[slot], place.sibling).wait_recv()
            attend_rows(slot)
            if k == 1:
                sum_out.move()
                for chain in p_chains:
                    chain.tick_far(1)
        for i in (6, 5, 13):
            load(i).wait()
        for i in range(2, t - 1):
            for chain in p_chains:
                chain.tick_far(i)

        def part_block(i):
            slot = jnp.where(z < t // 2, t - 1 - i, i)
            at = pl.ds(pl.multiple_of(slot * R, R), R)
            values = [dq[j, at, :] for j in range(d.heads)]
            values += [ref[j, at, :].astype(BF16) for ref in (dk, dv) for j in range(d.heads)]
            grads[at, :] = jnp.concatenate(values, axis=1)
            f_part[slot] = dot(grads[at, :], wqkv[...], NT).astype(BF16)
            for chain in f_chains:

                @pl.when(slot > 0)
                def _():
                    chain.launch_right(slot)

                @pl.when(slot < t - 1)
                def _():
                    chain.launch_left(slot)

        for i in range(t):
            part_block(i)
        for chain in p_chains[1:]:
            chain.launch_right(1)
            chain.launch_left(t - 2)

        def weight_block(i):
            value = first[:, :, i * third : (i + 1) * third].reshape(d.seq, third)
            w_part[i * third : (i + 1) * third, :] = dot(value, grads[...], TN).astype(BF16)

        for i in range(3):
            weight_block(i)
        sum_qkv.start()
        g_up[...] = sum_up.finish()[:, : d.hidden]
        for chain in f_chains:
            chain.tick_far(1)
        sum_qkv.move()
        g_down[...] = sum_down.finish()[:, : d.hidden]
        for i in range(2, t - 1):
            for chain in f_chains:
                chain.tick_far(i)
        out_total = sum_out.finish().astype(BF16)
        for i in range(t):
            o_mid[i] = jnp.concatenate(
                [out_total[j * d.fold : (j + 1) * d.fold, i * d.cols : (i + 1) * d.cols] for j in range(d.folds)], axis=1
            )
        exchange.start()
        v_send[...] = jnp.zeros_like(v_send)
        q_row = jnp.concatenate([q_sum[j, 0:1, :] for j in range(d.heads)], axis=1)
        v_row = jnp.concatenate([jnp.sum(dv[j], axis=0, keepdims=True) for j in range(d.heads)], axis=1)
        for j in range(per_line):
            slot = z * per_line + j
            v_send[slot, 2:3, :share] = q_row[:, j * share : (j + 1) * share]
            v_send[slot, 3:4, :share] = v_row[:, j * share : (j + 1) * share]
            v_send[slot, 8:9, : d.up_share] = bias_part[0:1, j * d.up_share : (j + 1) * d.up_share]
        for (lo, m), chain in zip(split, f_chains):
            chain.finish(f_sum, pl.ds(lo, m))
        if R > d.sent_rows:
            f_sum[d.sent_rows :, :] = jnp.zeros((R - d.sent_rows, D), F32)

        def norm_one_sums(r):
            normed = normalize(tok_p[r, :].astype(F32))[0]
            grad = f_sum[r, :]
            add_row(0, grad * normed)
            add_row(1, grad)

        def norm_one(r):
            normed, inv = normalize(tok_p[r, :].astype(F32))
            scaled = f_sum[r, :] * vec[0:1, :]
            mean = jnp.mean(scaled, axis=-1, keepdims=True)
            pull = jnp.mean(scaled * normed, axis=-1, keepdims=True)
            input_grad[r, :] = gh[r, :] + inv * (scaled - mean - normed * pull)

        chunks(d, norm_one_sums)
        for i in (0, 1, 4, 5, 6, 7):
            for j in range(n):
                v_send[j, i : i + 1, :share] = acc[i : i + 1, j * share : (j + 1) * share]
        others = [lax.rem(dp + k, n) for k in range(1, n)]
        for k in range(1, n):
            to = others[k - 1]
            remote(v_send.at[to], v_got.at[k], v_sent.at[k], v_recv.at[k], (to, z)).start()
        chunks(d, norm_one)
        total = v_send[dp]
        for k in range(1, n):
            remote(v_got.at[k], v_got.at[k], v_sent.at[k], v_recv.at[k], place.sibling).wait()
            total += v_got[k]
        v_mid[...] = total
        for k in range(1, t):
            remote(v_mid, v_line.at[k], v_sent_line.at[k], v_recv_line.at[k], place.along(k)).start()
        qkv_total = sum_qkv.finish()
        for i, ref in enumerate((g_q, g_k, g_v)):
            ref[...] = qkv_total[:, i * d.cols : (i + 1) * d.cols]
        exchange.finish()
        out_sum = jnp.sum(o_got[...].astype(F32), axis=0)
        for i in range(d.folds):
            g_out[i * d.fold : (i + 1) * d.fold, :] = out_sum[:, i * d.cols : (i + 1) * d.cols]
        for (lo, m), chain in zip(split, p_chains):
            chain.finish(f_sum, pl.ds(lo, m))
        if R > d.sent_rows:
            f_sum[d.sent_rows :, :] = jnp.zeros((R - d.sent_rows, D), F32)
        output[...] = (hidden[...] + f_sum[...] + vec[7:8, :]).astype(BF16)
        for k in range(1, t):
            remote(v_mid, v_line.at[k], v_sent_line.at[k], v_recv_line.at[k], place.sibling).wait()
            total += v_line[k]
        g_vec[...] = total
        for k in range(1, t):
            remote(send.at[0], got.at[0], x_sent.at[k], x_recv.at[0], place.sibling).wait_send()

    outs = [
        shape(R, D),
        shape(R, D, dtype=F32),
        shape(share, d.cols, dtype=F32),
        shape(share, d.cols, dtype=F32),
        shape(share, d.cols, dtype=F32),
        shape(share, d.cols, dtype=F32),
        shape(share, d.hidden, dtype=F32),
        shape(share, d.hidden, dtype=F32),
        shape(16, d.vec_lanes, dtype=F32),
    ]
    heads = (d.heads, d.seq, HD)
    scratch = [pltpu.VMEM(a.shape, a.dtype) for a in args[2:]]
    scratch += [
        pltpu.VMEM((R, D), BF16),
        pltpu.VMEM((R, D), BF16),
        pltpu.VMEM((R, D), F32),
        pltpu.VMEM((R, D), BF16),
        pltpu.VMEM((t, d.packed, D), BF16),
        pltpu.VMEM((t, d.packed, D), BF16),
        pltpu.VMEM(heads, BF16),
        pltpu.VMEM(heads, F32),
        pltpu.VMEM(heads, F32),
        pltpu.VMEM((d.heads, 8, HD), F32),
        pltpu.VMEM((d.seq, wide), BF16),
        pltpu.VMEM((D, D), BF16),
        pltpu.VMEM((D, wide), BF16),
        pltpu.VMEM((t, R, D), BF16),
        pltpu.VMEM((t + 1, R, D), BF16),
        pltpu.VMEM((t + 1, R, D), BF16),
        pltpu.VMEM((R, D), F32),
        pltpu.VMEM((16, D), F32),
        pltpu.VMEM((t, d.fold, d.folds * d.cols), BF16),
        pltpu.VMEM((t, d.fold, d.folds * d.cols), BF16),
        pltpu.VMEM((n, 16, d.vec_lanes), F32),
        pltpu.VMEM((n, 16, d.vec_lanes), F32),
        pltpu.VMEM((16, d.vec_lanes), F32),
        pltpu.VMEM((t, 16, d.vec_lanes), F32),
    ]
    for width in (HP, HP, D, wide):
        scratch += [pltpu.VMEM((chips, share, width), BF16), pltpu.VMEM((chips - 1, share, width), BF16)]
    scratch += DpAdd.sems(chips) * 4 + LineChain.sems(t) * 4 + LineExchange.sems(t)
    scratch += [DMA((t,)), DMA((t,)), DMA((n,)), DMA((n,)), DMA((t,)), DMA((t,)), DMA((15,))]
    return pl.pallas_call(
        kernel,
        out_shape=outs,
        in_specs=[VM] * 2 + [ANY] * 15,
        out_specs=[VM] * len(outs),
        scratch_shapes=scratch,
        compiler_params=params(1),
        name="backward",
    )(*args)


def finalize(d, args):
    names = len(args) - 1
    f32 = partial(shape, dtype=F32)
    outs = [shape(d.rows, d.width), f32(d.rows, d.width)] + [f32(*a.shape) for a in args[2:-1]]
    vectors = [f32(d.share)] * 8 + [f32(d.up_share)]

    def kernel(*refs):
        ins, g_vec, results = refs[:names], refs[names], refs[names + 1 :]
        for src, dst in zip(ins, results):
            dst[...] = src[: dst.shape[0], :]
        for i, ref in enumerate(results[names:]):
            m = ref.shape[0]
            ref[...] = jnp.reshape(g_vec[i : i + 1, :m], (m,))

    return pl.pallas_call(
        kernel,
        out_shape=outs + vectors,
        in_specs=[VM] * len(args),
        out_specs=[VM] * (names + 9),
        compiler_params=pltpu.CompilerParams(vmem_limit_bytes=VMEM_BYTES),
        name="finalize",
    )(*args)


def shards(
    sizes,
    tokens,
    key_mask,
    query_weight,
    key_weight,
    value_weight,
    out_weight,
    up_weight,
    down_weight,
    first_gain,
    first_shift,
    query_bias,
    value_bias,
    out_bias,
    second_gain,
    second_shift,
    up_bias,
    down_bias,
    cotangent,
):
    rows, width = tokens.shape[1:]
    share, up_share = first_gain.shape[0], up_bias.shape[0]
    cols, hidden_cols = query_weight.shape[1], up_weight.shape[1]
    d = Dims(sizes, rows, width, share, cols, hidden_cols, up_share)
    small = [first_gain, first_shift, query_bias, value_bias, out_bias, second_gain, second_shift, down_bias]
    kept = forward(
        d,
        [tokens[0], cotangent[0], key_mask, query_weight, key_weight, value_weight, out_weight.T, up_weight, down_weight.T]
        + small
        + [up_bias],
    )
    parts = backward(d, [tokens[0], cotangent[0], *kept])
    outs = finalize(d, parts)
    vectors = outs[8:]
    return (outs[0][None], outs[1][None], *outs[2:5], outs[5].T, outs[6], outs[7].T, *vectors[:7], vectors[8], vectors[7])


def solution(mesh):
    sizes = (mesh.shape["dp"], mesh.shape["tensor"])
    split = P("dp", "tensor")
    return jax.shard_map(
        partial(shards, sizes),
        mesh=mesh,
        in_specs=(P("dp", "tensor", None), P("dp", None), split, split, split, P("tensor", "dp"), split, P("tensor", "dp"))
        + (P("dp"),) * 9
        + (P("dp", "tensor", None),),
        out_specs=(P("dp", "tensor", None), P("dp", "tensor", None), split, split, split, P("tensor", "dp"), split, P("tensor", "dp"))
        + (P("dp"),) * 9,
        check_vma=False,
    )
```

```python
from functools import partial
import math

import jax
import jax.numpy as jnp
from jax import lax
from jax.experimental import pallas as pl
from jax.experimental.pallas import tpu as pltpu
from jax.sharding import PartitionSpec as P

HD = 72
EPSILON = 1e-06
GELU_COEF = 0.7978845608028654
MASK_FILL = -1e30
MESH = pl.DeviceIdType.MESH
ANY = pl.BlockSpec(memory_space=pl.ANY)
VM = pl.BlockSpec(memory_space=pltpu.VMEM)
DMA = pltpu.SemaphoreType.DMA
VMEM_BYTES = 60 << 20
F32 = jnp.float32
BF16 = jnp.bfloat16


def remote(src, dst, send_sem, recv_sem, device):
    return pltpu.make_async_remote_copy(
        src_ref=src,
        dst_ref=dst,
        send_sem=send_sem,
        recv_sem=recv_sem,
        device_id=device,
        device_id_type=MESH,
    )


class Place:
    def __init__(self, dp_size, line):
        self.dp_size, self.line, self.chips = dp_size, line, dp_size // 2
        self.dp = lax.axis_index("dp")
        self.z = lax.axis_index("tensor")
        self.core = lax.rem(self.dp, 2)
        self.chip = lax.div(self.dp, 2)
        self.sibling = (2 * self.chip + 1 - self.core, self.z)

    def chip_at(self, k):
        return lax.rem(self.chip + k + self.chips, self.chips)

    def peer(self, k):
        return (2 * self.chip_at(k) + self.core, self.z)

    def along(self, k):
        return (self.dp, lax.rem(self.z + k + self.line, self.line))

    def greet(self, every=False):
        barrier = pltpu.get_barrier_semaphore()
        if every:
            devices = [(lax.rem(self.dp + k, self.dp_size), self.z) for k in range(1, self.dp_size)]
        else:
            devices = [self.peer(k) for k in range(1, self.chips)] + [self.sibling]
        devices += [self.along(k) for k in range(1, self.line)]
        for device in devices:
            pl.semaphore_signal(barrier, inc=1, device_id=device, device_id_type=MESH)
        self.partners = len(devices)

    def meet(self):
        pl.semaphore_wait(pltpu.get_barrier_semaphore(), self.partners)


class DpGather:
    @staticmethod
    def sems(chips):
        return [DMA((chips,)), DMA((chips,)), DMA((2 * chips,)), DMA(())]

    def __init__(self, place, src, dst, sems, at=None):
        self.p, self.src, self.dst = place, src, dst
        self.across, self.inside, self.recv, self.local = sems
        self.at = at if at is not None else (lambda slot: dst.at[slot])

    def start(self):
        p = self.p
        mine = self.at(p.dp)
        for k in range(1, p.chips):
            remote(self.src, mine, self.across.at[k], self.recv.at[p.dp], p.peer(k)).start()
        remote(self.src, mine, self.inside.at[0], self.recv.at[p.dp], p.sibling).start()
        pltpu.make_async_copy(self.src, mine, self.local).start()

    def forward(self):
        p = self.p
        for k in range(1, p.chips):
            slot = 2 * p.chip_at(-k) + p.core
            block = self.at(slot)
            remote(block, block, self.across.at[k], self.recv.at[slot], p.sibling).wait_recv()
            remote(block, block, self.inside.at[k], self.recv.at[slot], p.sibling).start()

    def finish(self):
        p = self.p
        mine = self.at(p.dp)
        for k in range(p.chips):
            slot = 2 * p.chip_at(-k) + 1 - p.core
            block = self.at(slot)
            remote(block, block, self.inside.at[k], self.recv.at[slot], p.sibling).wait_recv()
        for k in range(p.chips):
            remote(self.src, mine, self.inside.at[k], self.recv.at[0], p.sibling).wait_send()
            if k > 0:
                remote(self.src, mine, self.across.at[k], self.recv.at[0], p.sibling).wait_send()
        pltpu.make_async_copy(self.src, mine, self.local).wait()


class LineGather:
    @staticmethod
    def sems(line, many=()):
        return [DMA((*many, line)), DMA((*many, line)), DMA((*many, line))]

    def __init__(self, place, dst, sems, rows=None):
        self.p, self.dst = place, dst
        self.right, self.left, self.recv = sems
        self.at = (lambda slot: dst.at[slot]) if rows is None else (lambda slot: dst.at[slot, pl.ds(0, rows)])

    def send_right(self, slot):
        p = self.p
        block = self.at(slot)

        @pl.when(p.z < p.line - 1)
        def _():
            remote(block, block, self.right.at[slot], self.recv.at[slot], (p.dp, p.z + 1)).start()

    def send_left(self, slot):
        p = self.p
        block = self.at(slot)

        @pl.when(p.z > 0)
        def _():
            remote(block, block, self.left.at[slot], self.recv.at[slot], (p.dp, p.z - 1)).start()

    def start(self):
        self.send_right(self.p.z)
        self.send_left(self.p.z)

    def arrive(self, slot):
        block = self.at(slot)
        remote(block, block, self.right.at[slot], self.recv.at[slot], self.p.sibling).wait_recv()

    def relay(self, slot):
        p = self.p

        @pl.when(jnp.logical_and(p.z > slot, slot >= 0))
        def _():
            self.arrive(slot)
            self.send_right(slot)

        @pl.when(jnp.logical_and(p.z < slot, slot < p.line))
        def _():
            self.arrive(slot)
            self.send_left(slot)

    def step(self, s):
        self.relay(self.p.z - s)
        self.relay(self.p.z + s)

    def finish(self):
        p = self.p
        for slot in range(p.line):
            block = self.at(slot)

            @pl.when(jnp.logical_and(p.z >= slot, p.z < p.line - 1))
            def _():
                remote(block, block, self.right.at[slot], self.recv.at[slot], p.sibling).wait_send()

            @pl.when(jnp.logical_and(p.z <= slot, p.z > 0))
            def _():
                remote(block, block, self.left.at[slot], self.recv.at[slot], p.sibling).wait_send()


class DirectGather:
    @staticmethod
    def sems(line, many=()):
        return [DMA((*many, line)), DMA((*many, line))]

    def __init__(self, place, dst, sems):
        self.p, self.dst = place, dst
        self.sent, self.recv = sems

    def start(self):
        p = self.p
        block = self.dst.at[p.z]
        for k in range(1, p.line):
            step = jnp.where(p.z < p.line // 2, p.line - k, k)
            remote(block, block, self.sent.at[k], self.recv.at[p.z], p.along(step)).start()

    def finish(self):
        p = self.p
        for k in range(1, p.line):
            slot = p.along(k)[1]
            block = self.dst.at[slot]
            remote(block, block, self.sent.at[k], self.recv.at[slot], p.sibling).wait()


class LineExchange:
    @staticmethod
    def sems(line):
        return [DMA((line,)), DMA((line,)), DMA(())]

    def __init__(self, place, src, dst, sems):
        self.p, self.src, self.dst = place, src, dst
        self.sent, self.recv, self.local = sems

    def start(self):
        p = self.p
        for k in range(1, p.line):
            to = p.along(k)
            remote(self.src.at[to[1]], self.dst.at[p.z], self.sent.at[k], self.recv.at[p.z], to).start()
        pltpu.make_async_copy(self.src.at[p.z], self.dst.at[p.z], self.local).start()

    def finish(self):
        p = self.p
        for k in range(1, p.line):
            slot = p.along(k)[1]
            block = self.dst.at[slot]
            remote(block, block, self.sent.at[k], self.recv.at[slot], p.sibling).wait_recv()
        for k in range(1, p.line):
            block = self.src.at[0]
            remote(block, block, self.sent.at[k], self.recv.at[0], p.sibling).wait_send()
        pltpu.make_async_copy(self.src.at[p.z], self.dst.at[p.z], self.local).wait()


def params(collective_id):
    return pltpu.CompilerParams(
        collective_id=collective_id, has_side_effects=True, vmem_limit_bytes=VMEM_BYTES
    )


def shape(*dims, dtype=BF16):
    return jax.ShapeDtypeStruct(dims, dtype)


def pad_to(count, unit):
    return -(-count // unit) * unit


def normalize(x):
    centred = x - jnp.mean(x, axis=-1, keepdims=True)
    inv_std = lax.rsqrt(jnp.mean(centred * centred, axis=-1, keepdims=True) + EPSILON)
    return centred * inv_std, inv_std


def dot(left, right, contract):
    return lax.dot_general(left, right, ((contract[:1], contract[1:]), ((), ())), preferred_element_type=F32)


NN, NT, TN = (1, 0), (1, 1), (0, 0)


class Dims:
    def __init__(self, sizes, rows, width, share, cols, hidden, up_share):
        self.n, self.t = sizes
        self.rows, self.width, self.share, self.cols = rows, width, share, cols
        self.hidden, self.up_share = hidden, up_share
        self.heads = cols // HD
        self.block = pad_to(rows, 16)
        self.sent_rows = rows if rows % 8 == 0 else self.block
        self.seq = self.t * self.block
        self.hidden_pad = pad_to(hidden, 128)
        self.vec_lanes = pad_to(max(up_share, share), 128)
        self.packed = self.block // self.t
        self.folds = 3 if share % 3 == 0 else 1
        self.fold = share // self.folds
        self.chunk = 32 if self.block % 32 == 0 else 16


def both_sides(place, s, work):
    def side(i, carry):
        slot = place.z - s + 2 * s * i

        @pl.when(jnp.logical_and(slot >= 0, slot < place.line))
        def _():
            work(slot)

        return carry

    lax.fori_loop(0, 2, side, 0)


def chunks(d, work):
    def one(i, carry):
        work(pl.ds(pl.multiple_of(i * d.chunk, d.chunk), d.chunk))
        return carry

    lax.fori_loop(0, d.block // d.chunk, one, 0)


def valid_keys(d, count):
    lane = lax.broadcasted_iota(jnp.int32, (1, d.seq), 1)
    zero = jnp.zeros((1, d.seq), jnp.int32)
    blk = sum([(lane >= d.block * i).astype(jnp.int32) for i in range(1, d.t)], zero)
    off = lane - blk * d.block
    inside = jnp.logical_and(off < d.rows, (off + blk * d.rows).astype(F32) < count)
    return jnp.where(inside, 1.0, 0.0)


class LineChain:
    @staticmethod
    def sems(line):
        return [DMA((line,)), DMA((line + 1,))]

    def __init__(self, place, part, inbox, sems):
        self.p, self.part, self.inbox = place, part, inbox
        self.sent, self.recv = sems

    def wait(self, slot):
        block = self.inbox.at[slot]
        remote(block, block, self.sent.at[0], self.recv.at[slot], self.p.sibling).wait_recv()

    def right(self, src, d):
        p = self.p
        remote(src.at[d], self.inbox.at[d], self.sent.at[d], self.recv.at[d], (p.dp, p.z + 1)).start()

    def left(self, src, d):
        p = self.p
        slot = jnp.where(d == p.z - 1, p.line, d)
        remote(src.at[d], self.inbox.at[slot], self.sent.at[d], self.recv.at[slot], (p.dp, p.z - 1)).start()

    def launch_right(self, d):
        @pl.when(self.p.z == 0)
        def _():
            self.right(self.part, d)

    def launch_left(self, d):
        @pl.when(self.p.z == self.p.line - 1)
        def _():
            self.left(self.part, d)

    def relay_right(self, d):
        p = self.p

        @pl.when((p.z > 0) & (p.z < d) & (d < p.line))
        def _():
            self.wait(d)
            self.inbox[d] = (self.inbox[d].astype(F32) + self.part[d].astype(F32)).astype(BF16)
            self.right(self.inbox, d)

    def relay_left(self, d):
        p = self.p

        @pl.when((p.z < p.line - 1) & (p.z > d) & (d >= 0))
        def _():
            self.wait(d)
            self.inbox[d] = (self.inbox[d].astype(F32) + self.part[d].astype(F32)).astype(BF16)
            self.left(self.inbox, d)

    def hop(self, h, d):
        p = self.p

        @pl.when(p.z == h)
        def _():
            self.relay_right(d)

        @pl.when(p.z == p.line - 1 - h)
        def _():
            self.relay_left(d)

    def tick_far(self, i):
        p = self.p
        self.relay_right(p.line - 1 + p.z - i)
        self.relay_left(i - p.line + 1 + p.z)

    def finish(self, out, rows):
        p = self.p
        out[rows, :] = self.part[p.z].astype(F32)

        @pl.when(p.z > 0)
        def _():
            self.wait(p.z)
            out[rows, :] += self.inbox[p.z].astype(F32)

        @pl.when(p.z < p.line - 1)
        def _():
            self.wait(p.line)
            out[rows, :] += self.inbox[p.line].astype(F32)

        for d in range(p.line):

            @pl.when(p.z != d)
            def _():
                block = self.part.at[d]
                remote(block, block, self.sent.at[d], self.recv.at[d], p.sibling).wait_send()


def halves(d):
    cut = pad_to(d.sent_rows // 2, 16)
    return ((0, cut), (cut, d.sent_rows - cut))


def gelu_both(u):
    square = u * u
    tanh_val = jnp.tanh(GELU_COEF * (u + 0.044715 * u * square))
    half = 0.5 * (1.0 + tanh_val)
    slope = half + 0.5 * u * (1.0 - tanh_val * tanh_val) * (GELU_COEF * (1.0 + 3.0 * 0.044715 * square))
    return u * half, slope


def forward(d, args):
    n, t, R, D, HP = d.n, d.t, d.block, d.width, d.hidden_pad
    chips = n // 2
    per_line = n // t
    scale_factor = 1.0 / math.sqrt(HD)
    split = halves(d)

    def kernel(*refs):
        refs = list(refs)
        take = lambda m: [refs.pop(0) for _ in range(m)]
        tok, cot_in, mask, wq, wk, wv, wo, wu, wd = take(9)
        vecs = take(9)
        (grad_second,) = take(1)
        kept_out = take(14)
        kept = take(14)
        qh, kh, vh, mix, probs, first, wqkv, out_t, grads, o_part, vec, hidden, mixed_rows, bias_part = kept
        tokbuf, w_st, o_mid, o_pack, u_st, d_st, v_st, v_all = take(8)
        mixbuf, second, cot, up, down, act, pre_grad, part, inbox, upb, total, grad_act = take(12)
        place = Place(n, t)
        place.greet()
        z = place.z
        rows_of = lambda ref: (lambda slot: ref.at[pl.ds(pl.multiple_of(slot * d.share, 8), d.share)])
        g_vec = DpGather(place, v_st, v_all, take(4))
        g_qkv = DpGather(place, w_st, wqkv, take(4), rows_of(wqkv))
        g_up = DpGather(place, u_st, up, take(4), rows_of(up))
        g_down = DpGather(place, d_st, down, take(4), rows_of(down))
        g_out = DpGather(place, o_pack, out_t, take(4), rows_of(out_t))
        l_tok = LineGather(place, tokbuf, take(3), d.sent_rows)
        l_out = DirectGather(place, o_mid, take(2))
        l_cot = LineGather(place, cot, take(3), d.sent_rows)
        mix_sems = take(2)
        l_mix = lambda r: DirectGather(place, mixbuf.at[r], [sem.at[r] for sem in mix_sems])
        view = lambda ref, lo, m: ref.at[:, pl.ds(lo, m)]
        chains = [LineChain(place, view(part, *h), view(inbox, *h), take(2)) for h in split]
        (kept_sems,) = take(1)

        def keep(*names):
            for i in names:
                pltpu.make_async_copy(kept[i], kept_out[i], kept_sems.at[i]).start()

        if R > d.rows:
            for i in range(t):
                tokbuf[i, d.rows :, :] = jnp.zeros((R - d.rows, D), BF16)
                cot[i, d.rows :, :] = jnp.zeros((R - d.rows, D), BF16)
        tokbuf[z, : d.rows, :] = tok[...]
        cot[z, : d.rows, :] = cot_in[...]
        for i, w in enumerate((wq, wk, wv)):
            w_st[:, i * d.cols : (i + 1) * d.cols] = w[...]
        v_st[...] = jnp.zeros_like(v_st)
        for i, v in enumerate(vecs):
            m = v.shape[0]
            v_st[i : i + 1, :m] = jnp.reshape(v[...].astype(F32), (1, m))
        o_mid[z] = jnp.concatenate([wo[i * d.fold : (i + 1) * d.fold, :] for i in range(d.folds)], axis=1)
        place.meet()
        g_vec.start()
        g_qkv.start()
        l_tok.start()
        l_out.start()
        at_end = jnp.logical_or(z == 0, z == t - 1)

        @pl.when(at_end)
        def _():
            l_cot.start()

        u_st[...] = jnp.zeros_like(u_st)
        u_st[:, : d.hidden] = wu[...]
        g_up.start()
        d_st[...] = jnp.zeros_like(d_st)
        d_st[:, : d.hidden] = wd[...]
        bias_part[...] = jnp.zeros_like(bias_part)
        g_vec.forward()
        g_vec.finish()
        vec[8:, :] = jnp.zeros((8, D), F32)
        for i in range(8):
            vec[i : i + 1, :] = jnp.concatenate([v_all[j, i : i + 1, : d.share] for j in range(n)], axis=1)
        upb[...] = jnp.zeros_like(upb)
        upb[0:1, : d.hidden] = jnp.concatenate(
            [v_all[z * per_line + j, 8:9, : d.up_share] for j in range(per_line)], axis=1
        )
        local = lambda i: jnp.concatenate(
            [v_all[z * per_line + j, i : i + 1, : d.share] for j in range(per_line)], axis=1
        )
        bias_row = jnp.concatenate([local(2), jnp.zeros((1, d.cols), F32), local(3)], axis=1)
        scale_row = jnp.concatenate(
            [jnp.full((1, d.cols), scale_factor, F32), jnp.ones((1, 2 * d.cols), F32)], axis=1
        )
        gain, shift = vec[0:1, :], vec[1:2, :]

        def norm_block(slot):
            def one(r):
                normed = normalize(tokbuf[slot, r, :].astype(F32))[0]
                first[slot, r, :] = (normed * gain + shift).astype(BF16)

            chunks(d, one)

        def project_block(slot):
            y = (dot(first[slot], wqkv[...], NN) + bias_row) * scale_row
            y = y.astype(BF16)
            at = pl.ds(pl.multiple_of(slot * R, R), R)
            for i, ref in enumerate((qh, kh, vh)):
                for j in range(d.heads):
                    start = i * d.cols + j * HD
                    ref[j, at, :] = y[:, start : start + HD]

        norm_block(z)
        l_tok.step(1)
        l_out.finish()
        for i in range(d.folds):
            o_pack[i * d.fold : (i + 1) * d.fold, :] = jnp.concatenate(
                [o_mid[j, :, i * d.cols : (i + 1) * d.cols] for j in range(t)], axis=1
            )
        g_out.start()
        g_down.start()
        g_qkv.forward()
        both_sides(place, 1, norm_block)
        g_qkv.finish()
        project_block(z)
        both_sides(place, 1, project_block)

        def norm_and_project(slot):
            norm_block(slot)
            project_block(slot)

        for s in range(2, t):
            l_tok.step(s)

            @pl.when(z == s - 1)
            def _():
                l_cot.relay(0)

            @pl.when(z == t - s)
            def _():
                l_cot.relay(t - 1)

            if s == 2:

                @pl.when(jnp.logical_not(at_end))
                def _():
                    l_cot.start()

            if s == 2:
                g_up.forward()
            both_sides(place, s, norm_and_project)
        g_out.forward()
        keep(0, 1, 2, 5, 6, 10)

        count = jnp.sum(mask[...].astype(F32), axis=1, keepdims=True)
        valid = valid_keys(d, count)


        def order(i):
            pair = lax.div(i, 2)
            return jnp.where(lax.rem(i + pair, 2) == 0, pair, t - 1 - pair)

        def attend_rows(i, carry):
            r = order(i)
            at = pl.ds(pl.multiple_of(r * R, R), R)

            def head(j, carry):
                scores = dot(qh[j, at, :], kh[j], NT)
                scores = jnp.where(valid > 0, scores, MASK_FILL)
                highest = jnp.max(scores, axis=-1, keepdims=True)
                raised = jnp.exp(scores - highest)
                share = 1.0 / jnp.sum(raised, axis=-1, keepdims=True)
                probs[j, at, :] = (raised * share).astype(BF16)
                mix[j, at, :] = dot(probs[j, at, :], vh[j], NN).astype(BF16)
                return carry

            lax.fori_loop(0, d.heads, head, 0)
            own = [mix[j, at, :] for j in range(d.heads)]
            piece = lambda i, j: own[j][i * d.packed : (i + 1) * d.packed]
            mixbuf[r, z] = jnp.concatenate([piece(i, j) for i in range(t) for j in range(d.heads)], axis=1)
            l_mix(r).start()

            return carry

        lax.fori_loop(0, t, attend_rows, 0)
        keep(3, 4)
        g_up.finish()
        g_out.finish()
        keep(7)

        def block(i, carry):
            r = order(i)

            @pl.when(jnp.logical_and(i == 1, jnp.logical_not(at_end)))
            def _():
                for slot in range(1, t - 1):
                    l_cot.relay(slot)

            @pl.when(at_end)
            def _():
                l_cot.relay(r)

            @pl.when(i == 0)
            def _():
                g_down.forward()
                g_down.finish()

            grad_act[...] = dot(cot[r], down[...], NN)
            l_mix(r).finish()

            rows = jnp.concatenate(
                [
                    jnp.concatenate([mixbuf[r, j, :, k * d.cols : (k + 1) * d.cols] for j in range(t)], axis=1)
                    for k in range(t)
                ],
                axis=0,
            )
            total[...] = tokbuf[r].astype(F32) + dot(rows, out_t[...], NT) + vec[4:5, :]

            @pl.when(r == z)
            def _():
                hidden[...] = total[...]
                mixed_rows[...] = rows

            def norm_two(c):
                normed = normalize(total[c, :])[0]
                second[r, c, :] = (normed * vec[5:6, :] + vec[6:7, :]).astype(BF16)

            chunks(d, norm_two)
            pre = dot(second[r], up[...], NN) + upb[0:1, :]
            value, slope = gelu_both(pre)
            act[r] = value.astype(BF16)
            grad = grad_act[...] * slope
            bias_part[0:1, :] += jnp.sum(grad, axis=0, keepdims=True)
            pre_grad[r] = grad.astype(BF16)
            part[r] = dot(pre_grad[r], up[...], NT).astype(BF16)

            def launch(these):
                for chain in these:

                    @pl.when(r > 0)
                    def _():
                        chain.launch_right(r)

                    @pl.when(r < t - 1)
                    def _():
                        chain.launch_left(r)

            launch(chains)
            o_part[r] = dot(act[r], down[...], NT).astype(BF16)
            for h in range(1, t - 1):

                @pl.when(i >= h)
                def _():
                    for chain in chains:
                        chain.hop(h, order(i - h))

            return carry

        lax.fori_loop(0, t, block, 0)

        width = D // 3

        def weight_grad(k, left, right, i):
            value = left[:, :, i * width : (i + 1) * width].reshape(d.seq, width)
            grads[k, i * width : (i + 1) * width, :] = dot(value, right[...].reshape(d.seq, HP), TN).astype(BF16)

        work = [partial(weight_grad, 0, second, pre_grad, i) for i in range(3)]
        work += [partial(weight_grad, 1, cot, act, i) for i in range(3)]
        for i in range(t, 2 * t - 2):
            work.pop(0)()
            for h in range(i - t + 1, t - 1):
                for chain in chains:
                    chain.hop(h, order(i - h))
        for item in work:
            item()
        keep(8, 9, 11, 12, 13)
        for (lo, m), chain in zip(split, chains):
            chain.finish(grad_second, pl.ds(lo, m))
        if R > d.sent_rows:
            grad_second[d.sent_rows :, :] = jnp.zeros((R - d.sent_rows, D), F32)
        for op in (l_tok, l_cot):
            op.finish()
        for i in range(14):
            pltpu.make_async_copy(kept[i], kept_out[i], kept_sems.at[i]).wait()

    heads = (d.heads, d.seq, HD)
    outs = [shape(R, D, dtype=F32)]
    kept = [
        shape(*heads),
        shape(*heads),
        shape(*heads),
        shape(*heads),
        shape(d.heads, d.seq, d.seq),
        shape(t, R, D),
        shape(D, 3 * d.cols),
        shape(D, D),
        shape(2, D, HP),
        shape(t, R, D),
        shape(16, D, dtype=F32),
        shape(R, D, dtype=F32),
        shape(R, D),
        shape(8, HP, dtype=F32),
    ]
    scratch = [pltpu.VMEM(a.shape, a.dtype) for a in kept]
    scratch += [
        pltpu.VMEM((t, R, D), BF16),
        pltpu.VMEM((d.share, 3 * d.cols), BF16),
        pltpu.VMEM((t, d.fold, d.folds * d.cols), BF16),
        pltpu.VMEM((d.share, D), BF16),
        pltpu.VMEM((d.share, HP), BF16),
        pltpu.VMEM((d.share, HP), BF16),
        pltpu.VMEM((16, d.vec_lanes), F32),
        pltpu.VMEM((n, 16, d.vec_lanes), F32),
        pltpu.VMEM((t, t, d.packed, D), BF16),
        pltpu.VMEM((t, R, D), BF16),
        pltpu.VMEM((t, R, D), BF16),
        pltpu.VMEM((D, HP), BF16),
        pltpu.VMEM((D, HP), BF16),
        pltpu.VMEM((t, R, HP), BF16),
        pltpu.VMEM((t, R, HP), BF16),
        pltpu.VMEM((t, R, D), BF16),
        pltpu.VMEM((t + 1, R, D), BF16),
        pltpu.VMEM((8, HP), F32),
        pltpu.VMEM((R, D), F32),
        pltpu.VMEM((R, HP), F32),
    ]
    for _ in range(5):
        scratch += DpGather.sems(chips)
    scratch += LineGather.sems(t) + DirectGather.sems(t) + LineGather.sems(t) + DirectGather.sems(t, (t,))
    scratch += LineChain.sems(t) * 2 + [DMA((14,))]
    return pl.pallas_call(
        kernel,
        out_shape=outs + kept,
        in_specs=[VM] * len(args),
        out_specs=[VM] * len(outs) + [ANY] * len(kept),
        scratch_shapes=scratch,
        compiler_params=params(0),
        name="forward",
    )(*args)


class DpAdd:
    @staticmethod
    def sems(chips):
        return [DMA((chips,)), DMA((chips,)), DMA((chips,)), DMA((chips,))]

    def __init__(self, place, part, rows, near, far, sems):
        self.p, self.part, self.rows, self.near, self.far = place, part, rows, near, far
        self.sent, self.recv, self.sent_far, self.recv_far = sems

    def at(self, slot):
        return pl.ds(pl.multiple_of(slot * self.rows, 8), self.rows)

    def start(self):
        p = self.p
        for k in [*range(1, p.chips), 0]:
            src = self.part.at[self.at(2 * p.chip_at(k) + 1 - p.core)]
            remote(src, self.near.at[k], self.sent.at[k], self.recv.at[k], p.sibling).start()

    def wait_near(self, k):
        block = self.near.at[k]
        remote(block, block, self.sent.at[k], self.recv.at[k], self.p.sibling).wait_recv()

    def move(self):
        p = self.p
        for k in range(1, p.chips):
            self.wait_near(k)
            mine = self.part[self.at(2 * p.chip_at(k) + p.core), :]
            self.near[k] = (mine.astype(F32) + self.near[k].astype(F32)).astype(BF16)
            remote(self.near.at[k], self.far.at[k - 1], self.sent_far.at[k], self.recv_far.at[k], p.peer(k)).start()

    def finish(self):
        p = self.p
        self.wait_near(0)
        total = self.part[self.at(p.dp), :].astype(F32) + self.near[0].astype(F32)
        for k in range(1, p.chips):
            block = self.far.at[k - 1]
            remote(block, block, self.sent_far.at[k], self.recv_far.at[k], p.sibling).wait_recv()
            total += self.far[k - 1].astype(F32)
        for k in range(p.chips):
            block = self.near.at[0]
            remote(block, block, self.sent.at[k], self.recv.at[0], p.sibling).wait_send()
            if k > 0:
                remote(block, block, self.sent_far.at[k], self.recv.at[0], p.sibling).wait_send()
        return total


def backward(d, args):
    n, t, R, D, HP = d.n, d.t, d.block, d.width, d.hidden_pad
    chips, per_line, share = n // 2, n // t, d.share
    scale_factor = 1.0 / math.sqrt(HD)
    wide = 3 * d.cols

    def kernel(*refs):
        refs = list(refs)
        take = lambda m: [refs.pop(0) for _ in range(m)]
        tok, cot = take(2)
        far = take(15)
        output, input_grad, g_q, g_k, g_v, g_out, g_up, g_down, g_vec = take(9)
        near = take(15)
        grad_second, qh, kh, vh, mix, probs, first, wqkv, out_t, grads_mlp, p_part, vec, hidden, mixed_rows, bias_part = near
        tok_p, cot_p, gh, low, send, got, dq, dk, dv, q_sum, grads = take(11)
        o_part, w_part, f_part, f_inbox, p_inbox, f_sum, acc = take(7)
        o_mid, o_got, v_send, v_got, v_mid, v_line = take(6)
        place = Place(n, t)
        place.greet(every=True)
        z, dp = place.z, place.dp

        def adder(part):
            near, far = take(2)
            return part, near, far

        up_grad, down_grad = grads_mlp.at[0], grads_mlp.at[1]
        spaces = [adder(part) for part in (up_grad, down_grad, o_part, w_part)]
        sum_up, sum_down, sum_out, sum_qkv = [
            DpAdd(place, part, share, near, far, take(4)) for part, near, far in spaces
        ]
        split = halves(d)
        view = lambda ref, lo, m: ref.at[:, pl.ds(lo, m)]
        f_chains = [LineChain(place, view(f_part, *h), view(f_inbox, *h), take(2)) for h in split]
        p_chains = [LineChain(place, view(p_part, *h), view(p_inbox, *h), take(2)) for h in split]
        exchange = LineExchange(place, o_mid, o_got, take(3))
        x_sent, x_recv, v_sent, v_recv, v_sent_line, v_recv_line, far_sems = take(7)
        load = lambda i: pltpu.make_async_copy(far[i + 1], near[i + 1], far_sems.at[i + 1])
        for i in (9, 11, -1, 10, 8, 7, 12, 4, 0, 1, 2, 3, 6, 5, 13):
            load(i).start()
        place.meet()
        load(9).wait()
        p_chains[0].launch_right(t - 1)
        p_chains[0].launch_left(0)
        load(8).wait()
        sum_up.start()
        sum_down.start()
        for ref, src in ((tok_p, tok), (cot_p, cot)):
            ref[: d.rows, :] = src[...]
            if R > d.rows:
                ref[d.rows :, :] = jnp.zeros((R - d.rows, D), BF16)
        acc[...] = jnp.zeros_like(acc)

        def add_row(i, value):
            acc[i : i + 1, :] += jnp.sum(value, axis=0, keepdims=True)

        def norm_two(r):
            normed, inv = normalize(hidden[r, :])
            grad = grad_second[r, :]
            scaled = grad * vec[5:6, :]
            cots = cot_p[r, :].astype(F32)
            mean = jnp.mean(scaled, axis=-1, keepdims=True)
            pull = jnp.mean(scaled * normed, axis=-1, keepdims=True)
            total = cots + inv * (scaled - mean - normed * pull)
            gh[r, :] = total
            low[r, :] = total.astype(BF16)
            add_row(5, grad * normed)
            add_row(6, grad)
            add_row(4, total)
            add_row(7, cots)

        for i in (11, -1, 10):
            load(i).wait()
        chunks(d, norm_two)
        load(7).wait()
        mixed_grad = dot(low[...], out_t[...], NN).astype(BF16)
        for i in range(t):
            own = mixed_grad[:, i * d.cols : (i + 1) * d.cols]
            send[i] = jnp.concatenate([own[j * d.packed : (j + 1) * d.packed] for j in range(t)], axis=1)
        for k in range(1, t):
            to = place.along(k)
            remote(send.at[to[1]], got.at[z], x_sent.at[k], x_recv.at[z], to).start()
        got[z] = send[z]
        for chain in p_chains[1:]:
            chain.launch_right(t - 1)
            chain.launch_left(0)
        for i in range(t - 2, 1, -1):
            for chain in p_chains:
                chain.launch_right(i)
                chain.launch_left(t - 1 - i)
        p_chains[0].launch_right(1)
        p_chains[0].launch_left(t - 2)
        sum_up.move()
        third = D // 3
        load(12).wait()
        for i in range(3):
            o_part[i * third : (i + 1) * third, :] = dot(
                low[:, i * third : (i + 1) * third], mixed_rows[...], TN
            ).astype(BF16)
        sum_out.start()
        for i in range(5):
            load(i).wait()

        for ref in (dk, dv, q_sum):
            ref[...] = jnp.zeros_like(ref)

        def attend_rows(r):
            at = pl.ds(pl.multiple_of(r * R, R), R)
            for j in range(d.heads):
                pieces = [got[r, :, i * d.cols + j * HD : i * d.cols + (j + 1) * HD] for i in range(t)]
                dq[j, at, :] = jnp.concatenate(pieces, axis=0)

            def head(j, carry):
                grad = dq[j, at, :]
                full = probs[j, at, :]
                dv[j] += dot(full, grad, TN)
                delta = jnp.sum(grad.astype(F32) * mix[j, at, :].astype(F32), axis=-1, keepdims=True)
                grad_scores = (full.astype(F32) * (dot(grad, vh[j], NT) - delta)).astype(BF16)
                dk[j] += dot(grad_scores, qh[j, at, :], TN)
                query = dot(grad_scores, kh[j], NN) * scale_factor
                q_sum[j, 0:1, :] += jnp.sum(query, axis=0, keepdims=True)
                dq[j, at, :] = query.astype(BF16)
                return carry

            lax.fori_loop(0, d.heads, head, 0)

        attend_rows(z)
        sum_down.move()
        for k in range(1, t):
            slot = place.along(k)[1]
            remote(got.at[slot], got.at[slot], x_sent.at[k], x_recv.at[slot], place.sibling).wait_recv()
            attend_rows(slot)
            if k == 1:
                sum_out.move()
                for chain in p_chains:
                    chain.tick_far(1)
        for i in (6, 5, 13):
            load(i).wait()
        for i in range(2, t - 1):
            for chain in p_chains:
                chain.tick_far(i)

        def part_block(i):
            slot = jnp.where(z < t // 2, t - 1 - i, i)
            at = pl.ds(pl.multiple_of(slot * R, R), R)
            values = [dq[j, at, :] for j in range(d.heads)]
            values += [ref[j, at, :].astype(BF16) for ref in (dk, dv) for j in range(d.heads)]
            grads[at, :] = jnp.concatenate(values, axis=1)
            f_part[slot] = dot(grads[at, :], wqkv[...], NT).astype(BF16)
            for chain in f_chains:

                @pl.when(slot > 0)
                def _():
                    chain.launch_right(slot)

                @pl.when(slot < t - 1)
                def _():
                    chain.launch_left(slot)

        for i in range(t):
            part_block(i)
        for chain in p_chains[1:]:
            chain.launch_right(1)
            chain.launch_left(t - 2)

        def weight_block(i):
            value = first[:, :, i * third : (i + 1) * third].reshape(d.seq, third)
            w_part[i * third : (i + 1) * third, :] = dot(value, grads[...], TN).astype(BF16)

        for i in range(3):
            weight_block(i)
        sum_qkv.start()
        g_up[...] = sum_up.finish()[:, : d.hidden]
        for chain in f_chains:
            chain.tick_far(1)
        sum_qkv.move()
        g_down[...] = sum_down.finish()[:, : d.hidden]
        for i in range(2, t - 1):
            for chain in f_chains:
                chain.tick_far(i)
        out_total = sum_out.finish().astype(BF16)
        for i in range(t):
            o_mid[i] = jnp.concatenate(
                [out_total[j * d.fold : (j + 1) * d.fold, i * d.cols : (i + 1) * d.cols] for j in range(d.folds)], axis=1
            )
        exchange.start()
        v_send[...] = jnp.zeros_like(v_send)
        q_row = jnp.concatenate([q_sum[j, 0:1, :] for j in range(d.heads)], axis=1)
        v_row = jnp.concatenate([jnp.sum(dv[j], axis=0, keepdims=True) for j in range(d.heads)], axis=1)
        for j in range(per_line):
            slot = z * per_line + j
            v_send[slot, 2:3, :share] = q_row[:, j * share : (j + 1) * share]
            v_send[slot, 3:4, :share] = v_row[:, j * share : (j + 1) * share]
            v_send[slot, 8:9, : d.up_share] = bias_part[0:1, j * d.up_share : (j + 1) * d.up_share]
        for (lo, m), chain in zip(split, f_chains):
            chain.finish(f_sum, pl.ds(lo, m))
        if R > d.sent_rows:
            f_sum[d.sent_rows :, :] = jnp.zeros((R - d.sent_rows, D), F32)

        def norm_one_sums(r):
            normed = normalize(tok_p[r, :].astype(F32))[0]
            grad = f_sum[r, :]
            add_row(0, grad * normed)
            add_row(1, grad)

        def norm_one(r):
            normed, inv = normalize(tok_p[r, :].astype(F32))
            scaled = f_sum[r, :] * vec[0:1, :]
            mean = jnp.mean(scaled, axis=-1, keepdims=True)
            pull = jnp.mean(scaled * normed, axis=-1, keepdims=True)
            input_grad[r, :] = gh[r, :] + inv * (scaled - mean - normed * pull)

        chunks(d, norm_one_sums)
        for i in (0, 1, 4, 5, 6, 7):
            for j in range(n):
                v_send[j, i : i + 1, :share] = acc[i : i + 1, j * share : (j + 1) * share]
        others = [lax.rem(dp + k, n) for k in range(1, n)]
        for k in range(1, n):
            to = others[k - 1]
            remote(v_send.at[to], v_got.at[k], v_sent.at[k], v_recv.at[k], (to, z)).start()
        chunks(d, norm_one)
        total = v_send[dp]
        for k in range(1, n):
            remote(v_got.at[k], v_got.at[k], v_sent.at[k], v_recv.at[k], place.sibling).wait()
            total += v_got[k]
        v_mid[...] = total
        for k in range(1, t):
            remote(v_mid, v_line.at[k], v_sent_line.at[k], v_recv_line.at[k], place.along(k)).start()
        qkv_total = sum_qkv.finish()
        for i, ref in enumerate((g_q, g_k, g_v)):
            ref[...] = qkv_total[:, i * d.cols : (i + 1) * d.cols]
        exchange.finish()
        out_sum = jnp.sum(o_got[...].astype(F32), axis=0)
        for i in range(d.folds):
            g_out[i * d.fold : (i + 1) * d.fold, :] = out_sum[:, i * d.cols : (i + 1) * d.cols]
        for (lo, m), chain in zip(split, p_chains):
            chain.finish(f_sum, pl.ds(lo, m))
        if R > d.sent_rows:
            f_sum[d.sent_rows :, :] = jnp.zeros((R - d.sent_rows, D), F32)
        output[...] = (hidden[...] + f_sum[...] + vec[7:8, :]).astype(BF16)
        for k in range(1, t):
            remote(v_mid, v_line.at[k], v_sent_line.at[k], v_recv_line.at[k], place.sibling).wait()
            total += v_line[k]
        g_vec[...] = total
        for k in range(1, t):
            remote(send.at[0], got.at[0], x_sent.at[k], x_recv.at[0], place.sibling).wait_send()

    outs = [
        shape(R, D),
        shape(R, D, dtype=F32),
        shape(share, d.cols, dtype=F32),
        shape(share, d.cols, dtype=F32),
        shape(share, d.cols, dtype=F32),
        shape(share, d.cols, dtype=F32),
        shape(share, d.hidden, dtype=F32),
        shape(share, d.hidden, dtype=F32),
        shape(16, d.vec_lanes, dtype=F32),
    ]
    heads = (d.heads, d.seq, HD)
    scratch = [pltpu.VMEM(a.shape, a.dtype) for a in args[2:]]
    scratch += [
        pltpu.VMEM((R, D), BF16),
        pltpu.VMEM((R, D), BF16),
        pltpu.VMEM((R, D), F32),
        pltpu.VMEM((R, D), BF16),
        pltpu.VMEM((t, d.packed, D), BF16),
        pltpu.VMEM((t, d.packed, D), BF16),
        pltpu.VMEM(heads, BF16),
        pltpu.VMEM(heads, F32),
        pltpu.VMEM(heads, F32),
        pltpu.VMEM((d.heads, 8, HD), F32),
        pltpu.VMEM((d.seq, wide), BF16),
        pltpu.VMEM((D, D), BF16),
        pltpu.VMEM((D, wide), BF16),
        pltpu.VMEM((t, R, D), BF16),
        pltpu.VMEM((t + 1, R, D), BF16),
        pltpu.VMEM((t + 1, R, D), BF16),
        pltpu.VMEM((R, D), F32),
        pltpu.VMEM((16, D), F32),
        pltpu.VMEM((t, d.fold, d.folds * d.cols), BF16),
        pltpu.VMEM((t, d.fold, d.folds * d.cols), BF16),
        pltpu.VMEM((n, 16, d.vec_lanes), F32),
        pltpu.VMEM((n, 16, d.vec_lanes), F32),
        pltpu.VMEM((16, d.vec_lanes), F32),
        pltpu.VMEM((t, 16, d.vec_lanes), F32),
    ]
    for width in (HP, HP, D, wide):
        scratch += [pltpu.VMEM((chips, share, width), BF16), pltpu.VMEM((chips - 1, share, width), BF16)]
    scratch += DpAdd.sems(chips) * 4 + LineChain.sems(t) * 4 + LineExchange.sems(t)
    scratch += [DMA((t,)), DMA((t,)), DMA((n,)), DMA((n,)), DMA((t,)), DMA((t,)), DMA((15,))]
    return pl.pallas_call(
        kernel,
        out_shape=[pltpu.VMEM(a.shape, a.dtype) for a in outs],
        in_specs=[VM] * 2 + [ANY] * 15,
        out_specs=[VM] * len(outs),
        scratch_shapes=scratch,
        compiler_params=params(1),
        name="backward",
    )(*args)


def finalize(d, args):
    names = len(args) - 1
    f32 = partial(shape, dtype=F32)
    outs = [shape(d.rows, d.width), f32(d.rows, d.width)] + [f32(*a.shape) for a in args[2:-1]]
    vectors = [f32(d.share)] * 8 + [f32(d.up_share)]

    def kernel(*refs):
        ins, g_vec, results = refs[:names], refs[names], refs[names + 1 :]
        for src, dst in zip(ins, results):
            dst[...] = src[: dst.shape[0], :]
        for i, ref in enumerate(results[names:]):
            m = ref.shape[0]
            ref[...] = jnp.reshape(g_vec[i : i + 1, :m], (m,))

    return pl.pallas_call(
        kernel,
        out_shape=outs + vectors,
        in_specs=[VM] * len(args),
        out_specs=[VM] * (names + 9),
        compiler_params=pltpu.CompilerParams(vmem_limit_bytes=VMEM_BYTES),
        name="finalize",
    )(*args)


def shards(
    sizes,
    tokens,
    key_mask,
    query_weight,
    key_weight,
    value_weight,
    out_weight,
    up_weight,
    down_weight,
    first_gain,
    first_shift,
    query_bias,
    value_bias,
    out_bias,
    second_gain,
    second_shift,
    up_bias,
    down_bias,
    cotangent,
):
    rows, width = tokens.shape[1:]
    share, up_share = first_gain.shape[0], up_bias.shape[0]
    cols, hidden_cols = query_weight.shape[1], up_weight.shape[1]
    d = Dims(sizes, rows, width, share, cols, hidden_cols, up_share)
    small = [first_gain, first_shift, query_bias, value_bias, out_bias, second_gain, second_shift, down_bias]
    kept = forward(
        d,
        [tokens[0], cotangent[0], key_mask, query_weight, key_weight, value_weight, out_weight.T, up_weight, down_weight.T]
        + small
        + [up_bias],
    )
    parts = backward(d, [tokens[0], cotangent[0], *kept])
    outs = finalize(d, [pltpu.with_memory_space_constraint(p, pltpu.VMEM) for p in parts])
    vectors = outs[8:]
    return (outs[0][None], outs[1][None], *outs[2:5], outs[5].T, outs[6], outs[7].T, *vectors[:7], vectors[8], vectors[7])


def solution(mesh):
    sizes = (mesh.shape["dp"], mesh.shape["tensor"])
    split = P("dp", "tensor")
    return jax.shard_map(
        partial(shards, sizes),
        mesh=mesh,
        in_specs=(P("dp", "tensor", None), P("dp", None), split, split, split, P("tensor", "dp"), split, P("tensor", "dp"))
        + (P("dp"),) * 9
        + (P("dp", "tensor", None),),
        out_specs=(P("dp", "tensor", None), P("dp", "tensor", None), split, split, split, P("tensor", "dp"), split, P("tensor", "dp"))
        + (P("dp"),) * 9,
        check_vma=False,
    )
```
